256 devices in a mesh: row: 16 (over z, core), col: 8 (over y_lo, x), chan: 2 (over y_hi).
Axes of the slice: x: 4, y: 4 (y_hi: 2, y_lo: 2; y = y_hi * 2 + y_lo), z: 8, core: 2. Of those that a mesh axis runs over, the one named last changes fastest.
Arguments:
- voltages: bfloat16 [128, 32, 137216], P('row', ('col', 'chan')), may hold values from -6 to 6
- lane_map: int32 [16, 8, 32], P('row', 'col'), may hold values from 0 to 31, each once within a row
- input_flags: int32 [128, 32], P('row', 'col'), may hold values 0 or 1
Outputs:
- visibility: bfloat16 [32, 2, 128, 32, 32, 128], P('chan', None, 'row', None, 'col')
The draws below stay inside these ranges and needn't reach their ends.
Inputs may be any that keep to these rules, and one draw needn't show every extreme that they name: For each block (row index, col index), lane_map lists every lane 0 to 31 once.
All inputs are finite; a program needn't handle non-finite values. No bound on the sum of `input_flags` on one device may be relied on, other than what follows from the above.
Results may differ from the reference program's by a relative error of at most 0.0069.
Values may be sent and summed in bfloat16 or wider, within the bound.
A program may use at most 64 MiB of HBM per device.

```python
import jax
import jax.numpy as jnp
from jax import lax

NFFT = 2048
TAPS = 4
P_DEV = 8
Q_DEV = 4
SPECTRA = 64
NP = 128
NQ = 32
LANES = 32
CHANS = 32
FRAMES = 67
SAMPLES = 137216
N_ROW = 16
N_COL = 8


def place_ends(result, rng, low, largest):
    longest = result.shape.index(max(result.shape))
    spots = []
    for shift in (0, 1):
        where = [jax.random.randint(jax.random.fold_in(rng, axis), (), 0, length) for axis, length in enumerate(result.shape)]
        where[longest] = (where[longest] + shift) % result.shape[longest]
        spots.append(tuple(where))
    return result.at[spots[0]].set(low).at[spots[1]].set(largest)


def levels(own_key, extent, split, low, high):
    factor_of, own = 1.0, jax.random.fold_in(own_key, 6)
    for axis_at, parts in split:
        heights = jnp.exp(jax.random.uniform(jax.random.fold_in(own, axis_at), (parts,), jnp.float32, low / len(split), high / len(split)))
        factor_of = factor_of * jnp.repeat(heights, extent[axis_at] // parts).reshape([-1 if axis == axis_at else 1 for axis in range(len(extent))])
    return factor_of


def noise(key, dims, width, bound, shards=(), kind=jnp.bfloat16):
    factor_of = levels(key, dims, shards, -0.22, 0.18) if shards else 1.0
    result = jax.random.normal(key, dims, jnp.float32) * width * factor_of
    return jnp.minimum(jnp.maximum(result, -bound), bound).astype(kind)


def setup_inputs(seed: int = 0) -> dict:
    arg_keys = jax.random.split(jax.random.key(seed), 4)
    return {
        "voltages": noise(arg_keys[0], (NP, NQ, SAMPLES), 1.0, 6.0, ((0, 16), (1, 16))),
        "lane_map": jax.vmap(lambda own: jax.random.permutation(own, LANES))(jax.random.split(arg_keys[1], N_ROW * N_COL)).reshape((N_ROW, N_COL, LANES)).astype(jnp.int32),
        "input_flags": place_ends((jax.random.randint(arg_keys[2], (NP, NQ), 0, 8) < 7).astype(jnp.int32), jax.random.fold_in(arg_keys[2], 1), 0, 1),
    }


def kernel_table(nfft, taps, chans):
    length = taps * nfft
    position = jnp.arange(length, dtype=jnp.float32)
    centre = (position - length / 2 + 0.5) / nfft
    window = jnp.sinc(centre) * (0.5 - 0.5 * jnp.cos(2.0 * jnp.pi * (position + 0.5) / length))
    norm_scale = jnp.sqrt(2.0 / jnp.sum(window * window))
    window = (window * norm_scale).reshape(taps, nfft)
    sample = jnp.arange(nfft, dtype=jnp.int32)
    bin_index = nfft // 4 + jnp.arange(chans, dtype=jnp.int32)
    phase_index = bin_index[:, None] * sample[None, :] % nfft
    phases = phase_index.astype(jnp.float32) * (2.0 * jnp.pi / nfft)
    both_parts = jnp.stack([jnp.cos(phases).T, -jnp.sin(phases).T], -1)
    built = window.T[:, :, None, None] * both_parts[:, None, :, :]
    return built.reshape(nfft, taps * chans * 2).astype(jnp.bfloat16)

def one_channel(rows):
    real_part = rows[:, :SPECTRA]
    imag_part = rows[:, SPECTRA:]
    turned = jnp.concatenate([-imag_part, real_part], axis=-1)
    real_vis = jnp.dot(rows, rows.T, preferred_element_type=jnp.float32)
    imag_vis = jnp.dot(rows, turned.T, preferred_element_type=jnp.float32)
    stacked = (jnp.stack([real_vis, imag_vis]) * (1.0 / SPECTRA)).astype(jnp.bfloat16)
    return stacked.reshape(2, NP, NQ, NP, NQ).transpose(0, 1, 2, 4, 3)

def reference(voltages, lane_map, input_flags):
    table_rows = kernel_table(NFFT, TAPS, CHANS)
    frames = voltages.reshape(NP * NQ * FRAMES, NFFT)
    frame_sums = jnp.dot(frames, table_rows, preferred_element_type=jnp.float32)
    frame_sums = frame_sums.reshape(NP, NQ, FRAMES, TAPS, CHANS, 2)
    tap_sum = frame_sums[:, :, 0:SPECTRA, 0]
    for tap_idx in range(1, TAPS):
        tap_sum = tap_sum + frame_sums[:, :, tap_idx:tap_idx + SPECTRA, tap_idx]
    filtered = tap_sum.astype(jnp.bfloat16)
    blocks = filtered.reshape(N_ROW, P_DEV, N_COL, Q_DEV, SPECTRA, CHANS, 2)
    blocks = blocks.transpose(0, 2, 1, 3, 4, 5, 6).reshape(N_ROW, N_COL, LANES, SPECTRA, CHANS, 2)
    picked = jax.vmap(jax.vmap(lambda block_rows, lane_index: block_rows[lane_index]))(blocks, lane_map)
    picked = picked.reshape(N_ROW, N_COL, P_DEV, Q_DEV, SPECTRA, CHANS, 2)
    picked = picked.transpose(0, 2, 1, 3, 4, 5, 6).reshape(NP, NQ, SPECTRA, CHANS, 2)
    weights = input_flags.astype(jnp.float32)[:, :, None, None, None]
    channelised = (picked.astype(jnp.float32) * weights).astype(jnp.bfloat16)
    channel_major = channelised.transpose(3, 0, 1, 4, 2).reshape(CHANS, NP * NQ, 2 * SPECTRA)
    return lax.map(one_channel, channel_major)
```

```python
import jax
import jax.numpy as jnp
from jax import lax
from jax.sharding import PartitionSpec as P

NFFT = 2048
TAPS = 4
P_DEV = 8
Q_DEV = 4
CH_DEV = 16
SPECTRA = 64
LANES = 32
FRAMES = 67


def kernel_table(nfft, taps, chans):
    length = taps * nfft
    position = jnp.arange(length, dtype=jnp.float32)
    centre = (position - length / 2 + 0.5) / nfft
    window = jnp.sinc(centre) * (0.5 - 0.5 * jnp.cos(2.0 * jnp.pi * (position + 0.5) / length))
    norm_scale = jnp.sqrt(2.0 / jnp.sum(window * window))
    window = (window * norm_scale).reshape(taps, nfft)
    sample = jnp.arange(nfft, dtype=jnp.int32)
    bin_index = nfft // 4 + jnp.arange(chans, dtype=jnp.int32)
    phase_index = bin_index[:, None] * sample[None, :] % nfft
    phases = phase_index.astype(jnp.float32) * (2.0 * jnp.pi / nfft)
    both_parts = jnp.stack([jnp.cos(phases).T, -jnp.sin(phases).T], -1)
    built = window.T[:, :, None, None] * both_parts[:, None, :, :]
    return built.reshape(nfft, taps * chans * 2).astype(jnp.bfloat16)


def ring_gather(x, axis, inner, gather_axis):
    n = lax.axis_size(axis)
    outer = n // inner
    me = lax.axis_index(axis)
    my_in = me % inner
    my_out = me // inner

    def shifted(d):
        return [(i, (i // inner) * inner + (i % inner + d) % inner) for i in range(n)]

    other_perm = [(i, (i + inner) % n) for i in range(n)]
    got = {0: x}
    fwd = bwd = x
    for s in range(1, inner // 2 + 1):
        fwd = lax.ppermute(fwd, axis, shifted(1))
        got[(-s) % inner] = fwd
        if s <= (inner - 1) // 2:
            bwd = lax.ppermute(bwd, axis, shifted(-1))
            got[s] = bwd
    mine = jnp.stack([got[k] for k in range(inner)])
    theirs = jnp.stack([lax.ppermute(got[k], axis, other_perm) for k in range(inner)])
    mine = jnp.roll(mine, my_in, axis=0)
    theirs = jnp.roll(theirs, my_in, axis=0)
    first = jnp.where(my_out == 0, mine, theirs)
    second = jnp.where(my_out == 0, theirs, mine)
    full = jnp.stack([first, second])
    nd = x.ndim
    perm = list(range(2, 2 + gather_axis)) + [0, 1] + list(range(2 + gather_axis, 2 + nd))
    full = full.transpose(perm)
    shape = list(x.shape)
    shape[gather_axis] *= n
    return full.reshape(shape)


def per_device(voltages, lane_map, input_flags):
    n_chan = lax.axis_size("chan")
    all_chans = CH_DEV * n_chan
    half_q = voltages.shape[1]
    table_rows = kernel_table(NFFT, TAPS, all_chans)
    frames = voltages.reshape(P_DEV, half_q, FRAMES, NFFT)
    frame_sums = jnp.einsum("pqfn,nk->pqfk", frames, table_rows, preferred_element_type=jnp.float32)
    frame_sums = frame_sums.reshape(P_DEV, half_q, FRAMES, TAPS, all_chans, 2)
    tap_sum = frame_sums[:, :, 0:SPECTRA, 0]
    for tap_idx in range(1, TAPS):
        tap_sum = tap_sum + frame_sums[:, :, tap_idx : tap_idx + SPECTRA, tap_idx]
    filtered = tap_sum.astype(jnp.bfloat16)
    filtered = filtered.transpose(3, 0, 1, 4, 2).reshape(all_chans, P_DEV, half_q, 2 * SPECTRA)
    me_chan = lax.axis_index("chan")
    halves = filtered.reshape(n_chan, CH_DEV, P_DEV, half_q, 2 * SPECTRA)
    kept = jnp.where(me_chan == 0, halves[0], halves[1])
    sent = jnp.where(me_chan == 0, halves[1], halves[0])
    received = lax.ppermute(sent, "chan", [(0, 1), (1, 0)])
    first = jnp.where(me_chan == 0, kept, received)
    second = jnp.where(me_chan == 0, received, kept)
    turned_over = jnp.concatenate([first, second], axis=2)
    lane_rows = turned_over.reshape(CH_DEV, LANES, 2 * SPECTRA)
    lane_index = lane_map.reshape(LANES)
    selector = (lane_index[:, None] == jnp.arange(LANES, dtype=jnp.int32)[None, :]).astype(
        jnp.bfloat16
    )
    reordered = jnp.einsum("kl,clz->ckz", selector, lane_rows, preferred_element_type=jnp.float32)
    weights = input_flags.reshape(LANES).astype(jnp.float32)[None, :, None]
    channelised = (
        (reordered * weights).astype(jnp.bfloat16).reshape(CH_DEV, P_DEV, Q_DEV, 2 * SPECTRA)
    )
    row_group = ring_gather(channelised, "col", 4, 2)
    grid_cols = row_group.shape[2]
    row_block = row_group.reshape(CH_DEV, P_DEV * grid_cols, 2 * SPECTRA)
    col_set = ring_gather_row(channelised)
    real_part = col_set[..., :SPECTRA]
    imag_part = col_set[..., SPECTRA:]
    turned = jnp.concatenate([-imag_part, real_part], axis=-1)
    col_block = jnp.stack([col_set, turned], axis=1)
    products = jnp.einsum(
        "cik,crpqk->criqp", row_block, col_block, preferred_element_type=jnp.float32
    )
    products = (products * (1.0 / SPECTRA)).astype(jnp.bfloat16)
    return products.reshape(CH_DEV, 2, P_DEV, grid_cols, Q_DEV, col_set.shape[1])


def ring_gather_row(x):
    axis = "row"
    n = lax.axis_size(axis)
    nz = n // 2
    me = lax.axis_index(axis)
    my_z = me // 2
    my_core = me % 2
    fwd_perm = [(i, (i + 2) % n) for i in range(n)]
    bwd_perm = [(i, (i - 2) % n) for i in range(n)]
    sib_perm = [(i, i ^ 1) for i in range(n)]
    got = {0: x}
    fwd = bwd = x
    for s in range(1, nz // 2 + 1):
        fwd = lax.ppermute(fwd, axis, fwd_perm)
        got[(-s) % nz] = fwd
        if s <= (nz - 1) // 2:
            bwd = lax.ppermute(bwd, axis, bwd_perm)
            got[s] = bwd
    mine = jnp.stack([got[k] for k in range(nz)])
    theirs = jnp.stack([lax.ppermute(got[k], axis, sib_perm) for k in range(nz)])
    mine = jnp.roll(mine, my_z, axis=0)
    theirs = jnp.roll(theirs, my_z, axis=0)
    c0 = jnp.where(my_core == 0, mine, theirs)
    c1 = jnp.where(my_core == 0, theirs, mine)
    full = jnp.stack([c0, c1], axis=1)
    full = full.transpose(2, 0, 1, 3, 4, 5)
    c, p, q, k = x.shape
    return full.reshape(c, n * p, q, k)


def solution(mesh):
    return jax.shard_map(
        per_device,
        mesh=mesh,
        in_specs=(P("row", ("col", "chan"), None), P("row", "col", None), P("row", "col")),
        out_specs=P("chan", None, "row", None, "col", None),
        check_vma=False,
    )
```

```python
import jax
import jax.numpy as jnp
from jax import lax
from jax.sharding import PartitionSpec as P
from jax.experimental import pallas as pl
from jax.experimental.pallas import tpu as pltpu

NFFT = 2048
TAPS = 4
P_DEV = 8
Q_DEV = 4
CH_DEV = 16
SPECTRA = 64
LANES = 32
FRAMES = 67


def kernel_table(nfft, taps, chans):
    length = taps * nfft
    position = jnp.arange(length, dtype=jnp.float32)
    centre = (position - length / 2 + 0.5) / nfft
    window = jnp.sinc(centre) * (0.5 - 0.5 * jnp.cos(2.0 * jnp.pi * (position + 0.5) / length))
    norm_scale = jnp.sqrt(2.0 / jnp.sum(window * window))
    window = (window * norm_scale).reshape(taps, nfft)
    sample = jnp.arange(nfft, dtype=jnp.int32)
    bin_index = nfft // 4 + jnp.arange(chans, dtype=jnp.int32)
    phase_index = bin_index[:, None] * sample[None, :] % nfft
    phases = phase_index.astype(jnp.float32) * (2.0 * jnp.pi / nfft)
    both_parts = jnp.stack([jnp.cos(phases).T, -jnp.sin(phases).T], -1)
    built = window.T[:, :, None, None] * both_parts[:, None, :, :]
    return built.reshape(nfft, taps * chans * 2).astype(jnp.bfloat16)


def _gather_kernel(x_ref, rowg_ref, colg_ref, send_sems, recv_sems, local_sems):
    nrow = lax.axis_size("row")
    ncol = lax.axis_size("col")
    r = lax.axis_index("row")
    c = lax.axis_index("col")
    ch = lax.axis_index("chan")
    nz = nrow // 2
    z = r // 2
    core = r % 2
    nx = ncol // 2
    yl = c // nx
    xx = c % nx
    mesh_ids = pl.DeviceIdType.MESH

    def row_slot(zz, cc):
        return ((zz + nz) % nz) * 2 + cc

    def col_slot(yy, xv):
        return yy * nx + (xv + nx) % nx

    z_up = (row_slot(z + 1, core), c, ch)
    z_down = (row_slot(z - 1, core), c, ch)
    sibling = (row_slot(z, 1 - core), c, ch)
    x_up = (r, col_slot(yl, xx + 1), ch)
    x_down = (r, col_slot(yl, xx - 1), ch)
    y_other = (r, col_slot(1 - yl, xx), ch)

    barrier = pltpu.get_barrier_semaphore()
    for dev in (z_up, z_down, sibling, x_up, x_down, y_other):
        pl.semaphore_signal(barrier, inc=1, device_id=dev, device_id_type=mesh_ids)
    pl.semaphore_wait(barrier, 6)

    n_fwd = nz // 2
    n_bwd = (nz - 1) // 2
    nx_fwd = nx // 2
    nx_bwd = (nx - 1) // 2
    s_rf = 0
    s_rb = s_rf + n_fwd
    s_sib = s_rb + n_bwd
    s_cf = s_sib + nz
    s_cb = s_cf + nx_fwd
    s_y = s_cb + nx_bwd

    def copy(src, dst, sem, dev):
        return pltpu.make_async_remote_copy(
            src_ref=src, dst_ref=dst, send_sem=send_sems.at[sem],
            recv_sem=recv_sems.at[sem], device_id=dev, device_id_type=mesh_ids)

    started = []

    def start(src, dst, sem, dev):
        d = copy(src, dst, sem, dev)
        d.start()
        started.append(d)

    def wait_in(ref, slot, sem):
        copy(ref.at[slot], ref.at[slot], sem, z_up).wait_recv()

    local_row = pltpu.make_async_copy(x_ref, rowg_ref.at[r], local_sems.at[0])
    local_col = pltpu.make_async_copy(x_ref, colg_ref.at[c], local_sems.at[1])
    local_row.start()
    local_col.start()

    start(x_ref, rowg_ref.at[r], s_rf, z_up)
    if n_bwd:
        start(x_ref, rowg_ref.at[r], s_rb, z_down)
    start(x_ref, rowg_ref.at[r], s_sib, sibling)
    start(x_ref, colg_ref.at[c], s_cf, x_up)
    if nx_bwd:
        start(x_ref, colg_ref.at[c], s_cb, x_down)
    start(x_ref, colg_ref.at[c], s_y, y_other)

    for s in range(1, max(n_fwd, nx_fwd) + 1):
        if s <= n_fwd:
            slot = row_slot(z - s, core)
            wait_in(rowg_ref, slot, s_rf + s - 1)
            if s < n_fwd:
                start(rowg_ref.at[slot], rowg_ref.at[slot], s_rf + s, z_up)
            start(rowg_ref.at[slot], rowg_ref.at[slot], s_sib + s, sibling)
        if s <= n_bwd:
            slot = row_slot(z + s, core)
            wait_in(rowg_ref, slot, s_rb + s - 1)
            if s < n_bwd:
                start(rowg_ref.at[slot], rowg_ref.at[slot], s_rb + s, z_down)
            start(rowg_ref.at[slot], rowg_ref.at[slot], s_sib + n_fwd + s, sibling)
        if s <= nx_fwd:
            slot = col_slot(yl, xx - s)
            wait_in(colg_ref, slot, s_cf + s - 1)
            if s < nx_fwd:
                start(colg_ref.at[slot], colg_ref.at[slot], s_cf + s, x_up)
            start(colg_ref.at[slot], colg_ref.at[slot], s_y + s, y_other)
        if s <= nx_bwd:
            slot = col_slot(yl, xx + s)
            wait_in(colg_ref, slot, s_cb + s - 1)
            if s < nx_bwd:
                start(colg_ref.at[slot], colg_ref.at[slot], s_cb + s, x_down)
            start(colg_ref.at[slot], colg_ref.at[slot], s_y + nx_fwd + s, y_other)

    wait_in(rowg_ref, row_slot(z, 1 - core), s_sib)
    for s in range(1, n_fwd + 1):
        wait_in(rowg_ref, row_slot(z - s, 1 - core), s_sib + s)
    for s in range(1, n_bwd + 1):
        wait_in(rowg_ref, row_slot(z + s, 1 - core), s_sib + n_fwd + s)
    wait_in(colg_ref, col_slot(1 - yl, xx), s_y)
    for s in range(1, nx_fwd + 1):
        wait_in(colg_ref, col_slot(1 - yl, xx - s), s_y + s)
    for s in range(1, nx_bwd + 1):
        wait_in(colg_ref, col_slot(1 - yl, xx + s), s_y + nx_fwd + s)
    for d in started:
        d.wait_send()
    local_row.wait()
    local_col.wait()


def gather_both(x):
    nrow = lax.axis_size("row")
    ncol = lax.axis_size("col")
    nz = nrow // 2
    nx = ncol // 2
    n_sems = nz // 2 + (nz - 1) // 2 + nz + nx // 2 + (nx - 1) // 2 + nx
    any_spec = pl.BlockSpec(memory_space=pl.ANY)
    return pl.pallas_call(
        _gather_kernel,
        out_shape=(
            jax.ShapeDtypeStruct((nrow,) + x.shape, x.dtype),
            jax.ShapeDtypeStruct((ncol,) + x.shape, x.dtype),
        ),
        in_specs=[any_spec],
        out_specs=(any_spec, any_spec),
        scratch_shapes=[
            pltpu.SemaphoreType.DMA((n_sems,)),
            pltpu.SemaphoreType.DMA((n_sems,)),
            pltpu.SemaphoreType.DMA((2,)),
        ],
        compiler_params=pltpu.CompilerParams(collective_id=0, has_side_effects=True),
    )(x)


def per_device(voltages, lane_map, input_flags):
    n_chan = lax.axis_size("chan")
    all_chans = CH_DEV * n_chan
    half_q = voltages.shape[1]
    table_rows = kernel_table(NFFT, TAPS, all_chans)
    frames = voltages.reshape(P_DEV, half_q, FRAMES, NFFT)
    frame_sums = jnp.einsum("pqfn,nk->pqfk", frames, table_rows, preferred_element_type=jnp.float32)
    frame_sums = frame_sums.reshape(P_DEV, half_q, FRAMES, TAPS, all_chans, 2)
    tap_sum = frame_sums[:, :, 0:SPECTRA, 0]
    for tap_idx in range(1, TAPS):
        tap_sum = tap_sum + frame_sums[:, :, tap_idx : tap_idx + SPECTRA, tap_idx]
    filtered = tap_sum.astype(jnp.bfloat16)
    filtered = filtered.transpose(3, 0, 1, 4, 2).reshape(all_chans, P_DEV, half_q, 2 * SPECTRA)
    me_chan = lax.axis_index("chan")
    halves = filtered.reshape(n_chan, CH_DEV, P_DEV, half_q, 2 * SPECTRA)
    kept = jnp.where(me_chan == 0, halves[0], halves[1])
    sent = jnp.where(me_chan == 0, halves[1], halves[0])
    received = lax.ppermute(sent, "chan", [(0, 1), (1, 0)])
    first = jnp.where(me_chan == 0, kept, received)
    second = jnp.where(me_chan == 0, received, kept)
    turned_over = jnp.concatenate([first, second], axis=2)
    lane_rows = turned_over.reshape(CH_DEV, LANES, 2 * SPECTRA)
    lane_index = lane_map.reshape(LANES)
    selector = (lane_index[:, None] == jnp.arange(LANES, dtype=jnp.int32)[None, :]).astype(
        jnp.bfloat16
    )
    reordered = jnp.einsum("kl,clz->ckz", selector, lane_rows, preferred_element_type=jnp.float32)
    weights = input_flags.reshape(LANES).astype(jnp.float32)[None, :, None]
    channelised = (
        (reordered * weights).astype(jnp.bfloat16).reshape(CH_DEV, P_DEV, Q_DEV, 2 * SPECTRA)
    )
    by_row, by_col = gather_both(channelised.reshape(CH_DEV, P_DEV * Q_DEV, 2 * SPECTRA))
    n_row = by_row.shape[0]
    grid_cols = by_col.shape[0] * Q_DEV
    row_block = (
        by_col.reshape(-1, CH_DEV, P_DEV, Q_DEV, 2 * SPECTRA)
        .transpose(1, 2, 0, 3, 4)
        .reshape(CH_DEV, P_DEV * grid_cols, 2 * SPECTRA)
    )
    col_set = (
        by_row.reshape(n_row, CH_DEV, P_DEV, Q_DEV, 2 * SPECTRA)
        .transpose(1, 0, 2, 3, 4)
        .reshape(CH_DEV, n_row * P_DEV, Q_DEV, 2 * SPECTRA)
    )
    real_part = col_set[..., :SPECTRA]
    imag_part = col_set[..., SPECTRA:]
    turned = jnp.concatenate([-imag_part, real_part], axis=-1)
    col_block = jnp.stack([col_set, turned], axis=1)
    products = jnp.einsum(
        "cik,crpqk->criqp", row_block, col_block, preferred_element_type=jnp.float32
    )
    products = (products * (1.0 / SPECTRA)).astype(jnp.bfloat16)
    return products.reshape(CH_DEV, 2, P_DEV, grid_cols, Q_DEV, col_set.shape[1])


def solution(mesh):
    return jax.shard_map(
        per_device,
        mesh=mesh,
        in_specs=(P("row", ("col", "chan"), None), P("row", "col", None), P("row", "col")),
        out_specs=P("chan", None, "row", None, "col", None),
        check_vma=False,
    )
```

```python
import jax
import jax.numpy as jnp
from jax import lax
from jax.sharding import PartitionSpec as P
from jax.experimental import pallas as pl
from jax.experimental.pallas import tpu as pltpu

NFFT = 2048
TAPS = 4
P_DEV = 8
Q_DEV = 4
CH_DEV = 16
SPECTRA = 64
LANES = 32
FRAMES = 67


def kernel_table(nfft, taps, chans):
    length = taps * nfft
    position = jnp.arange(length, dtype=jnp.float32)
    centre = (position - length / 2 + 0.5) / nfft
    window = jnp.sinc(centre) * (0.5 - 0.5 * jnp.cos(2.0 * jnp.pi * (position + 0.5) / length))
    norm_scale = jnp.sqrt(2.0 / jnp.sum(window * window))
    window = (window * norm_scale).reshape(taps, nfft)
    sample = jnp.arange(nfft, dtype=jnp.int32)
    bin_index = nfft // 4 + jnp.arange(chans, dtype=jnp.int32)
    phase_index = bin_index[:, None] * sample[None, :] % nfft
    phases = phase_index.astype(jnp.float32) * (2.0 * jnp.pi / nfft)
    both_parts = jnp.stack([jnp.cos(phases).T, -jnp.sin(phases).T], -1)
    built = window.T[:, :, None, None] * both_parts[:, None, :, :]
    return built.reshape(nfft, taps * chans * 2).astype(jnp.bfloat16)


def _gather_kernel(x_ref, rowg_ref, colg_ref, send_sems, recv_sems, local_sems):
    nrow = lax.axis_size("row")
    ncol = lax.axis_size("col")
    r = lax.axis_index("row")
    c = lax.axis_index("col")
    ch = lax.axis_index("chan")
    nz = nrow // 2
    z = r // 2
    core = r % 2
    nx = ncol // 2
    yl = c // nx
    xx = c % nx
    mesh_ids = pl.DeviceIdType.MESH

    def row_slot(zz, cc):
        return ((zz + nz) % nz) * 2 + cc

    def col_slot(yy, xv):
        return yy * nx + (xv + nx) % nx

    z_up = (row_slot(z + 1, core), c, ch)
    z_down = (row_slot(z - 1, core), c, ch)
    sibling = (row_slot(z, 1 - core), c, ch)
    x_up = (r, col_slot(yl, xx + 1), ch)
    x_down = (r, col_slot(yl, xx - 1), ch)
    y_other = (r, col_slot(1 - yl, xx), ch)

    barrier = pltpu.get_barrier_semaphore()
    for dev in (z_up, z_down, sibling, x_up, x_down, y_other):
        pl.semaphore_signal(barrier, inc=1, device_id=dev, device_id_type=mesh_ids)
    pl.semaphore_wait(barrier, 6)

    n_fwd = nz // 2
    n_bwd = (nz - 1) // 2
    nx_fwd = nx // 2
    nx_bwd = (nx - 1) // 2
    s_rf = 0
    s_rb = s_rf + n_fwd
    s_sib = s_rb + n_bwd
    s_cf = s_sib + nz
    s_cb = s_cf + nx_fwd
    s_y = s_cb + nx_bwd

    def copy(src, dst, sem, dev):
        return pltpu.make_async_remote_copy(
            src_ref=src, dst_ref=dst, send_sem=send_sems.at[sem],
            recv_sem=recv_sems.at[sem], device_id=dev, device_id_type=mesh_ids)

    started = []

    def start(src, dst, sem, dev):
        d = copy(src, dst, sem, dev)
        d.start()
        started.append(d)

    def wait_in(ref, slot, sem):
        copy(ref.at[slot], ref.at[slot], sem, z_up).wait_recv()

    local_row = pltpu.make_async_copy(x_ref, rowg_ref.at[r], local_sems.at[0])
    local_col = pltpu.make_async_copy(x_ref, colg_ref.at[c], local_sems.at[1])
    local_row.start()
    local_col.start()

    start(x_ref, rowg_ref.at[r], s_rf, z_up)
    if n_bwd:
        start(x_ref, rowg_ref.at[r], s_rb, z_down)
    start(x_ref, rowg_ref.at[r], s_sib, sibling)
    start(x_ref, colg_ref.at[c], s_cf, x_up)
    if nx_bwd:
        start(x_ref, colg_ref.at[c], s_cb, x_down)
    start(x_ref, colg_ref.at[c], s_y, y_other)

    for s in range(1, max(n_fwd, nx_fwd) + 1):
        if s <= n_fwd:
            slot = row_slot(z - s, core)
            wait_in(rowg_ref, slot, s_rf + s - 1)
            if s < n_fwd:
                start(rowg_ref.at[slot], rowg_ref.at[slot], s_rf + s, z_up)
            start(rowg_ref.at[slot], rowg_ref.at[slot], s_sib + s, sibling)
        if s <= n_bwd:
            slot = row_slot(z + s, core)
            wait_in(rowg_ref, slot, s_rb + s - 1)
            if s < n_bwd:
                start(rowg_ref.at[slot], rowg_ref.at[slot], s_rb + s, z_down)
            start(rowg_ref.at[slot], rowg_ref.at[slot], s_sib + n_fwd + s, sibling)
        if s <= nx_fwd:
            slot = col_slot(yl, xx - s)
            wait_in(colg_ref, slot, s_cf + s - 1)
            if s < nx_fwd:
                start(colg_ref.at[slot], colg_ref.at[slot], s_cf + s, x_up)
            start(colg_ref.at[slot], colg_ref.at[slot], s_y + s, y_other)
        if s <= nx_bwd:
            slot = col_slot(yl, xx + s)
            wait_in(colg_ref, slot, s_cb + s - 1)
            if s < nx_bwd:
                start(colg_ref.at[slot], colg_ref.at[slot], s_cb + s, x_down)
            start(colg_ref.at[slot], colg_ref.at[slot], s_y + nx_fwd + s, y_other)

    wait_in(rowg_ref, row_slot(z, 1 - core), s_sib)
    for s in range(1, n_fwd + 1):
        wait_in(rowg_ref, row_slot(z - s, 1 - core), s_sib + s)
    for s in range(1, n_bwd + 1):
        wait_in(rowg_ref, row_slot(z + s, 1 - core), s_sib + n_fwd + s)
    wait_in(colg_ref, col_slot(1 - yl, xx), s_y)
    for s in range(1, nx_fwd + 1):
        wait_in(colg_ref, col_slot(1 - yl, xx - s), s_y + s)
    for s in range(1, nx_bwd + 1):
        wait_in(colg_ref, col_slot(1 - yl, xx + s), s_y + nx_fwd + s)
    for d in started:
        d.wait_send()
    local_row.wait()
    local_col.wait()


def gather_both(x):
    nrow = lax.axis_size("row")
    ncol = lax.axis_size("col")
    nz = nrow // 2
    nx = ncol // 2
    n_sems = nz // 2 + (nz - 1) // 2 + nz + nx // 2 + (nx - 1) // 2 + nx
    any_spec = pl.BlockSpec(memory_space=pl.ANY)
    return pl.pallas_call(
        _gather_kernel,
        out_shape=(
            jax.ShapeDtypeStruct((nrow,) + x.shape, x.dtype),
            jax.ShapeDtypeStruct((ncol,) + x.shape, x.dtype),
        ),
        in_specs=[any_spec],
        out_specs=(any_spec, any_spec),
        scratch_shapes=[
            pltpu.SemaphoreType.DMA((n_sems,)),
            pltpu.SemaphoreType.DMA((n_sems,)),
            pltpu.SemaphoreType.DMA((2,)),
        ],
        compiler_params=pltpu.CompilerParams(collective_id=0, has_side_effects=True),
    )(x)


def per_device(voltages, lane_map, input_flags):
    n_chan = lax.axis_size("chan")
    all_chans = CH_DEV * n_chan
    half_q = voltages.shape[1]
    table_rows = kernel_table(NFFT, TAPS, all_chans)
    frames = voltages.reshape(P_DEV, half_q, FRAMES, NFFT)
    frame_sums = jnp.einsum("pqfn,nk->pqfk", frames, table_rows, preferred_element_type=jnp.float32)
    frame_sums = frame_sums.reshape(P_DEV, half_q, FRAMES, TAPS, all_chans, 2)
    tap_sum = frame_sums[:, :, 0:SPECTRA, 0]
    for tap_idx in range(1, TAPS):
        tap_sum = tap_sum + frame_sums[:, :, tap_idx : tap_idx + SPECTRA, tap_idx]
    filtered = tap_sum.astype(jnp.bfloat16)
    filtered = filtered.transpose(3, 0, 1, 4, 2).reshape(all_chans, P_DEV, half_q, 2 * SPECTRA)
    me_chan = lax.axis_index("chan")
    halves = filtered.reshape(n_chan, CH_DEV, P_DEV, half_q, 2 * SPECTRA)
    kept = jnp.where(me_chan == 0, halves[0], halves[1])
    sent = jnp.where(me_chan == 0, halves[1], halves[0])
    received = lax.ppermute(sent, "chan", [(0, 1), (1, 0)])
    first = jnp.where(me_chan == 0, kept, received)
    second = jnp.where(me_chan == 0, received, kept)
    turned_over = jnp.concatenate([first, second], axis=2)
    lane_rows = turned_over.reshape(CH_DEV, LANES, 2 * SPECTRA)
    lane_index = lane_map.reshape(LANES)
    selector = (lane_index[:, None] == jnp.arange(LANES, dtype=jnp.int32)[None, :]).astype(
        jnp.bfloat16
    )
    reordered = jnp.einsum("kl,clz->ckz", selector, lane_rows, preferred_element_type=jnp.float32)
    weights = input_flags.reshape(LANES).astype(jnp.float32)[None, :, None]
    channelised = (
        (reordered * weights).astype(jnp.bfloat16).reshape(CH_DEV, P_DEV, Q_DEV, 2 * SPECTRA)
    )
    by_row, by_col = gather_both(channelised.reshape(CH_DEV, P_DEV * Q_DEV, 2 * SPECTRA))
    n_row = by_row.shape[0]
    grid_cols = by_col.shape[0] * Q_DEV
    row_block = (
        by_col.reshape(-1, CH_DEV, P_DEV, Q_DEV, 2 * SPECTRA)
        .transpose(1, 2, 0, 3, 4)
        .reshape(CH_DEV, P_DEV * grid_cols, 2 * SPECTRA)
    )
    col_set = (
        by_row.reshape(n_row, CH_DEV, P_DEV, Q_DEV, 2 * SPECTRA)
        .transpose(1, 0, 2, 3, 4)
        .reshape(CH_DEV, n_row * P_DEV, Q_DEV, 2 * SPECTRA)
    )
    rotated = jnp.concatenate([row_block[..., SPECTRA:], -row_block[..., :SPECTRA]], axis=-1)
    lhs = jnp.stack([row_block, rotated], axis=1).reshape(CH_DEV, 2 * row_block.shape[1], 2 * SPECTRA)
    rhs = col_set.transpose(0, 2, 1, 3)
    products = correlate(lhs, rhs)
    return products.reshape(CH_DEV, 2, P_DEV, grid_cols, Q_DEV, col_set.shape[1])


CH_STEP = 2


def _corr_kernel(lhs_ref, rhs_ref, out_ref, acc_ref):
    rows = lhs_ref.shape[1]
    n_q = rhs_ref.shape[1]
    for cc in range(lhs_ref.shape[0]):
        a = lhs_ref[cc]
        for q2 in range(n_q):
            acc_ref[pl.ds(q2, rows, stride=n_q), :] = lax.dot_general(
                a, rhs_ref[cc, q2], (((1,), (1,)), ((), ())), preferred_element_type=jnp.float32
            )
        out_ref[cc] = (acc_ref[...] * (1.0 / SPECTRA)).astype(out_ref.dtype).reshape(out_ref.shape[1:])


def correlate(lhs, rhs):
    n_c, rows, k = lhs.shape
    n_q, n_p = rhs.shape[1], rhs.shape[2]
    out_rows = rows * n_q // (2 * P_DEV)
    return pl.pallas_call(
        _corr_kernel,
        grid=(n_c // CH_STEP,),
        out_shape=jax.ShapeDtypeStruct((n_c, 2, P_DEV, out_rows, n_p), jnp.bfloat16),
        in_specs=[
            pl.BlockSpec((CH_STEP, rows, k), lambda i: (i, 0, 0)),
            pl.BlockSpec((CH_STEP, n_q, n_p, k), lambda i: (i, 0, 0, 0)),
        ],
        out_specs=pl.BlockSpec((CH_STEP, 2, P_DEV, out_rows, n_p), lambda i: (i, 0, 0, 0, 0)),
        scratch_shapes=[pltpu.VMEM((rows * n_q, n_p), jnp.float32)],
    )(lhs, rhs)


def solution(mesh):
    return jax.shard_map(
        per_device,
        mesh=mesh,
        in_specs=(P("row", ("col", "chan"), None), P("row", "col", None), P("row", "col")),
        out_specs=P("chan", None, "row", None, "col", None),
        check_vma=False,
    )
```

```python
import jax
import ml_dtypes
import numpy as np
import jax.numpy as jnp
from jax import lax
from jax.sharding import PartitionSpec as P
from jax.experimental import pallas as pl
from jax.experimental.pallas import tpu as pltpu

NFFT = 2048
TAPS = 4
P_DEV = 8
Q_DEV = 4
CH_DEV = 16
SPECTRA = 64
LANES = 32
FRAMES = 67


def kernel_table(nfft, taps, chans):
    length = taps * nfft
    position = np.arange(length, dtype=np.float64)
    centre = (position - length / 2 + 0.5) / nfft
    window = np.sinc(centre) * (0.5 - 0.5 * np.cos(2.0 * np.pi * (position + 0.5) / length))
    window = window * np.sqrt(2.0 / np.sum(window * window))
    window = window.reshape(taps, nfft)
    sample = np.arange(nfft, dtype=np.int64)
    bin_index = nfft // 4 + np.arange(chans, dtype=np.int64)
    phase_index = bin_index[:, None] * sample[None, :] % nfft
    phases = phase_index.astype(np.float64) * (2.0 * np.pi / nfft)
    both_parts = np.stack([np.cos(phases).T, -np.sin(phases).T], -1)
    built = window.T[:, :, None, None] * both_parts[:, None, :, :]
    return jnp.asarray(built.reshape(nfft, taps * chans * 2).astype(ml_dtypes.bfloat16))


def _gather_kernel(x_ref, rowg_ref, colg_ref, send_sems, recv_sems, local_sems):
    nrow = lax.axis_size("row")
    ncol = lax.axis_size("col")
    r = lax.axis_index("row")
    c = lax.axis_index("col")
    ch = lax.axis_index("chan")
    nz = nrow // 2
    z = r // 2
    core = r % 2
    nx = ncol // 2
    yl = c // nx
    xx = c % nx
    mesh_ids = pl.DeviceIdType.MESH

    def row_slot(zz, cc):
        return ((zz + nz) % nz) * 2 + cc

    def col_slot(yy, xv):
        return yy * nx + (xv + nx) % nx

    z_up = (row_slot(z + 1, core), c, ch)
    z_down = (row_slot(z - 1, core), c, ch)
    sibling = (row_slot(z, 1 - core), c, ch)
    x_up = (r, col_slot(yl, xx + 1), ch)
    x_down = (r, col_slot(yl, xx - 1), ch)
    y_other = (r, col_slot(1 - yl, xx), ch)

    barrier = pltpu.get_barrier_semaphore()
    for dev in (z_up, z_down, sibling, x_up, x_down, y_other):
        pl.semaphore_signal(barrier, inc=1, device_id=dev, device_id_type=mesh_ids)
    pl.semaphore_wait(barrier, 6)

    n_fwd = nz // 2
    n_bwd = (nz - 1) // 2
    nx_fwd = nx // 2
    nx_bwd = (nx - 1) // 2
    s_rf = 0
    s_rb = s_rf + n_fwd
    s_sib = s_rb + n_bwd
    s_cf = s_sib + nz
    s_cb = s_cf + nx_fwd
    s_y = s_cb + nx_bwd

    def copy(src, dst, sem, dev):
        return pltpu.make_async_remote_copy(
            src_ref=src, dst_ref=dst, send_sem=send_sems.at[sem],
            recv_sem=recv_sems.at[sem], device_id=dev, device_id_type=mesh_ids)

    started = []

    def start(src, dst, sem, dev):
        d = copy(src, dst, sem, dev)
        d.start()
        started.append(d)

    def wait_in(ref, slot, sem):
        copy(ref.at[slot], ref.at[slot], sem, z_up).wait_recv()

    local_row = pltpu.make_async_copy(x_ref, rowg_ref.at[r], local_sems.at[0])
    local_col = pltpu.make_async_copy(x_ref, colg_ref.at[c], local_sems.at[1])
    local_row.start()
    local_col.start()

    start(x_ref, rowg_ref.at[r], s_rf, z_up)
    if n_bwd:
        start(x_ref, rowg_ref.at[r], s_rb, z_down)
    start(x_ref, rowg_ref.at[r], s_sib, sibling)
    start(x_ref, colg_ref.at[c], s_cf, x_up)
    if nx_bwd:
        start(x_ref, colg_ref.at[c], s_cb, x_down)
    start(x_ref, colg_ref.at[c], s_y, y_other)

    for s in range(1, max(n_fwd, nx_fwd) + 1):
        if s <= n_fwd:
            slot = row_slot(z - s, core)
            wait_in(rowg_ref, slot, s_rf + s - 1)
            if s < n_fwd:
                start(rowg_ref.at[slot], rowg_ref.at[slot], s_rf + s, z_up)
            start(rowg_ref.at[slot], rowg_ref.at[slot], s_sib + s, sibling)
        if s <= n_bwd:
            slot = row_slot(z + s, core)
            wait_in(rowg_ref, slot, s_rb + s - 1)
            if s < n_bwd:
                start(rowg_ref.at[slot], rowg_ref.at[slot], s_rb + s, z_down)
            start(rowg_ref.at[slot], rowg_ref.at[slot], s_sib + n_fwd + s, sibling)
        if s <= nx_fwd:
            slot = col_slot(yl, xx - s)
            wait_in(colg_ref, slot, s_cf + s - 1)
            if s < nx_fwd:
                start(colg_ref.at[slot], colg_ref.at[slot], s_cf + s, x_up)
            start(colg_ref.at[slot], colg_ref.at[slot], s_y + s, y_other)
        if s <= nx_bwd:
            slot = col_slot(yl, xx + s)
            wait_in(colg_ref, slot, s_cb + s - 1)
            if s < nx_bwd:
                start(colg_ref.at[slot], colg_ref.at[slot], s_cb + s, x_down)
            start(colg_ref.at[slot], colg_ref.at[slot], s_y + nx_fwd + s, y_other)

    wait_in(rowg_ref, row_slot(z, 1 - core), s_sib)
    for s in range(1, n_fwd + 1):
        wait_in(rowg_ref, row_slot(z - s, 1 - core), s_sib + s)
    for s in range(1, n_bwd + 1):
        wait_in(rowg_ref, row_slot(z + s, 1 - core), s_sib + n_fwd + s)
    wait_in(colg_ref, col_slot(1 - yl, xx), s_y)
    for s in range(1, nx_fwd + 1):
        wait_in(colg_ref, col_slot(1 - yl, xx - s), s_y + s)
    for s in range(1, nx_bwd + 1):
        wait_in(colg_ref, col_slot(1 - yl, xx + s), s_y + nx_fwd + s)
    for d in started:
        d.wait_send()
    local_row.wait()
    local_col.wait()


def gather_both(x):
    nrow = lax.axis_size("row")
    ncol = lax.axis_size("col")
    nz = nrow // 2
    nx = ncol // 2
    n_sems = nz // 2 + (nz - 1) // 2 + nz + nx // 2 + (nx - 1) // 2 + nx
    any_spec = pl.BlockSpec(memory_space=pl.ANY)
    return pl.pallas_call(
        _gather_kernel,
        out_shape=(
            jax.ShapeDtypeStruct((nrow,) + x.shape, x.dtype),
            jax.ShapeDtypeStruct((ncol,) + x.shape, x.dtype),
        ),
        in_specs=[any_spec],
        out_specs=(any_spec, any_spec),
        scratch_shapes=[
            pltpu.SemaphoreType.DMA((n_sems,)),
            pltpu.SemaphoreType.DMA((n_sems,)),
            pltpu.SemaphoreType.DMA((2,)),
        ],
        compiler_params=pltpu.CompilerParams(collective_id=0, has_side_effects=True),
    )(x)


def per_device(voltages, lane_map, input_flags):
    n_chan = lax.axis_size("chan")
    all_chans = CH_DEV * n_chan
    half_q = voltages.shape[1]
    table_rows = kernel_table(NFFT, TAPS, all_chans)
    frames = voltages.reshape(P_DEV, half_q, FRAMES, NFFT)
    frame_sums = jnp.einsum("pqfn,nk->pqfk", frames, table_rows, preferred_element_type=jnp.float32)
    frame_sums = frame_sums.reshape(P_DEV, half_q, FRAMES, TAPS, all_chans, 2)
    tap_sum = frame_sums[:, :, 0:SPECTRA, 0]
    for tap_idx in range(1, TAPS):
        tap_sum = tap_sum + frame_sums[:, :, tap_idx : tap_idx + SPECTRA, tap_idx]
    filtered = tap_sum.astype(jnp.bfloat16)
    filtered = filtered.transpose(3, 0, 1, 4, 2).reshape(all_chans, P_DEV, half_q, 2 * SPECTRA)
    me_chan = lax.axis_index("chan")
    halves = filtered.reshape(n_chan, CH_DEV, P_DEV, half_q, 2 * SPECTRA)
    kept = jnp.where(me_chan == 0, halves[0], halves[1])
    sent = jnp.where(me_chan == 0, halves[1], halves[0])
    received = lax.ppermute(sent, "chan", [(0, 1), (1, 0)])
    first = jnp.where(me_chan == 0, kept, received)
    second = jnp.where(me_chan == 0, received, kept)
    turned_over = jnp.concatenate([first, second], axis=2)
    lane_rows = turned_over.reshape(CH_DEV, LANES, 2 * SPECTRA)
    lane_index = lane_map.reshape(LANES)
    selector = (lane_index[:, None] == jnp.arange(LANES, dtype=jnp.int32)[None, :]).astype(
        jnp.bfloat16
    )
    reordered = jnp.einsum("kl,clz->ckz", selector, lane_rows, preferred_element_type=jnp.float32)
    weights = input_flags.reshape(LANES).astype(jnp.float32)[None, :, None]
    channelised = (
        (reordered * weights).astype(jnp.bfloat16).reshape(CH_DEV, P_DEV, Q_DEV, 2 * SPECTRA)
    )
    by_row, by_col = gather_both(channelised.reshape(CH_DEV, P_DEV * Q_DEV, 2 * SPECTRA))
    n_row = by_row.shape[0]
    grid_cols = by_col.shape[0] * Q_DEV
    row_block = (
        by_col.reshape(-1, CH_DEV, P_DEV, Q_DEV, 2 * SPECTRA)
        .transpose(1, 2, 0, 3, 4)
        .reshape(CH_DEV, P_DEV * grid_cols, 2 * SPECTRA)
    )
    col_set = (
        by_row.reshape(n_row, CH_DEV, P_DEV, Q_DEV, 2 * SPECTRA)
        .transpose(1, 0, 2, 3, 4)
        .reshape(CH_DEV, n_row * P_DEV, Q_DEV, 2 * SPECTRA)
    )
    rotated = jnp.concatenate([row_block[..., SPECTRA:], -row_block[..., :SPECTRA]], axis=-1)
    lhs = jnp.stack([row_block, rotated], axis=1).reshape(CH_DEV, 2 * row_block.shape[1], 2 * SPECTRA)
    rhs = col_set.transpose(0, 2, 1, 3)
    products = correlate(lhs, rhs)
    return products.reshape(CH_DEV, 2, P_DEV, grid_cols, Q_DEV, col_set.shape[1])


CH_STEP = 2


def _corr_kernel(lhs_ref, rhs_ref, out_ref, acc_ref):
    rows = lhs_ref.shape[1]
    n_q = rhs_ref.shape[1]
    for cc in range(lhs_ref.shape[0]):
        a = lhs_ref[cc]
        for q2 in range(n_q):
            acc_ref[pl.ds(q2, rows, stride=n_q), :] = lax.dot_general(
                a, rhs_ref[cc, q2], (((1,), (1,)), ((), ())), preferred_element_type=jnp.float32
            )
        out_ref[cc] = (acc_ref[...] * (1.0 / SPECTRA)).astype(out_ref.dtype).reshape(out_ref.shape[1:])


def correlate(lhs, rhs):
    n_c, rows, k = lhs.shape
    n_q, n_p = rhs.shape[1], rhs.shape[2]
    out_rows = rows * n_q // (2 * P_DEV)
    return pl.pallas_call(
        _corr_kernel,
        grid=(n_c // CH_STEP,),
        out_shape=jax.ShapeDtypeStruct((n_c, 2, P_DEV, out_rows, n_p), jnp.bfloat16),
        in_specs=[
            pl.BlockSpec((CH_STEP, rows, k), lambda i: (i, 0, 0)),
            pl.BlockSpec((CH_STEP, n_q, n_p, k), lambda i: (i, 0, 0, 0)),
        ],
        out_specs=pl.BlockSpec((CH_STEP, 2, P_DEV, out_rows, n_p), lambda i: (i, 0, 0, 0, 0)),
        scratch_shapes=[pltpu.VMEM((rows * n_q, n_p), jnp.float32)],
    )(lhs, rhs)


def solution(mesh):
    return jax.shard_map(
        per_device,
        mesh=mesh,
        in_specs=(P("row", ("col", "chan"), None), P("row", "col", None), P("row", "col")),
        out_specs=P("chan", None, "row", None, "col", None),
        check_vma=False,
    )
```

```python
import functools

import jax
import ml_dtypes
import numpy as np
import jax.numpy as jnp
from jax import lax
from jax.sharding import PartitionSpec as P
from jax.experimental import pallas as pl
from jax.experimental.pallas import tpu as pltpu

NFFT = 2048
TAPS = 4
P_DEV = 8
Q_DEV = 4
CH_DEV = 16
SPECTRA = 64
LANES = 32
FRAMES = 67


def kernel_table(nfft, taps, chans):
    length = taps * nfft
    position = np.arange(length, dtype=np.float64)
    centre = (position - length / 2 + 0.5) / nfft
    window = np.sinc(centre) * (0.5 - 0.5 * np.cos(2.0 * np.pi * (position + 0.5) / length))
    window = window * np.sqrt(2.0 / np.sum(window * window))
    window = window.reshape(taps, nfft)
    sample = np.arange(nfft, dtype=np.int64)
    bin_index = nfft // 4 + np.arange(chans, dtype=np.int64)
    phase_index = bin_index[:, None] * sample[None, :] % nfft
    phases = phase_index.astype(np.float64) * (2.0 * np.pi / nfft)
    both_parts = np.stack([np.cos(phases).T, -np.sin(phases).T], -1)
    built = window.T[:, :, None, None] * both_parts[:, None, :, :]
    return jnp.asarray(built.reshape(nfft, taps * chans * 2).astype(ml_dtypes.bfloat16))


N_CHUNK = 2


def _gather_plan(nz, nx):
    keys = []
    last = nz // 2
    for s in range(1, last + 1):
        for h in range(N_CHUNK):
            if s < last or nz % 2 or h < N_CHUNK // 2:
                keys.append(("rf", s, h))
            if s < last or (nz % 2 == 0 and h >= N_CHUNK // 2) or (nz % 2 and s <= (nz - 1) // 2):
                keys.append(("rb", s, h))
    for off in range(nz):
        for h in range(N_CHUNK):
            keys.append(("sib", off, h))
    for h in range(N_CHUNK):
        for kind in ("cf1", "cb1", "y0", "cf2", "y1", "of", "ob"):
            keys.append((kind, 0, h))
    return {k: i for i, k in enumerate(keys)}


def _gather_kernel(plan, x_ref, rowg_ref, colg_ref, send_sems, recv_sems, local_sems):
    nrow = lax.axis_size("row")
    ncol = lax.axis_size("col")
    r = lax.axis_index("row")
    c = lax.axis_index("col")
    ch = lax.axis_index("chan")
    nz = nrow // 2
    z = r // 2
    core = r % 2
    nx = ncol // 2
    yl = c // nx
    xx = c % nx
    cs = x_ref.shape[0] // N_CHUNK
    mesh_ids = pl.DeviceIdType.MESH

    def row_slot(zz, cc):
        return ((zz + nz) % nz) * 2 + cc

    def col_slot(yy, xv):
        return yy * nx + (xv + nx) % nx

    z_up = (row_slot(z + 1, core), c, ch)
    z_down = (row_slot(z - 1, core), c, ch)
    sibling = (row_slot(z, 1 - core), c, ch)
    x_up = (r, col_slot(yl, xx + 1), ch)
    x_down = (r, col_slot(yl, xx - 1), ch)
    y_other = (r, col_slot(1 - yl, xx), ch)

    barrier = pltpu.get_barrier_semaphore()
    for dev in (z_up, z_down, sibling, x_up, x_down, y_other):
        pl.semaphore_signal(barrier, inc=1, device_id=dev, device_id_type=mesh_ids)
    pl.semaphore_wait(barrier, 6)

    def chunk(ref, slot, h):
        return ref.at[slot, pl.ds(h * cs, cs)]

    def desc(src, dst, key, dev):
        i = plan[key]
        return pltpu.make_async_remote_copy(
            src_ref=src, dst_ref=dst, send_sem=send_sems.at[i],
            recv_sem=recv_sems.at[i], device_id=dev, device_id_type=mesh_ids)

    started = []

    def send(ref, slot, h, key, dev, from_input=False):
        src = x_ref.at[pl.ds(h * cs, cs)] if from_input else chunk(ref, slot, h)
        d = desc(src, chunk(ref, slot, h), key, dev)
        d.start()
        started.append(d)

    def wait_in(ref, slot, h, key):
        if key in plan:
            desc(chunk(ref, slot, h), chunk(ref, slot, h), key, z_up).wait_recv()

    local_row = pltpu.make_async_copy(x_ref, rowg_ref.at[r], local_sems.at[0])
    local_col = pltpu.make_async_copy(x_ref, colg_ref.at[c], local_sems.at[1])
    local_row.start()
    local_col.start()

    own_r = row_slot(z, core)
    own_c = col_slot(yl, xx)
    for h in range(N_CHUNK):
        if ("rf", 1, h) in plan:
            send(rowg_ref, own_r, h, ("rf", 1, h), z_up, True)
        if ("rb", 1, h) in plan:
            send(rowg_ref, own_r, h, ("rb", 1, h), z_down, True)
        send(rowg_ref, own_r, h, ("sib", 0, h), sibling, True)
        send(colg_ref, own_c, h, ("cf1", 0, h), x_up, True)
        send(colg_ref, own_c, h, ("cb1", 0, h), x_down, True)
        send(colg_ref, own_c, h, ("y0", 0, h), y_other, True)

    last = nz // 2
    for s in range(1, last + 1):
        for h in range(N_CHUNK):
            if ("rf", s, h) in plan:
                slot = row_slot(z - s, core)
                wait_in(rowg_ref, slot, h, ("rf", s, h))
                if ("rf", s + 1, h) in plan:
                    send(rowg_ref, slot, h, ("rf", s + 1, h), z_up)
                send(rowg_ref, slot, h, ("sib", (nz - s) % nz, h), sibling)
            if ("rb", s, h) in plan:
                slot = row_slot(z + s, core)
                wait_in(rowg_ref, slot, h, ("rb", s, h))
                if ("rb", s + 1, h) in plan:
                    send(rowg_ref, slot, h, ("rb", s + 1, h), z_down)
                send(rowg_ref, slot, h, ("sib", s, h), sibling)
            if s == 1:
                slot = col_slot(yl, xx - 1)
                wait_in(colg_ref, slot, h, ("cf1", 0, h))
                send(colg_ref, slot, h, ("cf2", 0, h), x_up)
                send(colg_ref, slot, h, ("y1", 0, h), y_other)
                slot = col_slot(1 - yl, xx)
                wait_in(colg_ref, slot, h, ("y0", 0, h))
                send(colg_ref, slot, h, ("ob", 0, h), x_down)
            if s == 2:
                slot = col_slot(1 - yl, xx - 1)
                wait_in(colg_ref, slot, h, ("y1", 0, h))
                send(colg_ref, slot, h, ("of", 0, h), x_up)

    for h in range(N_CHUNK):
        wait_in(colg_ref, col_slot(yl, xx + 1), h, ("cb1", 0, h))
        wait_in(colg_ref, col_slot(yl, xx - 2), h, ("cf2", 0, h))
        wait_in(colg_ref, col_slot(1 - yl, xx + 1), h, ("ob", 0, h))
        wait_in(colg_ref, col_slot(1 - yl, xx - 2), h, ("of", 0, h))
    for off in range(nz):
        for h in range(N_CHUNK):
            wait_in(rowg_ref, row_slot(z + off, 1 - core), h, ("sib", off, h))
    for d in started:
        d.wait_send()
    local_row.wait()
    local_col.wait()


def gather_both(x):
    nrow = lax.axis_size("row")
    ncol = lax.axis_size("col")
    assert ncol == 8 and nrow % 2 == 0 and x.shape[0] % N_CHUNK == 0
    plan = _gather_plan(nrow // 2, ncol // 2)
    any_spec = pl.BlockSpec(memory_space=pl.ANY)
    return pl.pallas_call(
        functools.partial(_gather_kernel, plan),
        out_shape=(
            jax.ShapeDtypeStruct((nrow,) + x.shape, x.dtype),
            jax.ShapeDtypeStruct((ncol,) + x.shape, x.dtype),
        ),
        in_specs=[any_spec],
        out_specs=(any_spec, any_spec),
        scratch_shapes=[
            pltpu.SemaphoreType.DMA((len(plan),)),
            pltpu.SemaphoreType.DMA((len(plan),)),
            pltpu.SemaphoreType.DMA((2,)),
        ],
        compiler_params=pltpu.CompilerParams(collective_id=0, has_side_effects=True),
    )(x)


def per_device(voltages, lane_map, input_flags):
    n_chan = lax.axis_size("chan")
    all_chans = CH_DEV * n_chan
    half_q = voltages.shape[1]
    table_rows = kernel_table(NFFT, TAPS, all_chans)
    frames = voltages.reshape(P_DEV, half_q, FRAMES, NFFT)
    frame_sums = jnp.einsum("pqfn,nk->pqfk", frames, table_rows, preferred_element_type=jnp.float32)
    frame_sums = frame_sums.reshape(P_DEV, half_q, FRAMES, TAPS, all_chans, 2)
    tap_sum = frame_sums[:, :, 0:SPECTRA, 0]
    for tap_idx in range(1, TAPS):
        tap_sum = tap_sum + frame_sums[:, :, tap_idx : tap_idx + SPECTRA, tap_idx]
    filtered = tap_sum.astype(jnp.bfloat16)
    filtered = filtered.transpose(3, 0, 1, 4, 2).reshape(all_chans, P_DEV, half_q, 2 * SPECTRA)
    me_chan = lax.axis_index("chan")
    halves = filtered.reshape(n_chan, CH_DEV, P_DEV, half_q, 2 * SPECTRA)
    kept = jnp.where(me_chan == 0, halves[0], halves[1])
    sent = jnp.where(me_chan == 0, halves[1], halves[0])
    received = lax.ppermute(sent, "chan", [(0, 1), (1, 0)])
    first = jnp.where(me_chan == 0, kept, received)
    second = jnp.where(me_chan == 0, received, kept)
    turned_over = jnp.concatenate([first, second], axis=2)
    lane_rows = turned_over.reshape(CH_DEV, LANES, 2 * SPECTRA)
    lane_index = lane_map.reshape(LANES)
    selector = (lane_index[:, None] == jnp.arange(LANES, dtype=jnp.int32)[None, :]).astype(
        jnp.bfloat16
    )
    reordered = jnp.einsum("kl,clz->ckz", selector, lane_rows, preferred_element_type=jnp.float32)
    weights = input_flags.reshape(LANES).astype(jnp.float32)[None, :, None]
    channelised = (
        (reordered * weights).astype(jnp.bfloat16).reshape(CH_DEV, P_DEV, Q_DEV, 2 * SPECTRA)
    )
    by_row, by_col = gather_both(channelised.reshape(CH_DEV, P_DEV * Q_DEV, 2 * SPECTRA))
    n_row = by_row.shape[0]
    grid_cols = by_col.shape[0] * Q_DEV
    row_block = (
        by_col.reshape(-1, CH_DEV, P_DEV, Q_DEV, 2 * SPECTRA)
        .transpose(1, 2, 0, 3, 4)
        .reshape(CH_DEV, P_DEV * grid_cols, 2 * SPECTRA)
    )
    col_set = (
        by_row.reshape(n_row, CH_DEV, P_DEV, Q_DEV, 2 * SPECTRA)
        .transpose(1, 0, 2, 3, 4)
        .reshape(CH_DEV, n_row * P_DEV, Q_DEV, 2 * SPECTRA)
    )
    rotated = jnp.concatenate([row_block[..., SPECTRA:], -row_block[..., :SPECTRA]], axis=-1)
    lhs = jnp.stack([row_block, rotated], axis=1).reshape(CH_DEV, 2 * row_block.shape[1], 2 * SPECTRA)
    rhs = col_set.transpose(0, 2, 1, 3)
    products = correlate(lhs, rhs)
    return products.reshape(CH_DEV, 2, P_DEV, grid_cols, Q_DEV, col_set.shape[1])


CH_STEP = 2


def _corr_kernel(lhs_ref, rhs_ref, out_ref, acc_ref):
    rows = lhs_ref.shape[1]
    n_q = rhs_ref.shape[1]
    for cc in range(lhs_ref.shape[0]):
        a = lhs_ref[cc]
        for q2 in range(n_q):
            acc_ref[pl.ds(q2, rows, stride=n_q), :] = lax.dot_general(
                a, rhs_ref[cc, q2], (((1,), (1,)), ((), ())), preferred_element_type=jnp.float32
            )
        out_ref[cc] = (acc_ref[...] * (1.0 / SPECTRA)).astype(out_ref.dtype).reshape(out_ref.shape[1:])


def correlate(lhs, rhs):
    n_c, rows, k = lhs.shape
    n_q, n_p = rhs.shape[1], rhs.shape[2]
    out_rows = rows * n_q // (2 * P_DEV)
    return pl.pallas_call(
        _corr_kernel,
        grid=(n_c // CH_STEP,),
        out_shape=jax.ShapeDtypeStruct((n_c, 2, P_DEV, out_rows, n_p), jnp.bfloat16),
        in_specs=[
            pl.BlockSpec((CH_STEP, rows, k), lambda i: (i, 0, 0)),
            pl.BlockSpec((CH_STEP, n_q, n_p, k), lambda i: (i, 0, 0, 0)),
        ],
        out_specs=pl.BlockSpec((CH_STEP, 2, P_DEV, out_rows, n_p), lambda i: (i, 0, 0, 0, 0)),
        scratch_shapes=[pltpu.VMEM((rows * n_q, n_p), jnp.float32)],
    )(lhs, rhs)


def solution(mesh):
    return jax.shard_map(
        per_device,
        mesh=mesh,
        in_specs=(P("row", ("col", "chan"), None), P("row", "col", None), P("row", "col")),
        out_specs=P("chan", None, "row", None, "col", None),
        check_vma=False,
    )
```

```python
import functools

import jax
import ml_dtypes
import numpy as np
import jax.numpy as jnp
from jax import lax
from jax.sharding import PartitionSpec as P
from jax.experimental import pallas as pl
from jax.experimental.pallas import tpu as pltpu

NFFT = 2048
TAPS = 4
P_DEV = 8
Q_DEV = 4
CH_DEV = 16
SPECTRA = 64
LANES = 32
FRAMES = 67


def kernel_table(nfft, taps, chans):
    length = taps * nfft
    position = np.arange(length, dtype=np.float64)
    centre = (position - length / 2 + 0.5) / nfft
    window = np.sinc(centre) * (0.5 - 0.5 * np.cos(2.0 * np.pi * (position + 0.5) / length))
    window = window * np.sqrt(2.0 / np.sum(window * window))
    window = window.reshape(taps, nfft)
    sample = np.arange(nfft, dtype=np.int64)
    bin_index = nfft // 4 + np.arange(chans, dtype=np.int64)
    phase_index = bin_index[:, None] * sample[None, :] % nfft
    phases = phase_index.astype(np.float64) * (2.0 * np.pi / nfft)
    both_parts = np.stack([np.cos(phases).T, -np.sin(phases).T], -1)
    built = window.T[:, :, None, None] * both_parts[:, None, :, :]
    return jnp.asarray(built.reshape(nfft, taps * chans * 2).astype(ml_dtypes.bfloat16))


def _fb_kernel(x_ref, t_ref, o_ref, xs_ref):
    half_q, frames = o_ref.shape[1], o_ref.shape[2]
    per_frame = t_ref.shape[0] // 128
    stride = per_frame * half_q
    xs_ref[...] = x_ref[0].astype(jnp.float32)
    for q in range(half_q):
        acc = None
        for j in range(0, per_frame, 2):
            a = xs_ref[pl.ds(j * half_q + q, frames, stride=stride), :]
            b = xs_ref[pl.ds((j + 1) * half_q + q, frames, stride=stride), :]
            lhs = jnp.concatenate([a, b], axis=1).astype(jnp.bfloat16)
            d = jnp.dot(lhs, t_ref[pl.ds(j * 128, 256), :], preferred_element_type=jnp.float32)
            acc = d if acc is None else acc + d
        o_ref[0, q] = acc


def filter_bank(native, table, half_q):
    n_p, rows, lanes = native.shape
    n_k = table.shape[1]
    return pl.pallas_call(
        _fb_kernel,
        grid=(n_p,),
        out_shape=jax.ShapeDtypeStruct((n_p, half_q, FRAMES, n_k), jnp.float32),
        in_specs=[
            pl.BlockSpec((1, rows, lanes), lambda i: (i, 0, 0)),
            pl.BlockSpec(table.shape, lambda i: (0, 0)),
        ],
        out_specs=pl.BlockSpec((1, half_q, FRAMES, n_k), lambda i: (i, 0, 0, 0)),
        scratch_shapes=[pltpu.VMEM((rows, lanes), jnp.float32)],
    )(native, table)


N_CHUNK = 2


def _gather_plan(nz, nx):
    keys = []
    last = nz // 2
    for s in range(1, last + 1):
        for h in range(N_CHUNK):
            if s < last or nz % 2 or h < N_CHUNK // 2:
                keys.append(("rf", s, h))
            if s < last or (nz % 2 == 0 and h >= N_CHUNK // 2) or (nz % 2 and s <= (nz - 1) // 2):
                keys.append(("rb", s, h))
    for off in range(nz):
        for h in range(N_CHUNK):
            keys.append(("sib", off, h))
    for h in range(N_CHUNK):
        for kind in ("cf1", "cb1", "y0", "cf2", "y1", "of", "ob"):
            keys.append((kind, 0, h))
    return {k: i for i, k in enumerate(keys)}


def _gather_kernel(plan, x_ref, rowg_ref, colg_ref, send_sems, recv_sems, local_sems):
    nrow = lax.axis_size("row")
    ncol = lax.axis_size("col")
    r = lax.axis_index("row")
    c = lax.axis_index("col")
    ch = lax.axis_index("chan")
    nz = nrow // 2
    z = r // 2
    core = r % 2
    nx = ncol // 2
    yl = c // nx
    xx = c % nx
    cs = x_ref.shape[0] // N_CHUNK
    mesh_ids = pl.DeviceIdType.MESH

    def row_slot(zz, cc):
        return ((zz + nz) % nz) * 2 + cc

    def col_slot(yy, xv):
        return yy * nx + (xv + nx) % nx

    z_up = (row_slot(z + 1, core), c, ch)
    z_down = (row_slot(z - 1, core), c, ch)
    sibling = (row_slot(z, 1 - core), c, ch)
    x_up = (r, col_slot(yl, xx + 1), ch)
    x_down = (r, col_slot(yl, xx - 1), ch)
    y_other = (r, col_slot(1 - yl, xx), ch)

    barrier = pltpu.get_barrier_semaphore()
    for dev in (z_up, z_down, sibling, x_up, x_down, y_other):
        pl.semaphore_signal(barrier, inc=1, device_id=dev, device_id_type=mesh_ids)
    pl.semaphore_wait(barrier, 6)

    def chunk(ref, slot, h):
        return ref.at[slot, pl.ds(h * cs, cs)]

    def desc(src, dst, key, dev):
        i = plan[key]
        return pltpu.make_async_remote_copy(
            src_ref=src, dst_ref=dst, send_sem=send_sems.at[i],
            recv_sem=recv_sems.at[i], device_id=dev, device_id_type=mesh_ids)

    started = []

    def send(ref, slot, h, key, dev, from_input=False):
        src = x_ref.at[pl.ds(h * cs, cs)] if from_input else chunk(ref, slot, h)
        d = desc(src, chunk(ref, slot, h), key, dev)
        d.start()
        started.append(d)

    def wait_in(ref, slot, h, key):
        if key in plan:
            desc(chunk(ref, slot, h), chunk(ref, slot, h), key, z_up).wait_recv()

    local_row = pltpu.make_async_copy(x_ref, rowg_ref.at[r], local_sems.at[0])
    local_col = pltpu.make_async_copy(x_ref, colg_ref.at[c], local_sems.at[1])
    local_row.start()
    local_col.start()

    own_r = row_slot(z, core)
    own_c = col_slot(yl, xx)
    for h in range(N_CHUNK):
        if ("rf", 1, h) in plan:
            send(rowg_ref, own_r, h, ("rf", 1, h), z_up, True)
        if ("rb", 1, h) in plan:
            send(rowg_ref, own_r, h, ("rb", 1, h), z_down, True)
        send(rowg_ref, own_r, h, ("sib", 0, h), sibling, True)
        send(colg_ref, own_c, h, ("cf1", 0, h), x_up, True)
        send(colg_ref, own_c, h, ("cb1", 0, h), x_down, True)
        send(colg_ref, own_c, h, ("y0", 0, h), y_other, True)

    last = nz // 2
    for s in range(1, last + 1):
        for h in range(N_CHUNK):
            if ("rf", s, h) in plan:
                slot = row_slot(z - s, core)
                wait_in(rowg_ref, slot, h, ("rf", s, h))
                if ("rf", s + 1, h) in plan:
                    send(rowg_ref, slot, h, ("rf", s + 1, h), z_up)
                send(rowg_ref, slot, h, ("sib", (nz - s) % nz, h), sibling)
            if ("rb", s, h) in plan:
                slot = row_slot(z + s, core)
                wait_in(rowg_ref, slot, h, ("rb", s, h))
                if ("rb", s + 1, h) in plan:
                    send(rowg_ref, slot, h, ("rb", s + 1, h), z_down)
                send(rowg_ref, slot, h, ("sib", s, h), sibling)
            if s == 1:
                slot = col_slot(yl, xx - 1)
                wait_in(colg_ref, slot, h, ("cf1", 0, h))
                send(colg_ref, slot, h, ("cf2", 0, h), x_up)
                send(colg_ref, slot, h, ("y1", 0, h), y_other)
                slot = col_slot(1 - yl, xx)
                wait_in(colg_ref, slot, h, ("y0", 0, h))
                send(colg_ref, slot, h, ("ob", 0, h), x_down)
            if s == 2:
                slot = col_slot(1 - yl, xx - 1)
                wait_in(colg_ref, slot, h, ("y1", 0, h))
                send(colg_ref, slot, h, ("of", 0, h), x_up)

    for h in range(N_CHUNK):
        wait_in(colg_ref, col_slot(yl, xx + 1), h, ("cb1", 0, h))
        wait_in(colg_ref, col_slot(yl, xx - 2), h, ("cf2", 0, h))
        wait_in(colg_ref, col_slot(1 - yl, xx + 1), h, ("ob", 0, h))
        wait_in(colg_ref, col_slot(1 - yl, xx - 2), h, ("of", 0, h))
    for off in range(nz):
        for h in range(N_CHUNK):
            wait_in(rowg_ref, row_slot(z + off, 1 - core), h, ("sib", off, h))
    for d in started:
        d.wait_send()
    local_row.wait()
    local_col.wait()


def gather_both(x):
    nrow = lax.axis_size("row")
    ncol = lax.axis_size("col")
    assert ncol == 8 and nrow % 2 == 0 and x.shape[0] % N_CHUNK == 0
    plan = _gather_plan(nrow // 2, ncol // 2)
    any_spec = pl.BlockSpec(memory_space=pl.ANY)
    return pl.pallas_call(
        functools.partial(_gather_kernel, plan),
        out_shape=(
            jax.ShapeDtypeStruct((nrow,) + x.shape, x.dtype),
            jax.ShapeDtypeStruct((ncol,) + x.shape, x.dtype),
        ),
        in_specs=[any_spec],
        out_specs=(any_spec, any_spec),
        scratch_shapes=[
            pltpu.SemaphoreType.DMA((len(plan),)),
            pltpu.SemaphoreType.DMA((len(plan),)),
            pltpu.SemaphoreType.DMA((2,)),
        ],
        compiler_params=pltpu.CompilerParams(collective_id=0, has_side_effects=True),
    )(x)


def per_device(voltages, lane_map, input_flags):
    n_chan = lax.axis_size("chan")
    all_chans = CH_DEV * n_chan
    half_q = voltages.shape[1]
    table_rows = kernel_table(NFFT, TAPS, all_chans)
    lane_chunks = voltages.shape[2] // 128
    native = (
        voltages.reshape(P_DEV, half_q, lane_chunks, 128)
        .transpose(0, 2, 1, 3)
        .reshape(P_DEV, lane_chunks * half_q, 128)
    )
    frame_sums = filter_bank(native, table_rows, half_q)
    frame_sums = frame_sums.reshape(P_DEV, half_q, FRAMES, TAPS, all_chans, 2)
    tap_sum = frame_sums[:, :, 0:SPECTRA, 0]
    for tap_idx in range(1, TAPS):
        tap_sum = tap_sum + frame_sums[:, :, tap_idx : tap_idx + SPECTRA, tap_idx]
    filtered = tap_sum.astype(jnp.bfloat16)
    filtered = filtered.transpose(3, 0, 1, 4, 2).reshape(all_chans, P_DEV, half_q, 2 * SPECTRA)
    me_chan = lax.axis_index("chan")
    halves = filtered.reshape(n_chan, CH_DEV, P_DEV, half_q, 2 * SPECTRA)
    kept = jnp.where(me_chan == 0, halves[0], halves[1])
    sent = jnp.where(me_chan == 0, halves[1], halves[0])
    received = lax.ppermute(sent, "chan", [(0, 1), (1, 0)])
    first = jnp.where(me_chan == 0, kept, received)
    second = jnp.where(me_chan == 0, received, kept)
    turned_over = jnp.concatenate([first, second], axis=2)
    lane_rows = turned_over.reshape(CH_DEV, LANES, 2 * SPECTRA)
    lane_index = lane_map.reshape(LANES)
    selector = (lane_index[:, None] == jnp.arange(LANES, dtype=jnp.int32)[None, :]).astype(
        jnp.bfloat16
    )
    reordered = jnp.einsum("kl,clz->ckz", selector, lane_rows, preferred_element_type=jnp.float32)
    weights = input_flags.reshape(LANES).astype(jnp.float32)[None, :, None]
    channelised = (
        (reordered * weights).astype(jnp.bfloat16).reshape(CH_DEV, P_DEV, Q_DEV, 2 * SPECTRA)
    )
    by_row, by_col = gather_both(channelised.reshape(CH_DEV, P_DEV * Q_DEV, 2 * SPECTRA))
    n_row = by_row.shape[0]
    grid_cols = by_col.shape[0] * Q_DEV
    row_block = (
        by_col.reshape(-1, CH_DEV, P_DEV, Q_DEV, 2 * SPECTRA)
        .transpose(1, 2, 0, 3, 4)
        .reshape(CH_DEV, P_DEV * grid_cols, 2 * SPECTRA)
    )
    col_set = (
        by_row.reshape(n_row, CH_DEV, P_DEV, Q_DEV, 2 * SPECTRA)
        .transpose(1, 0, 2, 3, 4)
        .reshape(CH_DEV, n_row * P_DEV, Q_DEV, 2 * SPECTRA)
    )
    rotated = jnp.concatenate([row_block[..., SPECTRA:], -row_block[..., :SPECTRA]], axis=-1)
    lhs = jnp.stack([row_block, rotated], axis=1).reshape(CH_DEV, 2 * row_block.shape[1], 2 * SPECTRA)
    rhs = col_set.transpose(0, 2, 1, 3)
    products = correlate(lhs, rhs)
    return products.reshape(CH_DEV, 2, P_DEV, grid_cols, Q_DEV, col_set.shape[1])


CH_STEP = 2


def _corr_kernel(lhs_ref, rhs_ref, out_ref, acc_ref):
    rows = lhs_ref.shape[1]
    n_q = rhs_ref.shape[1]
    for cc in range(lhs_ref.shape[0]):
        a = lhs_ref[cc]
        for q2 in range(n_q):
            acc_ref[pl.ds(q2, rows, stride=n_q), :] = lax.dot_general(
                a, rhs_ref[cc, q2], (((1,), (1,)), ((), ())), preferred_element_type=jnp.float32
            )
        out_ref[cc] = (acc_ref[...] * (1.0 / SPECTRA)).astype(out_ref.dtype).reshape(out_ref.shape[1:])


def correlate(lhs, rhs):
    n_c, rows, k = lhs.shape
    n_q, n_p = rhs.shape[1], rhs.shape[2]
    out_rows = rows * n_q // (2 * P_DEV)
    return pl.pallas_call(
        _corr_kernel,
        grid=(n_c // CH_STEP,),
        out_shape=jax.ShapeDtypeStruct((n_c, 2, P_DEV, out_rows, n_p), jnp.bfloat16),
        in_specs=[
            pl.BlockSpec((CH_STEP, rows, k), lambda i: (i, 0, 0)),
            pl.BlockSpec((CH_STEP, n_q, n_p, k), lambda i: (i, 0, 0, 0)),
        ],
        out_specs=pl.BlockSpec((CH_STEP, 2, P_DEV, out_rows, n_p), lambda i: (i, 0, 0, 0, 0)),
        scratch_shapes=[pltpu.VMEM((rows * n_q, n_p), jnp.float32)],
    )(lhs, rhs)


def solution(mesh):
    return jax.shard_map(
        per_device,
        mesh=mesh,
        in_specs=(P("row", ("col", "chan"), None), P("row", "col", None), P("row", "col")),
        out_specs=P("chan", None, "row", None, "col", None),
        check_vma=False,
    )
```

```python
import functools

import jax
import ml_dtypes
import numpy as np
import jax.numpy as jnp
from jax import lax
from jax.sharding import PartitionSpec as P
from jax.experimental import pallas as pl
from jax.experimental.pallas import tpu as pltpu

NFFT = 2048
TAPS = 4
P_DEV = 8
Q_DEV = 4
CH_DEV = 16
SPECTRA = 64
LANES = 32
FRAMES = 67


def kernel_table(nfft, taps, chans):
    length = taps * nfft
    position = np.arange(length, dtype=np.float64)
    centre = (position - length / 2 + 0.5) / nfft
    window = np.sinc(centre) * (0.5 - 0.5 * np.cos(2.0 * np.pi * (position + 0.5) / length))
    window = window * np.sqrt(2.0 / np.sum(window * window))
    window = window.reshape(taps, nfft)
    sample = np.arange(nfft, dtype=np.int64)
    bin_index = nfft // 4 + np.arange(chans, dtype=np.int64)
    phase_index = bin_index[:, None] * sample[None, :] % nfft
    phases = phase_index.astype(np.float64) * (2.0 * np.pi / nfft)
    both_parts = np.stack([np.cos(phases).T, -np.sin(phases).T], -1)
    built = window.T[:, :, None, None] * both_parts[:, None, :, :]
    return jnp.asarray(built.reshape(nfft, taps * chans * 2).astype(ml_dtypes.bfloat16))


P_STEP = 2
F_PAD = 72


def _fb_kernel(x_ref, t_ref, o_ref, xs_ref, lhs_ref, acc_ref):
    n_pp, half_q, spectra = o_ref.shape[0], o_ref.shape[1], o_ref.shape[2]
    width = o_ref.shape[3]
    frames = spectra + TAPS - 1
    per_frame = t_ref.shape[0] // 128
    stride = per_frame * half_q
    for pp in range(n_pp):
        xs_ref[pp] = x_ref[pp].astype(jnp.float32)
    lhs_ref[...] = jnp.zeros_like(lhs_ref)
    for jp in range(per_frame // 2):
        for pp in range(n_pp):
            for q in range(half_q):
                base = (pp * half_q + q) * F_PAD
                for half in range(2):
                    j = 2 * jp + half
                    lhs_ref[pl.ds(base, frames), pl.ds(half * 128, 128)] = xs_ref[
                        pp, pl.ds(j * half_q + q, frames, stride=stride), :
                    ]
        d = jnp.dot(
            lhs_ref[...].astype(jnp.bfloat16),
            t_ref[pl.ds(jp * 256, 256), :],
            preferred_element_type=jnp.float32,
        )
        if jp == 0:
            acc_ref[...] = d
        else:
            acc_ref[...] += d
    for pp in range(n_pp):
        for q in range(half_q):
            base = (pp * half_q + q) * F_PAD
            tap = None
            for m in range(TAPS):
                col = (m * width) // 128
                v = acc_ref[pl.ds(base + m, spectra), pl.ds(col * 128, 128)]
                shift = (m * width) % 128
                if shift:
                    v = pltpu.roll(v, 128 - shift, 1)
                v = v[:, :width]
                tap = v if tap is None else tap + v
            o_ref[pp, q] = tap.astype(o_ref.dtype)


def filter_bank(native, table, half_q):
    n_p, rows, lanes = native.shape
    n_k = table.shape[1]
    width = n_k // TAPS
    m_rows = P_STEP * half_q * F_PAD
    return pl.pallas_call(
        _fb_kernel,
        grid=(n_p // P_STEP,),
        out_shape=jax.ShapeDtypeStruct((n_p, half_q, SPECTRA, width), jnp.bfloat16),
        in_specs=[
            pl.BlockSpec((P_STEP, rows, lanes), lambda i: (i, 0, 0)),
            pl.BlockSpec(table.shape, lambda i: (0, 0)),
        ],
        out_specs=pl.BlockSpec((P_STEP, half_q, SPECTRA, width), lambda i: (i, 0, 0, 0)),
        scratch_shapes=[
            pltpu.VMEM((P_STEP, rows, lanes), jnp.float32),
            pltpu.VMEM((m_rows, 256), jnp.float32),
            pltpu.VMEM((m_rows, n_k), jnp.float32),
        ],
    )(native, table)


N_CHUNK = 2


def _gather_plan(nz, nx):
    keys = []
    last = nz // 2
    for s in range(1, last + 1):
        for h in range(N_CHUNK):
            if s < last or nz % 2 or h < N_CHUNK // 2:
                keys.append(("rf", s, h))
            if s < last or (nz % 2 == 0 and h >= N_CHUNK // 2) or (nz % 2 and s <= (nz - 1) // 2):
                keys.append(("rb", s, h))
    for off in range(nz):
        for h in range(N_CHUNK):
            keys.append(("sib", off, h))
    for h in range(N_CHUNK):
        for kind in ("cf1", "cb1", "y0", "cf2", "y1", "of", "ob"):
            keys.append((kind, 0, h))
    return {k: i for i, k in enumerate(keys)}


def _gather_kernel(plan, x_ref, rowg_ref, colg_ref, send_sems, recv_sems, local_sems):
    nrow = lax.axis_size("row")
    ncol = lax.axis_size("col")
    r = lax.axis_index("row")
    c = lax.axis_index("col")
    ch = lax.axis_index("chan")
    nz = nrow // 2
    z = r // 2
    core = r % 2
    nx = ncol // 2
    yl = c // nx
    xx = c % nx
    cs = x_ref.shape[0] // N_CHUNK
    mesh_ids = pl.DeviceIdType.MESH

    def row_slot(zz, cc):
        return ((zz + nz) % nz) * 2 + cc

    def col_slot(yy, xv):
        return yy * nx + (xv + nx) % nx

    z_up = (row_slot(z + 1, core), c, ch)
    z_down = (row_slot(z - 1, core), c, ch)
    sibling = (row_slot(z, 1 - core), c, ch)
    x_up = (r, col_slot(yl, xx + 1), ch)
    x_down = (r, col_slot(yl, xx - 1), ch)
    y_other = (r, col_slot(1 - yl, xx), ch)

    barrier = pltpu.get_barrier_semaphore()
    for dev in (z_up, z_down, sibling, x_up, x_down, y_other):
        pl.semaphore_signal(barrier, inc=1, device_id=dev, device_id_type=mesh_ids)
    pl.semaphore_wait(barrier, 6)

    def chunk(ref, slot, h):
        return ref.at[slot, pl.ds(h * cs, cs)]

    def desc(src, dst, key, dev):
        i = plan[key]
        return pltpu.make_async_remote_copy(
            src_ref=src, dst_ref=dst, send_sem=send_sems.at[i],
            recv_sem=recv_sems.at[i], device_id=dev, device_id_type=mesh_ids)

    started = []

    def send(ref, slot, h, key, dev, from_input=False):
        src = x_ref.at[pl.ds(h * cs, cs)] if from_input else chunk(ref, slot, h)
        d = desc(src, chunk(ref, slot, h), key, dev)
        d.start()
        started.append(d)

    def wait_in(ref, slot, h, key):
        if key in plan:
            desc(chunk(ref, slot, h), chunk(ref, slot, h), key, z_up).wait_recv()

    local_row = pltpu.make_async_copy(x_ref, rowg_ref.at[r], local_sems.at[0])
    local_col = pltpu.make_async_copy(x_ref, colg_ref.at[c], local_sems.at[1])
    local_row.start()
    local_col.start()

    own_r = row_slot(z, core)
    own_c = col_slot(yl, xx)
    for h in range(N_CHUNK):
        if ("rf", 1, h) in plan:
            send(rowg_ref, own_r, h, ("rf", 1, h), z_up, True)
        if ("rb", 1, h) in plan:
            send(rowg_ref, own_r, h, ("rb", 1, h), z_down, True)
        send(rowg_ref, own_r, h, ("sib", 0, h), sibling, True)
        send(colg_ref, own_c, h, ("cf1", 0, h), x_up, True)
        send(colg_ref, own_c, h, ("cb1", 0, h), x_down, True)
        send(colg_ref, own_c, h, ("y0", 0, h), y_other, True)

    last = nz // 2
    for s in range(1, last + 1):
        for h in range(N_CHUNK):
            if ("rf", s, h) in plan:
                slot = row_slot(z - s, core)
                wait_in(rowg_ref, slot, h, ("rf", s, h))
                if ("rf", s + 1, h) in plan:
                    send(rowg_ref, slot, h, ("rf", s + 1, h), z_up)
                send(rowg_ref, slot, h, ("sib", (nz - s) % nz, h), sibling)
            if ("rb", s, h) in plan:
                slot = row_slot(z + s, core)
                wait_in(rowg_ref, slot, h, ("rb", s, h))
                if ("rb", s + 1, h) in plan:
                    send(rowg_ref, slot, h, ("rb", s + 1, h), z_down)
                send(rowg_ref, slot, h, ("sib", s, h), sibling)
            if s == 1:
                slot = col_slot(yl, xx - 1)
                wait_in(colg_ref, slot, h, ("cf1", 0, h))
                send(colg_ref, slot, h, ("cf2", 0, h), x_up)
                send(colg_ref, slot, h, ("y1", 0, h), y_other)
                slot = col_slot(1 - yl, xx)
                wait_in(colg_ref, slot, h, ("y0", 0, h))
                send(colg_ref, slot, h, ("ob", 0, h), x_down)
            if s == 2:
                slot = col_slot(1 - yl, xx - 1)
                wait_in(colg_ref, slot, h, ("y1", 0, h))
                send(colg_ref, slot, h, ("of", 0, h), x_up)

    for h in range(N_CHUNK):
        wait_in(colg_ref, col_slot(yl, xx + 1), h, ("cb1", 0, h))
        wait_in(colg_ref, col_slot(yl, xx - 2), h, ("cf2", 0, h))
        wait_in(colg_ref, col_slot(1 - yl, xx + 1), h, ("ob", 0, h))
        wait_in(colg_ref, col_slot(1 - yl, xx - 2), h, ("of", 0, h))
    for off in range(nz):
        for h in range(N_CHUNK):
            wait_in(rowg_ref, row_slot(z + off, 1 - core), h, ("sib", off, h))
    for d in started:
        d.wait_send()
    local_row.wait()
    local_col.wait()


def gather_both(x):
    nrow = lax.axis_size("row")
    ncol = lax.axis_size("col")
    assert ncol == 8 and nrow % 2 == 0 and x.shape[0] % N_CHUNK == 0
    plan = _gather_plan(nrow // 2, ncol // 2)
    any_spec = pl.BlockSpec(memory_space=pl.ANY)
    return pl.pallas_call(
        functools.partial(_gather_kernel, plan),
        out_shape=(
            jax.ShapeDtypeStruct((nrow,) + x.shape, x.dtype),
            jax.ShapeDtypeStruct((ncol,) + x.shape, x.dtype),
        ),
        in_specs=[any_spec],
        out_specs=(any_spec, any_spec),
        scratch_shapes=[
            pltpu.SemaphoreType.DMA((len(plan),)),
            pltpu.SemaphoreType.DMA((len(plan),)),
            pltpu.SemaphoreType.DMA((2,)),
        ],
        compiler_params=pltpu.CompilerParams(collective_id=0, has_side_effects=True),
    )(x)


def per_device(voltages, lane_map, input_flags):
    n_chan = lax.axis_size("chan")
    all_chans = CH_DEV * n_chan
    half_q = voltages.shape[1]
    table_rows = kernel_table(NFFT, TAPS, all_chans)
    lane_chunks = voltages.shape[2] // 128
    native = (
        voltages.reshape(P_DEV, half_q, lane_chunks, 128)
        .transpose(0, 2, 1, 3)
        .reshape(P_DEV, lane_chunks * half_q, 128)
    )
    filtered = filter_bank(native, table_rows, half_q)
    filtered = filtered.reshape(P_DEV, half_q, SPECTRA, all_chans, 2)
    filtered = filtered.transpose(3, 0, 1, 4, 2).reshape(all_chans, P_DEV, half_q, 2 * SPECTRA)
    me_chan = lax.axis_index("chan")
    halves = filtered.reshape(n_chan, CH_DEV, P_DEV, half_q, 2 * SPECTRA)
    kept = jnp.where(me_chan == 0, halves[0], halves[1])
    sent = jnp.where(me_chan == 0, halves[1], halves[0])
    received = lax.ppermute(sent, "chan", [(0, 1), (1, 0)])
    first = jnp.where(me_chan == 0, kept, received)
    second = jnp.where(me_chan == 0, received, kept)
    turned_over = jnp.concatenate([first, second], axis=2)
    lane_rows = turned_over.reshape(CH_DEV, LANES, 2 * SPECTRA)
    lane_index = lane_map.reshape(LANES)
    selector = (lane_index[:, None] == jnp.arange(LANES, dtype=jnp.int32)[None, :]).astype(
        jnp.bfloat16
    )
    reordered = jnp.einsum("kl,clz->ckz", selector, lane_rows, preferred_element_type=jnp.float32)
    weights = input_flags.reshape(LANES).astype(jnp.float32)[None, :, None]
    channelised = (
        (reordered * weights).astype(jnp.bfloat16).reshape(CH_DEV, P_DEV, Q_DEV, 2 * SPECTRA)
    )
    by_row, by_col = gather_both(channelised.reshape(CH_DEV, P_DEV * Q_DEV, 2 * SPECTRA))
    n_row = by_row.shape[0]
    grid_cols = by_col.shape[0] * Q_DEV
    row_block = (
        by_col.reshape(-1, CH_DEV, P_DEV, Q_DEV, 2 * SPECTRA)
        .transpose(1, 2, 0, 3, 4)
        .reshape(CH_DEV, P_DEV * grid_cols, 2 * SPECTRA)
    )
    col_set = (
        by_row.reshape(n_row, CH_DEV, P_DEV, Q_DEV, 2 * SPECTRA)
        .transpose(1, 0, 2, 3, 4)
        .reshape(CH_DEV, n_row * P_DEV, Q_DEV, 2 * SPECTRA)
    )
    rotated = jnp.concatenate([row_block[..., SPECTRA:], -row_block[..., :SPECTRA]], axis=-1)
    lhs = jnp.stack([row_block, rotated], axis=1).reshape(CH_DEV, 2 * row_block.shape[1], 2 * SPECTRA)
    rhs = col_set.transpose(0, 2, 1, 3)
    products = correlate(lhs, rhs)
    return products.reshape(CH_DEV, 2, P_DEV, grid_cols, Q_DEV, col_set.shape[1])


CH_STEP = 2


def _corr_kernel(lhs_ref, rhs_ref, out_ref, acc_ref):
    rows = lhs_ref.shape[1]
    n_q = rhs_ref.shape[1]
    for cc in range(lhs_ref.shape[0]):
        a = lhs_ref[cc]
        for q2 in range(n_q):
            acc_ref[pl.ds(q2, rows, stride=n_q), :] = lax.dot_general(
                a, rhs_ref[cc, q2], (((1,), (1,)), ((), ())), preferred_element_type=jnp.float32
            )
        out_ref[cc] = (acc_ref[...] * (1.0 / SPECTRA)).astype(out_ref.dtype).reshape(out_ref.shape[1:])


def correlate(lhs, rhs):
    n_c, rows, k = lhs.shape
    n_q, n_p = rhs.shape[1], rhs.shape[2]
    out_rows = rows * n_q // (2 * P_DEV)
    return pl.pallas_call(
        _corr_kernel,
        grid=(n_c // CH_STEP,),
        out_shape=jax.ShapeDtypeStruct((n_c, 2, P_DEV, out_rows, n_p), jnp.bfloat16),
        in_specs=[
            pl.BlockSpec((CH_STEP, rows, k), lambda i: (i, 0, 0)),
            pl.BlockSpec((CH_STEP, n_q, n_p, k), lambda i: (i, 0, 0, 0)),
        ],
        out_specs=pl.BlockSpec((CH_STEP, 2, P_DEV, out_rows, n_p), lambda i: (i, 0, 0, 0, 0)),
        scratch_shapes=[pltpu.VMEM((rows * n_q, n_p), jnp.float32)],
    )(lhs, rhs)


def solution(mesh):
    return jax.shard_map(
        per_device,
        mesh=mesh,
        in_specs=(P("row", ("col", "chan"), None), P("row", "col", None), P("row", "col")),
        out_specs=P("chan", None, "row", None, "col", None),
        check_vma=False,
    )
```

```python
import functools

import jax
import ml_dtypes
import numpy as np
import jax.numpy as jnp
from jax import lax
from jax.sharding import PartitionSpec as P
from jax.experimental import pallas as pl
from jax.experimental.pallas import tpu as pltpu

NFFT = 2048
TAPS = 4
P_DEV = 8
Q_DEV = 4
CH_DEV = 16
SPECTRA = 64
LANES = 32
FRAMES = 67


def kernel_table(nfft, taps, chans):
    length = taps * nfft
    position = np.arange(length, dtype=np.float64)
    centre = (position - length / 2 + 0.5) / nfft
    window = np.sinc(centre) * (0.5 - 0.5 * np.cos(2.0 * np.pi * (position + 0.5) / length))
    window = window * np.sqrt(2.0 / np.sum(window * window))
    window = window.reshape(taps, nfft)
    sample = np.arange(nfft, dtype=np.int64)
    bin_index = nfft // 4 + np.arange(chans, dtype=np.int64)
    phase_index = bin_index[:, None] * sample[None, :] % nfft
    phases = phase_index.astype(np.float64) * (2.0 * np.pi / nfft)
    both_parts = np.stack([np.cos(phases).T, -np.sin(phases).T], -1)
    built = window.T[:, :, None, None] * both_parts[:, None, :, :]
    return jnp.asarray(built.reshape(nfft, taps * chans * 2).astype(ml_dtypes.bfloat16))


P_STEP = 2
F_PAD = 72


def _fb_kernel(x_ref, t_ref, o_ref, xs_ref, lhs_ref, acc_ref):
    n_pp, half_q, spectra = o_ref.shape[0], o_ref.shape[1], o_ref.shape[2]
    width = o_ref.shape[3]
    frames = spectra + TAPS - 1
    per_frame = t_ref.shape[0] // 128
    stride = per_frame * half_q
    for pp in range(n_pp):
        xs_ref[pp] = x_ref[pp].astype(jnp.float32)
    lhs_ref[...] = jnp.zeros_like(lhs_ref)
    for jp in range(per_frame // 2):
        for pp in range(n_pp):
            for q in range(half_q):
                base = (pp * half_q + q) * F_PAD
                for half in range(2):
                    j = 2 * jp + half
                    lhs_ref[pl.ds(base, frames), pl.ds(half * 128, 128)] = xs_ref[
                        pp, pl.ds(j * half_q + q, frames, stride=stride), :
                    ]
        d = jnp.dot(
            lhs_ref[...].astype(jnp.bfloat16),
            t_ref[pl.ds(jp * 256, 256), :],
            preferred_element_type=jnp.float32,
        )
        if jp == 0:
            acc_ref[...] = d
        else:
            acc_ref[...] += d
    for pp in range(n_pp):
        for q in range(half_q):
            base = (pp * half_q + q) * F_PAD
            tap = None
            for m in range(TAPS):
                col = (m * width) // 128
                v = acc_ref[pl.ds(base + m, spectra), pl.ds(col * 128, 128)]
                shift = (m * width) % 128
                if shift:
                    v = pltpu.roll(v, 128 - shift, 1)
                v = v[:, :width]
                tap = v if tap is None else tap + v
            o_ref[pp, q] = tap.astype(o_ref.dtype)


def filter_bank(native, table, half_q):
    n_p, rows, lanes = native.shape
    n_k = table.shape[1]
    width = n_k // TAPS
    m_rows = P_STEP * half_q * F_PAD
    return pl.pallas_call(
        _fb_kernel,
        grid=(n_p // P_STEP,),
        out_shape=jax.ShapeDtypeStruct((n_p, half_q, SPECTRA, width), jnp.bfloat16),
        in_specs=[
            pl.BlockSpec((P_STEP, rows, lanes), lambda i: (i, 0, 0)),
            pl.BlockSpec(table.shape, lambda i: (0, 0)),
        ],
        out_specs=pl.BlockSpec((P_STEP, half_q, SPECTRA, width), lambda i: (i, 0, 0, 0)),
        scratch_shapes=[
            pltpu.VMEM((P_STEP, rows, lanes), jnp.float32),
            pltpu.VMEM((m_rows, 256), jnp.float32),
            pltpu.VMEM((m_rows, n_k), jnp.float32),
        ],
    )(native, table)


N_CHUNK = 2


def _gather_plan(nz, nx):
    keys = []
    last = nz // 2
    for s in range(1, last + 1):
        for h in range(N_CHUNK):
            if s < last or nz % 2 or h < N_CHUNK // 2:
                keys.append(("rf", s, h))
            if s < last or (nz % 2 == 0 and h >= N_CHUNK // 2) or (nz % 2 and s <= (nz - 1) // 2):
                keys.append(("rb", s, h))
    for off in range(nz):
        for h in range(N_CHUNK):
            keys.append(("sib", off, h))
    for h in range(N_CHUNK):
        for kind in ("cf1", "cb1", "y0", "cf2", "y1", "of", "ob"):
            keys.append((kind, 0, h))
    return {k: i for i, k in enumerate(keys)}


def _gather_kernel(plan, x_ref, rowg_ref, colg_ref, send_sems, recv_sems, local_sems):
    nrow = lax.axis_size("row")
    ncol = lax.axis_size("col")
    r = lax.axis_index("row")
    c = lax.axis_index("col")
    ch = lax.axis_index("chan")
    nz = nrow // 2
    z = r // 2
    core = r % 2
    nx = ncol // 2
    yl = c // nx
    xx = c % nx
    cs = x_ref.shape[0] // N_CHUNK
    mesh_ids = pl.DeviceIdType.MESH

    def row_slot(zz, cc):
        return ((zz + nz) % nz) * 2 + cc

    def col_slot(yy, xv):
        return yy * nx + (xv + nx) % nx

    z_up = (row_slot(z + 1, core), c, ch)
    z_down = (row_slot(z - 1, core), c, ch)
    sibling = (row_slot(z, 1 - core), c, ch)
    x_up = (r, col_slot(yl, xx + 1), ch)
    x_down = (r, col_slot(yl, xx - 1), ch)
    y_other = (r, col_slot(1 - yl, xx), ch)

    barrier = pltpu.get_barrier_semaphore()
    for dev in (z_up, z_down, sibling, x_up, x_down, y_other):
        pl.semaphore_signal(barrier, inc=1, device_id=dev, device_id_type=mesh_ids)
    pl.semaphore_wait(barrier, 6)

    def chunk(ref, slot, h):
        return ref.at[slot, pl.ds(h * cs, cs)]

    def desc(src, dst, key, dev):
        i = plan[key]
        return pltpu.make_async_remote_copy(
            src_ref=src, dst_ref=dst, send_sem=send_sems.at[i],
            recv_sem=recv_sems.at[i], device_id=dev, device_id_type=mesh_ids)

    started = []

    def send(ref, slot, h, key, dev, from_input=False):
        src = x_ref.at[pl.ds(h * cs, cs)] if from_input else chunk(ref, slot, h)
        d = desc(src, chunk(ref, slot, h), key, dev)
        d.start()
        started.append(d)

    def wait_in(ref, slot, h, key):
        if key in plan:
            desc(chunk(ref, slot, h), chunk(ref, slot, h), key, z_up).wait_recv()

    local_row = pltpu.make_async_copy(x_ref, rowg_ref.at[r], local_sems.at[0])
    local_col = pltpu.make_async_copy(x_ref, colg_ref.at[c], local_sems.at[1])
    local_row.start()
    local_col.start()

    own_r = row_slot(z, core)
    own_c = col_slot(yl, xx)
    for h in range(N_CHUNK):
        if ("rf", 1, h) in plan:
            send(rowg_ref, own_r, h, ("rf", 1, h), z_up, True)
        if ("rb", 1, h) in plan:
            send(rowg_ref, own_r, h, ("rb", 1, h), z_down, True)
        send(rowg_ref, own_r, h, ("sib", 0, h), sibling, True)
        send(colg_ref, own_c, h, ("cf1", 0, h), x_up, True)
        send(colg_ref, own_c, h, ("cb1", 0, h), x_down, True)
        send(colg_ref, own_c, h, ("y0", 0, h), y_other, True)

    last = nz // 2
    for s in range(1, last + 1):
        for h in range(N_CHUNK):
            if ("rf", s, h) in plan:
                slot = row_slot(z - s, core)
                wait_in(rowg_ref, slot, h, ("rf", s, h))
                if ("rf", s + 1, h) in plan:
                    send(rowg_ref, slot, h, ("rf", s + 1, h), z_up)
                send(rowg_ref, slot, h, ("sib", (nz - s) % nz, h), sibling)
            if ("rb", s, h) in plan:
                slot = row_slot(z + s, core)
                wait_in(rowg_ref, slot, h, ("rb", s, h))
                if ("rb", s + 1, h) in plan:
                    send(rowg_ref, slot, h, ("rb", s + 1, h), z_down)
                send(rowg_ref, slot, h, ("sib", s, h), sibling)
            if s == 1:
                slot = col_slot(yl, xx - 1)
                wait_in(colg_ref, slot, h, ("cf1", 0, h))
                send(colg_ref, slot, h, ("cf2", 0, h), x_up)
                send(colg_ref, slot, h, ("y1", 0, h), y_other)
                slot = col_slot(1 - yl, xx)
                wait_in(colg_ref, slot, h, ("y0", 0, h))
                send(colg_ref, slot, h, ("ob", 0, h), x_down)
            if s == 2:
                slot = col_slot(1 - yl, xx - 1)
                wait_in(colg_ref, slot, h, ("y1", 0, h))
                send(colg_ref, slot, h, ("of", 0, h), x_up)

    for h in range(N_CHUNK):
        wait_in(colg_ref, col_slot(yl, xx + 1), h, ("cb1", 0, h))
        wait_in(colg_ref, col_slot(yl, xx - 2), h, ("cf2", 0, h))
        wait_in(colg_ref, col_slot(1 - yl, xx + 1), h, ("ob", 0, h))
        wait_in(colg_ref, col_slot(1 - yl, xx - 2), h, ("of", 0, h))
    for off in range(nz):
        for h in range(N_CHUNK):
            wait_in(rowg_ref, row_slot(z + off, 1 - core), h, ("sib", off, h))
    for d in started:
        d.wait_send()
    local_row.wait()
    local_col.wait()


def gather_both(x):
    nrow = lax.axis_size("row")
    ncol = lax.axis_size("col")
    assert ncol == 8 and nrow % 2 == 0 and x.shape[0] % N_CHUNK == 0
    plan = _gather_plan(nrow // 2, ncol // 2)
    any_spec = pl.BlockSpec(memory_space=pl.ANY)
    return pl.pallas_call(
        functools.partial(_gather_kernel, plan),
        out_shape=(
            jax.ShapeDtypeStruct((nrow,) + x.shape, x.dtype),
            jax.ShapeDtypeStruct((ncol,) + x.shape, x.dtype),
        ),
        in_specs=[any_spec],
        out_specs=(any_spec, any_spec),
        scratch_shapes=[
            pltpu.SemaphoreType.DMA((len(plan),)),
            pltpu.SemaphoreType.DMA((len(plan),)),
            pltpu.SemaphoreType.DMA((2,)),
        ],
        compiler_params=pltpu.CompilerParams(collective_id=0, has_side_effects=True),
    )(x)


def per_device(voltages, lane_map, input_flags):
    n_chan = lax.axis_size("chan")
    all_chans = CH_DEV * n_chan
    half_q = voltages.shape[1]
    table_rows = kernel_table(NFFT, TAPS, all_chans)
    lane_chunks = voltages.shape[2] // 128
    native = (
        voltages.reshape(P_DEV, half_q, lane_chunks, 128)
        .transpose(0, 2, 1, 3)
        .reshape(P_DEV, lane_chunks * half_q, 128)
    )
    filtered = filter_bank(native, table_rows, half_q)
    filtered = filtered.reshape(P_DEV, half_q, SPECTRA, all_chans, 2)
    filtered = filtered.transpose(3, 0, 1, 4, 2).reshape(all_chans, P_DEV, half_q, 2 * SPECTRA)
    me_chan = lax.axis_index("chan")
    halves = filtered.reshape(n_chan, CH_DEV, P_DEV, half_q, 2 * SPECTRA)
    kept = jnp.where(me_chan == 0, halves[0], halves[1])
    sent = jnp.where(me_chan == 0, halves[1], halves[0])
    received = lax.ppermute(sent, "chan", [(0, 1), (1, 0)])
    first = jnp.where(me_chan == 0, kept, received)
    second = jnp.where(me_chan == 0, received, kept)
    turned_over = jnp.concatenate([first, second], axis=2)
    lane_rows = turned_over.reshape(CH_DEV, LANES, 2 * SPECTRA)
    lane_index = lane_map.reshape(LANES)
    selector = (lane_index[:, None] == jnp.arange(LANES, dtype=jnp.int32)[None, :]).astype(
        jnp.bfloat16
    )
    reordered = jnp.einsum("kl,clz->ckz", selector, lane_rows, preferred_element_type=jnp.float32)
    weights = input_flags.reshape(LANES).astype(jnp.float32)[None, :, None]
    channelised = (
        (reordered * weights).astype(jnp.bfloat16).reshape(CH_DEV, P_DEV, Q_DEV, 2 * SPECTRA)
    )
    by_row, by_col = gather_both(channelised.reshape(CH_DEV, P_DEV * Q_DEV, 2 * SPECTRA))
    n_row = by_row.shape[0]
    grid_cols = by_col.shape[0] * Q_DEV
    row_block = (
        by_col.reshape(-1, CH_DEV, P_DEV, Q_DEV, 2 * SPECTRA)
        .transpose(1, 2, 0, 3, 4)
        .reshape(CH_DEV, P_DEV * grid_cols, 2 * SPECTRA)
    )
    products = correlate(row_block, by_row)
    return products.reshape(CH_DEV, 2, P_DEV, grid_cols, Q_DEV, n_row * P_DEV)


CH_STEP = 2


def _corr_kernel(a_ref, g_ref, out_ref, rf_ref, acc_ref):
    rows, width = a_ref.shape[1], a_ref.shape[2]
    n_j, blk = g_ref.shape[0], g_ref.shape[2]
    n_q = Q_DEV
    n_p2 = n_j * blk // n_q
    lane = lax.broadcasted_iota(jnp.int32, (rows, width), 1)
    for cc in range(a_ref.shape[0]):
        a = a_ref[cc]
        rolled = pltpu.roll(a.astype(jnp.float32), width // 2, 1)
        a_rot = jnp.where(lane >= width // 2, -rolled, rolled).astype(a.dtype)
        for j in range(n_j):
            rf_ref[pl.ds(j * blk, blk), :] = g_ref[j, cc].astype(jnp.float32)
        for q2 in range(n_q):
            b = rf_ref[pl.ds(q2, n_p2, stride=n_q), :].astype(a.dtype)
            for part, lhs in enumerate((a, a_rot)):
                acc_ref[pl.ds(part * rows * n_q + q2, rows, stride=n_q), :] = lax.dot_general(
                    lhs, b, (((1,), (1,)), ((), ())), preferred_element_type=jnp.float32
                )
        out_ref[cc] = (acc_ref[...] * (1.0 / SPECTRA)).astype(out_ref.dtype).reshape(out_ref.shape[1:])


def correlate(row_block, by_row):
    n_c, rows, k = row_block.shape
    n_j, _, blk, _ = by_row.shape
    n_p2 = n_j * blk // Q_DEV
    out_rows = rows * Q_DEV // P_DEV
    return pl.pallas_call(
        _corr_kernel,
        grid=(n_c // CH_STEP,),
        out_shape=jax.ShapeDtypeStruct((n_c, 2, P_DEV, out_rows, n_p2), jnp.bfloat16),
        in_specs=[
            pl.BlockSpec((CH_STEP, rows, k), lambda i: (i, 0, 0)),
            pl.BlockSpec((n_j, CH_STEP, blk, k), lambda i: (0, i, 0, 0)),
        ],
        out_specs=pl.BlockSpec((CH_STEP, 2, P_DEV, out_rows, n_p2), lambda i: (i, 0, 0, 0, 0)),
        scratch_shapes=[
            pltpu.VMEM((n_j * blk, k), jnp.float32),
            pltpu.VMEM((2 * rows * Q_DEV, n_p2), jnp.float32),
        ],
    )(row_block, by_row)


def solution(mesh):
    return jax.shard_map(
        per_device,
        mesh=mesh,
        in_specs=(P("row", ("col", "chan"), None), P("row", "col", None), P("row", "col")),
        out_specs=P("chan", None, "row", None, "col", None),
        check_vma=False,
    )
```

```python
import functools

import jax
import ml_dtypes
import numpy as np
import jax.numpy as jnp
from jax import lax
from jax.sharding import PartitionSpec as P
from jax.experimental import pallas as pl
from jax.experimental.pallas import tpu as pltpu

NFFT = 2048
TAPS = 4
P_DEV = 8
Q_DEV = 4
CH_DEV = 16
SPECTRA = 64
LANES = 32
FRAMES = 67


def kernel_table(nfft, taps, chans):
    length = taps * nfft
    position = np.arange(length, dtype=np.float64)
    centre = (position - length / 2 + 0.5) / nfft
    window = np.sinc(centre) * (0.5 - 0.5 * np.cos(2.0 * np.pi * (position + 0.5) / length))
    window = window * np.sqrt(2.0 / np.sum(window * window))
    window = window.reshape(taps, nfft)
    sample = np.arange(nfft, dtype=np.int64)
    bin_index = nfft // 4 + np.arange(chans, dtype=np.int64)
    phase_index = bin_index[:, None] * sample[None, :] % nfft
    phases = phase_index.astype(np.float64) * (2.0 * np.pi / nfft)
    both_parts = np.stack([np.cos(phases).T, -np.sin(phases).T], -1)
    built = window.T[:, :, None, None] * both_parts[:, None, :, :]
    return jnp.asarray(built.reshape(nfft, taps * chans * 2).astype(ml_dtypes.bfloat16))


P_STEP = 2
F_PAD = 72


def _fb_kernel(x_ref, t_ref, o_ref, xs_ref, lhs_ref, acc_ref):
    n_pp, half_q, spectra = o_ref.shape[0], o_ref.shape[1], o_ref.shape[2]
    width = o_ref.shape[3]
    frames = spectra + TAPS - 1
    per_frame = t_ref.shape[0] // 128
    stride = per_frame * half_q
    for pp in range(n_pp):
        xs_ref[pp] = x_ref[pp].astype(jnp.float32)
    lhs_ref[...] = jnp.zeros_like(lhs_ref)
    for jp in range(per_frame // 2):
        for pp in range(n_pp):
            for q in range(half_q):
                base = (pp * half_q + q) * F_PAD
                for half in range(2):
                    j = 2 * jp + half
                    lhs_ref[pl.ds(base, frames), pl.ds(half * 128, 128)] = xs_ref[
                        pp, pl.ds(j * half_q + q, frames, stride=stride), :
                    ]
        d = jnp.dot(
            lhs_ref[...].astype(jnp.bfloat16),
            t_ref[pl.ds(jp * 256, 256), :],
            preferred_element_type=jnp.float32,
        )
        if jp == 0:
            acc_ref[...] = d
        else:
            acc_ref[...] += d
    for pp in range(n_pp):
        for q in range(half_q):
            base = (pp * half_q + q) * F_PAD
            tap = None
            for m in range(TAPS):
                col = (m * width) // 128
                v = acc_ref[pl.ds(base + m, spectra), pl.ds(col * 128, 128)]
                shift = (m * width) % 128
                if shift:
                    v = pltpu.roll(v, 128 - shift, 1)
                v = v[:, :width]
                tap = v if tap is None else tap + v
            o_ref[pp, q] = tap.astype(o_ref.dtype)


def filter_bank(native, table, half_q):
    n_p, rows, lanes = native.shape
    n_k = table.shape[1]
    width = n_k // TAPS
    m_rows = P_STEP * half_q * F_PAD
    return pl.pallas_call(
        _fb_kernel,
        grid=(n_p // P_STEP,),
        out_shape=jax.ShapeDtypeStruct((n_p, half_q, SPECTRA, width), jnp.bfloat16),
        in_specs=[
            pl.BlockSpec((P_STEP, rows, lanes), lambda i: (i, 0, 0)),
            pl.BlockSpec(table.shape, lambda i: (0, 0)),
        ],
        out_specs=pl.BlockSpec((P_STEP, half_q, SPECTRA, width), lambda i: (i, 0, 0, 0)),
        scratch_shapes=[
            pltpu.VMEM((P_STEP, rows, lanes), jnp.float32),
            pltpu.VMEM((m_rows, 256), jnp.float32),
            pltpu.VMEM((m_rows, n_k), jnp.float32),
        ],
    )(native, table)


N_CHUNK = 2


def _gather_plan(nz, nx):
    keys = []
    last = nz // 2
    for s in range(1, last + 1):
        for h in range(N_CHUNK):
            if s < last or nz % 2 or h < N_CHUNK // 2:
                keys.append(("rf", s, h))
            if s < last or (nz % 2 == 0 and h >= N_CHUNK // 2) or (nz % 2 and s <= (nz - 1) // 2):
                keys.append(("rb", s, h))
    for off in range(nz):
        for h in range(N_CHUNK):
            keys.append(("sib", off, h))
    for h in range(N_CHUNK):
        for kind in ("cf1", "cb1", "y0", "cf2", "y1", "of", "ob"):
            keys.append((kind, 0, h))
    return {k: i for i, k in enumerate(keys)}


def _gather_kernel(plan, x_ref, rowg_ref, colg_ref, send_sems, recv_sems, local_sems):
    nrow = lax.axis_size("row")
    ncol = lax.axis_size("col")
    r = lax.axis_index("row")
    c = lax.axis_index("col")
    ch = lax.axis_index("chan")
    nz = nrow // 2
    z = r // 2
    core = r % 2
    nx = ncol // 2
    yl = c // nx
    xx = c % nx
    cs = x_ref.shape[0] // N_CHUNK
    mesh_ids = pl.DeviceIdType.MESH

    def row_slot(zz, cc):
        return ((zz + nz) % nz) * 2 + cc

    def col_slot(yy, xv):
        return yy * nx + (xv + nx) % nx

    z_up = (row_slot(z + 1, core), c, ch)
    z_down = (row_slot(z - 1, core), c, ch)
    sibling = (row_slot(z, 1 - core), c, ch)
    x_up = (r, col_slot(yl, xx + 1), ch)
    x_down = (r, col_slot(yl, xx - 1), ch)
    y_other = (r, col_slot(1 - yl, xx), ch)

    barrier = pltpu.get_barrier_semaphore()
    for dev in (z_up, z_down, sibling, x_up, x_down, y_other):
        pl.semaphore_signal(barrier, inc=1, device_id=dev, device_id_type=mesh_ids)
    pl.semaphore_wait(barrier, 6)

    def chunk(ref, slot, h):
        return ref.at[slot, pl.ds(h * cs, cs)]

    def desc(src, dst, key, dev):
        i = plan[key]
        return pltpu.make_async_remote_copy(
            src_ref=src, dst_ref=dst, send_sem=send_sems.at[i],
            recv_sem=recv_sems.at[i], device_id=dev, device_id_type=mesh_ids)

    started = []

    def send(ref, slot, h, key, dev, from_input=False):
        src = x_ref.at[pl.ds(h * cs, cs)] if from_input else chunk(ref, slot, h)
        d = desc(src, chunk(ref, slot, h), key, dev)
        d.start()
        started.append(d)

    def wait_in(ref, slot, h, key):
        if key in plan:
            desc(chunk(ref, slot, h), chunk(ref, slot, h), key, z_up).wait_recv()

    local_row = pltpu.make_async_copy(x_ref, rowg_ref.at[r], local_sems.at[0])
    local_col = pltpu.make_async_copy(x_ref, colg_ref.at[c], local_sems.at[1])
    local_row.start()
    local_col.start()

    own_r = row_slot(z, core)
    own_c = col_slot(yl, xx)
    for h in range(N_CHUNK):
        if ("rf", 1, h) in plan:
            send(rowg_ref, own_r, h, ("rf", 1, h), z_up, True)
        if ("rb", 1, h) in plan:
            send(rowg_ref, own_r, h, ("rb", 1, h), z_down, True)
        send(rowg_ref, own_r, h, ("sib", 0, h), sibling, True)
        send(colg_ref, own_c, h, ("cf1", 0, h), x_up, True)
        send(colg_ref, own_c, h, ("cb1", 0, h), x_down, True)
        send(colg_ref, own_c, h, ("y0", 0, h), y_other, True)

    last = nz // 2
    for s in range(1, last + 1):
        for h in range(N_CHUNK):
            if ("rf", s, h) in plan:
                slot = row_slot(z - s, core)
                wait_in(rowg_ref, slot, h, ("rf", s, h))
                if ("rf", s + 1, h) in plan:
                    send(rowg_ref, slot, h, ("rf", s + 1, h), z_up)
                send(rowg_ref, slot, h, ("sib", (nz - s) % nz, h), sibling)
            if ("rb", s, h) in plan:
                slot = row_slot(z + s, core)
                wait_in(rowg_ref, slot, h, ("rb", s, h))
                if ("rb", s + 1, h) in plan:
                    send(rowg_ref, slot, h, ("rb", s + 1, h), z_down)
                send(rowg_ref, slot, h, ("sib", s, h), sibling)
            if s == 1:
                slot = col_slot(yl, xx - 1)
                wait_in(colg_ref, slot, h, ("cf1", 0, h))
                send(colg_ref, slot, h, ("cf2", 0, h), x_up)
                send(colg_ref, slot, h, ("y1", 0, h), y_other)
                slot = col_slot(1 - yl, xx)
                wait_in(colg_ref, slot, h, ("y0", 0, h))
                send(colg_ref, slot, h, ("ob", 0, h), x_down)
            if s == 2:
                slot = col_slot(1 - yl, xx - 1)
                wait_in(colg_ref, slot, h, ("y1", 0, h))
                send(colg_ref, slot, h, ("of", 0, h), x_up)

    for h in range(N_CHUNK):
        wait_in(colg_ref, col_slot(yl, xx + 1), h, ("cb1", 0, h))
        wait_in(colg_ref, col_slot(yl, xx - 2), h, ("cf2", 0, h))
        wait_in(colg_ref, col_slot(1 - yl, xx + 1), h, ("ob", 0, h))
        wait_in(colg_ref, col_slot(1 - yl, xx - 2), h, ("of", 0, h))
    for off in range(nz):
        for h in range(N_CHUNK):
            wait_in(rowg_ref, row_slot(z + off, 1 - core), h, ("sib", off, h))
    for d in started:
        d.wait_send()
    local_row.wait()
    local_col.wait()


def gather_both(x):
    nrow = lax.axis_size("row")
    ncol = lax.axis_size("col")
    assert ncol == 8 and nrow % 2 == 0 and x.shape[0] % N_CHUNK == 0
    plan = _gather_plan(nrow // 2, ncol // 2)
    any_spec = pl.BlockSpec(memory_space=pl.ANY)
    return pl.pallas_call(
        functools.partial(_gather_kernel, plan),
        out_shape=(
            jax.ShapeDtypeStruct((nrow,) + x.shape, x.dtype),
            jax.ShapeDtypeStruct((ncol,) + x.shape, x.dtype),
        ),
        in_specs=[any_spec],
        out_specs=(any_spec, any_spec),
        scratch_shapes=[
            pltpu.SemaphoreType.DMA((len(plan),)),
            pltpu.SemaphoreType.DMA((len(plan),)),
            pltpu.SemaphoreType.DMA((2,)),
        ],
        compiler_params=pltpu.CompilerParams(collective_id=0, has_side_effects=True),
    )(x)


def per_device(voltages, lane_map, input_flags):
    n_chan = lax.axis_size("chan")
    all_chans = CH_DEV * n_chan
    half_q = voltages.shape[1]
    table_rows = kernel_table(NFFT, TAPS, all_chans)
    lane_chunks = voltages.shape[2] // 128
    native = (
        voltages.reshape(P_DEV, half_q, lane_chunks, 128)
        .transpose(0, 2, 1, 3)
        .reshape(P_DEV, lane_chunks * half_q, 128)
    )
    filtered = filter_bank(native, table_rows, half_q)
    filtered = filtered.reshape(P_DEV, half_q, SPECTRA, all_chans, 2)
    filtered = filtered.transpose(3, 0, 1, 4, 2).reshape(all_chans, P_DEV, half_q, 2 * SPECTRA)
    me_chan = lax.axis_index("chan")
    halves = filtered.reshape(n_chan, CH_DEV, P_DEV, half_q, 2 * SPECTRA)
    kept = jnp.where(me_chan == 0, halves[0], halves[1])
    sent = jnp.where(me_chan == 0, halves[1], halves[0])
    received = lax.ppermute(sent, "chan", [(0, 1), (1, 0)])
    first = jnp.where(me_chan == 0, kept, received)
    second = jnp.where(me_chan == 0, received, kept)
    turned_over = jnp.concatenate([first, second], axis=2)
    lane_rows = turned_over.reshape(CH_DEV, LANES, 2 * SPECTRA)
    lane_index = lane_map.reshape(LANES)
    selector = (lane_index[:, None] == jnp.arange(LANES, dtype=jnp.int32)[None, :]).astype(
        jnp.bfloat16
    )
    reordered = jnp.einsum("kl,clz->ckz", selector, lane_rows, preferred_element_type=jnp.float32)
    weights = input_flags.reshape(LANES).astype(jnp.float32)[None, :, None]
    channelised = (
        (reordered * weights).astype(jnp.bfloat16).reshape(CH_DEV, P_DEV, Q_DEV, 2 * SPECTRA)
    )
    by_row, by_col = gather_both(channelised.reshape(CH_DEV, P_DEV * Q_DEV, 2 * SPECTRA))
    n_row = by_row.shape[0]
    grid_cols = by_col.shape[0] * Q_DEV
    products = correlate(by_col, by_row)
    return products.reshape(CH_DEV, 2, P_DEV, grid_cols, Q_DEV, n_row * P_DEV)


CH_STEP = 2


def _corr_kernel(c_ref, g_ref, out_ref, cf_ref, lf_ref, rf_ref, acc_ref):
    n_i, blk_i, width = c_ref.shape[0], c_ref.shape[2], c_ref.shape[3]
    n_j, blk = g_ref.shape[0], g_ref.shape[2]
    n_q = Q_DEV
    n_pl = blk_i // n_q
    rows = n_i * blk_i
    n_p2 = n_j * blk // n_q
    lane = lax.broadcasted_iota(jnp.int32, (rows, width), 1)
    for cc in range(c_ref.shape[1]):
        for i in range(n_i):
            cf_ref[pl.ds(i * blk_i, blk_i), :] = c_ref[i, cc].astype(jnp.float32)
        for p in range(n_pl):
            for q in range(n_q):
                lf_ref[pl.ds(p * n_i * n_q + q, n_i, stride=n_q), :] = cf_ref[
                    pl.ds(p * n_q + q, n_i, stride=blk_i), :
                ]
        a32 = lf_ref[...]
        a = a32.astype(out_ref.dtype)
        rolled = pltpu.roll(a32, width // 2, 1)
        a_rot = jnp.where(lane >= width // 2, -rolled, rolled).astype(out_ref.dtype)
        for j in range(n_j):
            rf_ref[pl.ds(j * blk, blk), :] = g_ref[j, cc].astype(jnp.float32)
        for q2 in range(n_q):
            b = rf_ref[pl.ds(q2, n_p2, stride=n_q), :].astype(out_ref.dtype)
            for part, lhs in enumerate((a, a_rot)):
                acc_ref[pl.ds(part * rows * n_q + q2, rows, stride=n_q), :] = lax.dot_general(
                    lhs, b, (((1,), (1,)), ((), ())), preferred_element_type=jnp.float32
                )
        out_ref[cc] = (acc_ref[...] * (1.0 / SPECTRA)).astype(out_ref.dtype).reshape(out_ref.shape[1:])


def correlate(by_col, by_row):
    n_i, n_c, blk_i, k = by_col.shape
    n_j, _, blk, _ = by_row.shape
    rows = n_i * blk_i
    n_p2 = n_j * blk // Q_DEV
    out_rows = rows * Q_DEV // P_DEV
    return pl.pallas_call(
        _corr_kernel,
        grid=(n_c // CH_STEP,),
        out_shape=jax.ShapeDtypeStruct((n_c, 2, P_DEV, out_rows, n_p2), jnp.bfloat16),
        in_specs=[
            pl.BlockSpec((n_i, CH_STEP, blk_i, k), lambda i: (0, i, 0, 0)),
            pl.BlockSpec((n_j, CH_STEP, blk, k), lambda i: (0, i, 0, 0)),
        ],
        out_specs=pl.BlockSpec((CH_STEP, 2, P_DEV, out_rows, n_p2), lambda i: (i, 0, 0, 0, 0)),
        scratch_shapes=[
            pltpu.VMEM((rows, k), jnp.float32),
            pltpu.VMEM((rows, k), jnp.float32),
            pltpu.VMEM((n_j * blk, k), jnp.float32),
            pltpu.VMEM((2 * rows * Q_DEV, n_p2), jnp.float32),
        ],
    )(by_col, by_row)


def solution(mesh):
    return jax.shard_map(
        per_device,
        mesh=mesh,
        in_specs=(P("row", ("col", "chan"), None), P("row", "col", None), P("row", "col")),
        out_specs=P("chan", None, "row", None, "col", None),
        check_vma=False,
    )
```

```python
import functools

import jax
import ml_dtypes
import numpy as np
import jax.numpy as jnp
from jax import lax
from jax.sharding import PartitionSpec as P
from jax.experimental import pallas as pl
from jax.experimental.pallas import tpu as pltpu

NFFT = 2048
TAPS = 4
P_DEV = 8
Q_DEV = 4
CH_DEV = 16
SPECTRA = 64
LANES = 32
FRAMES = 67


def kernel_table(nfft, taps, chans):
    length = taps * nfft
    position = np.arange(length, dtype=np.float64)
    centre = (position - length / 2 + 0.5) / nfft
    window = np.sinc(centre) * (0.5 - 0.5 * np.cos(2.0 * np.pi * (position + 0.5) / length))
    window = window * np.sqrt(2.0 / np.sum(window * window))
    window = window.reshape(taps, nfft)
    sample = np.arange(nfft, dtype=np.int64)
    bin_index = nfft // 4 + np.arange(chans, dtype=np.int64)
    phase_index = bin_index[:, None] * sample[None, :] % nfft
    phases = phase_index.astype(np.float64) * (2.0 * np.pi / nfft)
    both_parts = np.stack([np.cos(phases).T, -np.sin(phases).T], -1)
    built = window.T[:, :, None, None] * both_parts[:, None, :, :]
    return jnp.asarray(built.reshape(nfft, taps * chans * 2).astype(ml_dtypes.bfloat16))


P_STEP = 2
F_PAD = 72


def _fb_kernel(x_ref, t_ref, o_ref, xs_ref, lhs_ref, acc_ref):
    n_pp, half_q, spectra = o_ref.shape[0], o_ref.shape[1], o_ref.shape[2]
    width = o_ref.shape[3]
    frames = spectra + TAPS - 1
    per_frame = t_ref.shape[0] // 128
    stride = per_frame * half_q
    for pp in range(n_pp):
        xs_ref[pp] = x_ref[pp].astype(jnp.float32)
    lhs_ref[...] = jnp.zeros_like(lhs_ref)
    for jp in range(per_frame // 2):
        for pp in range(n_pp):
            for q in range(half_q):
                base = (pp * half_q + q) * F_PAD
                for half in range(2):
                    j = 2 * jp + half
                    lhs_ref[pl.ds(base, frames), pl.ds(half * 128, 128)] = xs_ref[
                        pp, pl.ds(j * half_q + q, frames, stride=stride), :
                    ]
        d = jnp.dot(
            lhs_ref[...].astype(jnp.bfloat16),
            t_ref[pl.ds(jp * 256, 256), :],
            preferred_element_type=jnp.float32,
        )
        if jp == 0:
            acc_ref[...] = d
        else:
            acc_ref[...] += d
    for pp in range(n_pp):
        for q in range(half_q):
            base = (pp * half_q + q) * F_PAD
            tap = None
            for m in range(TAPS):
                col = (m * width) // 128
                v = acc_ref[pl.ds(base + m, spectra), pl.ds(col * 128, 128)]
                shift = (m * width) % 128
                if shift:
                    v = pltpu.roll(v, 128 - shift, 1)
                v = v[:, :width]
                tap = v if tap is None else tap + v
            o_ref[pp, q] = tap.astype(o_ref.dtype)


def filter_bank(native, table, half_q):
    n_p, rows, lanes = native.shape
    n_k = table.shape[1]
    width = n_k // TAPS
    m_rows = P_STEP * half_q * F_PAD
    return pl.pallas_call(
        _fb_kernel,
        grid=(n_p // P_STEP,),
        out_shape=jax.ShapeDtypeStruct((n_p, half_q, SPECTRA, width), jnp.bfloat16),
        in_specs=[
            pl.BlockSpec((P_STEP, rows, lanes), lambda i: (i, 0, 0)),
            pl.BlockSpec(table.shape, lambda i: (0, 0)),
        ],
        out_specs=pl.BlockSpec((P_STEP, half_q, SPECTRA, width), lambda i: (i, 0, 0, 0)),
        scratch_shapes=[
            pltpu.VMEM((P_STEP, rows, lanes), jnp.float32),
            pltpu.VMEM((m_rows, 256), jnp.float32),
            pltpu.VMEM((m_rows, n_k), jnp.float32),
        ],
    )(native, table)


N_CHUNK = 2


def _gather_plan(nz, nx):
    keys = []
    last = nz // 2
    for s in range(1, last + 1):
        for h in range(N_CHUNK):
            if s < last or nz % 2 or h < N_CHUNK // 2:
                keys.append(("rf", s, h))
            if s < last or (nz % 2 == 0 and h >= N_CHUNK // 2) or (nz % 2 and s <= (nz - 1) // 2):
                keys.append(("rb", s, h))
    for off in range(nz):
        for h in range(N_CHUNK):
            keys.append(("sib", off, h))
    for h in range(N_CHUNK):
        for kind in ("cf1", "cb1", "y0", "cf2", "y1", "of", "ob"):
            keys.append((kind, 0, h))
    return {k: i for i, k in enumerate(keys)}


def _gather_kernel(plan, x_ref, rowg_out, colg_out, rowg_ref, colg_ref, send_sems, recv_sems, local_sems):
    nrow = lax.axis_size("row")
    ncol = lax.axis_size("col")
    r = lax.axis_index("row")
    c = lax.axis_index("col")
    ch = lax.axis_index("chan")
    nz = nrow // 2
    z = r // 2
    core = r % 2
    nx = ncol // 2
    yl = c // nx
    xx = c % nx
    cs = x_ref.shape[0] // N_CHUNK
    mesh_ids = pl.DeviceIdType.MESH

    def row_slot(zz, cc):
        return ((zz + nz) % nz) * 2 + cc

    def col_slot(yy, xv):
        return yy * nx + (xv + nx) % nx

    z_up = (row_slot(z + 1, core), c, ch)
    z_down = (row_slot(z - 1, core), c, ch)
    sibling = (row_slot(z, 1 - core), c, ch)
    x_up = (r, col_slot(yl, xx + 1), ch)
    x_down = (r, col_slot(yl, xx - 1), ch)
    y_other = (r, col_slot(1 - yl, xx), ch)

    barrier = pltpu.get_barrier_semaphore()
    for dev in (z_up, z_down, sibling, x_up, x_down, y_other):
        pl.semaphore_signal(barrier, inc=1, device_id=dev, device_id_type=mesh_ids)
    pl.semaphore_wait(barrier, 6)

    def chunk(ref, slot, h):
        return ref.at[slot, pl.ds(h * cs, cs)]

    def desc(src, dst, key, dev):
        i = plan[key]
        return pltpu.make_async_remote_copy(
            src_ref=src, dst_ref=dst, send_sem=send_sems.at[i],
            recv_sem=recv_sems.at[i], device_id=dev, device_id_type=mesh_ids)

    started = []

    def send(ref, slot, h, key, dev, from_input=False):
        src = x_ref.at[pl.ds(h * cs, cs)] if from_input else chunk(ref, slot, h)
        d = desc(src, chunk(ref, slot, h), key, dev)
        d.start()
        started.append(d)

    def wait_in(ref, slot, h, key):
        if key in plan:
            desc(chunk(ref, slot, h), chunk(ref, slot, h), key, z_up).wait_recv()

    local_row = pltpu.make_async_copy(x_ref, rowg_ref.at[r], local_sems.at[0])
    local_col = pltpu.make_async_copy(x_ref, colg_ref.at[c], local_sems.at[1])
    local_row.start()
    local_col.start()

    own_r = row_slot(z, core)
    own_c = col_slot(yl, xx)
    for h in range(N_CHUNK):
        if ("rf", 1, h) in plan:
            send(rowg_ref, own_r, h, ("rf", 1, h), z_up, True)
        if ("rb", 1, h) in plan:
            send(rowg_ref, own_r, h, ("rb", 1, h), z_down, True)
        send(rowg_ref, own_r, h, ("sib", 0, h), sibling, True)
        send(colg_ref, own_c, h, ("cf1", 0, h), x_up, True)
        send(colg_ref, own_c, h, ("cb1", 0, h), x_down, True)
        send(colg_ref, own_c, h, ("y0", 0, h), y_other, True)

    last = nz // 2
    for s in range(1, last + 1):
        for h in range(N_CHUNK):
            if ("rf", s, h) in plan:
                slot = row_slot(z - s, core)
                wait_in(rowg_ref, slot, h, ("rf", s, h))
                if ("rf", s + 1, h) in plan:
                    send(rowg_ref, slot, h, ("rf", s + 1, h), z_up)
                send(rowg_ref, slot, h, ("sib", (nz - s) % nz, h), sibling)
            if ("rb", s, h) in plan:
                slot = row_slot(z + s, core)
                wait_in(rowg_ref, slot, h, ("rb", s, h))
                if ("rb", s + 1, h) in plan:
                    send(rowg_ref, slot, h, ("rb", s + 1, h), z_down)
                send(rowg_ref, slot, h, ("sib", s, h), sibling)
            if s == 1:
                slot = col_slot(yl, xx - 1)
                wait_in(colg_ref, slot, h, ("cf1", 0, h))
                send(colg_ref, slot, h, ("cf2", 0, h), x_up)
                send(colg_ref, slot, h, ("y1", 0, h), y_other)
                slot = col_slot(1 - yl, xx)
                wait_in(colg_ref, slot, h, ("y0", 0, h))
                send(colg_ref, slot, h, ("ob", 0, h), x_down)
            if s == 2:
                slot = col_slot(1 - yl, xx - 1)
                wait_in(colg_ref, slot, h, ("y1", 0, h))
                send(colg_ref, slot, h, ("of", 0, h), x_up)

    for h in range(N_CHUNK):
        wait_in(colg_ref, col_slot(yl, xx + 1), h, ("cb1", 0, h))
        wait_in(colg_ref, col_slot(yl, xx - 2), h, ("cf2", 0, h))
        wait_in(colg_ref, col_slot(1 - yl, xx + 1), h, ("ob", 0, h))
        wait_in(colg_ref, col_slot(1 - yl, xx - 2), h, ("of", 0, h))
    for off in range(nz):
        for h in range(N_CHUNK):
            wait_in(rowg_ref, row_slot(z + off, 1 - core), h, ("sib", off, h))
    for d in started:
        d.wait_send()
    local_row.wait()
    local_col.wait()
    out_row = pltpu.make_async_copy(rowg_ref, rowg_out, local_sems.at[0])
    out_col = pltpu.make_async_copy(colg_ref, colg_out, local_sems.at[1])
    out_row.start()
    out_col.start()
    out_row.wait()
    out_col.wait()


def gather_both(x):
    nrow = lax.axis_size("row")
    ncol = lax.axis_size("col")
    assert ncol == 8 and nrow % 2 == 0 and x.shape[0] % N_CHUNK == 0
    plan = _gather_plan(nrow // 2, ncol // 2)
    any_spec = pl.BlockSpec(memory_space=pl.ANY)
    return pl.pallas_call(
        functools.partial(_gather_kernel, plan),
        out_shape=(
            jax.ShapeDtypeStruct((nrow,) + x.shape, x.dtype),
            jax.ShapeDtypeStruct((ncol,) + x.shape, x.dtype),
        ),
        in_specs=[any_spec],
        out_specs=(any_spec, any_spec),
        scratch_shapes=[
            pltpu.VMEM((nrow,) + x.shape, x.dtype),
            pltpu.VMEM((ncol,) + x.shape, x.dtype),
            pltpu.SemaphoreType.DMA((len(plan),)),
            pltpu.SemaphoreType.DMA((len(plan),)),
            pltpu.SemaphoreType.DMA((2,)),
        ],
        compiler_params=pltpu.CompilerParams(collective_id=0, has_side_effects=True),
    )(x)


def per_device(voltages, lane_map, input_flags):
    n_chan = lax.axis_size("chan")
    all_chans = CH_DEV * n_chan
    half_q = voltages.shape[1]
    table_rows = kernel_table(NFFT, TAPS, all_chans)
    lane_chunks = voltages.shape[2] // 128
    native = (
        voltages.reshape(P_DEV, half_q, lane_chunks, 128)
        .transpose(0, 2, 1, 3)
        .reshape(P_DEV, lane_chunks * half_q, 128)
    )
    filtered = filter_bank(native, table_rows, half_q)
    filtered = filtered.reshape(P_DEV, half_q, SPECTRA, all_chans, 2)
    filtered = filtered.transpose(3, 0, 1, 4, 2).reshape(all_chans, P_DEV, half_q, 2 * SPECTRA)
    me_chan = lax.axis_index("chan")
    halves = filtered.reshape(n_chan, CH_DEV, P_DEV, half_q, 2 * SPECTRA)
    kept = jnp.where(me_chan == 0, halves[0], halves[1])
    sent = jnp.where(me_chan == 0, halves[1], halves[0])
    received = lax.ppermute(sent, "chan", [(0, 1), (1, 0)])
    first = jnp.where(me_chan == 0, kept, received)
    second = jnp.where(me_chan == 0, received, kept)
    turned_over = jnp.concatenate([first, second], axis=2)
    lane_rows = turned_over.reshape(CH_DEV, LANES, 2 * SPECTRA)
    lane_index = lane_map.reshape(LANES)
    selector = (lane_index[:, None] == jnp.arange(LANES, dtype=jnp.int32)[None, :]).astype(
        jnp.bfloat16
    )
    reordered = jnp.einsum("kl,clz->ckz", selector, lane_rows, preferred_element_type=jnp.float32)
    weights = input_flags.reshape(LANES).astype(jnp.float32)[None, :, None]
    channelised = (
        (reordered * weights).astype(jnp.bfloat16).reshape(CH_DEV, P_DEV, Q_DEV, 2 * SPECTRA)
    )
    by_row, by_col = gather_both(channelised.reshape(CH_DEV, P_DEV * Q_DEV, 2 * SPECTRA))
    n_row = by_row.shape[0]
    grid_cols = by_col.shape[0] * Q_DEV
    products = correlate(by_col, by_row)
    return products.reshape(CH_DEV, 2, P_DEV, grid_cols, Q_DEV, n_row * P_DEV)


CH_STEP = 2


def _corr_kernel(c_ref, g_ref, out_ref, cf_ref, lf_ref, rf_ref, acc_ref):
    n_i, blk_i, width = c_ref.shape[0], c_ref.shape[2], c_ref.shape[3]
    n_j, blk = g_ref.shape[0], g_ref.shape[2]
    n_q = Q_DEV
    n_pl = blk_i // n_q
    rows = n_i * blk_i
    n_p2 = n_j * blk // n_q
    lane = lax.broadcasted_iota(jnp.int32, (rows, width), 1)
    for cc in range(c_ref.shape[1]):
        for i in range(n_i):
            cf_ref[pl.ds(i * blk_i, blk_i), :] = c_ref[i, cc].astype(jnp.float32)
        for p in range(n_pl):
            for q in range(n_q):
                lf_ref[pl.ds(p * n_i * n_q + q, n_i, stride=n_q), :] = cf_ref[
                    pl.ds(p * n_q + q, n_i, stride=blk_i), :
                ]
        a32 = lf_ref[...]
        a = a32.astype(out_ref.dtype)
        rolled = pltpu.roll(a32, width // 2, 1)
        a_rot = jnp.where(lane >= width // 2, -rolled, rolled).astype(out_ref.dtype)
        for j in range(n_j):
            rf_ref[pl.ds(j * blk, blk), :] = g_ref[j, cc].astype(jnp.float32)
        for q2 in range(n_q):
            b = rf_ref[pl.ds(q2, n_p2, stride=n_q), :].astype(out_ref.dtype)
            for part, lhs in enumerate((a, a_rot)):
                acc_ref[pl.ds(part * rows * n_q + q2, rows, stride=n_q), :] = lax.dot_general(
                    lhs, b, (((1,), (1,)), ((), ())), preferred_element_type=jnp.float32
                )
        out_ref[cc] = (acc_ref[...] * (1.0 / SPECTRA)).astype(out_ref.dtype).reshape(out_ref.shape[1:])


def correlate(by_col, by_row):
    n_i, n_c, blk_i, k = by_col.shape
    n_j, _, blk, _ = by_row.shape
    rows = n_i * blk_i
    n_p2 = n_j * blk // Q_DEV
    out_rows = rows * Q_DEV // P_DEV
    return pl.pallas_call(
        _corr_kernel,
        grid=(n_c // CH_STEP,),
        out_shape=jax.ShapeDtypeStruct((n_c, 2, P_DEV, out_rows, n_p2), jnp.bfloat16),
        in_specs=[
            pl.BlockSpec((n_i, CH_STEP, blk_i, k), lambda i: (0, i, 0, 0)),
            pl.BlockSpec((n_j, CH_STEP, blk, k), lambda i: (0, i, 0, 0)),
        ],
        out_specs=pl.BlockSpec((CH_STEP, 2, P_DEV, out_rows, n_p2), lambda i: (i, 0, 0, 0, 0)),
        scratch_shapes=[
            pltpu.VMEM((rows, k), jnp.float32),
            pltpu.VMEM((rows, k), jnp.float32),
            pltpu.VMEM((n_j * blk, k), jnp.float32),
            pltpu.VMEM((2 * rows * Q_DEV, n_p2), jnp.float32),
        ],
    )(by_col, by_row)


def solution(mesh):
    return jax.shard_map(
        per_device,
        mesh=mesh,
        in_specs=(P("row", ("col", "chan"), None), P("row", "col", None), P("row", "col")),
        out_specs=P("chan", None, "row", None, "col", None),
        check_vma=False,
    )
```

```python
import functools

import jax
import ml_dtypes
import numpy as np
import jax.numpy as jnp
from jax import lax
from jax.sharding import PartitionSpec as P
from jax.experimental import pallas as pl
from jax.experimental.pallas import tpu as pltpu

NFFT = 2048
TAPS = 4
P_DEV = 8
Q_DEV = 4
CH_DEV = 16
SPECTRA = 64
LANES = 32
FRAMES = 67


def kernel_table(nfft, taps, chans):
    length = taps * nfft
    position = np.arange(length, dtype=np.float64)
    centre = (position - length / 2 + 0.5) / nfft
    window = np.sinc(centre) * (0.5 - 0.5 * np.cos(2.0 * np.pi * (position + 0.5) / length))
    window = window * np.sqrt(2.0 / np.sum(window * window))
    window = window.reshape(taps, nfft)
    sample = np.arange(nfft, dtype=np.int64)
    bin_index = nfft // 4 + np.arange(chans, dtype=np.int64)
    phase_index = bin_index[:, None] * sample[None, :] % nfft
    phases = phase_index.astype(np.float64) * (2.0 * np.pi / nfft)
    both_parts = np.stack([np.cos(phases).T, -np.sin(phases).T], -1)
    built = window.T[:, :, None, None] * both_parts[:, None, :, :]
    return jnp.asarray(built.reshape(nfft, taps * chans * 2).astype(ml_dtypes.bfloat16))


P_STEP = 2
F_PAD = 72


def _fb_kernel(x_ref, t_ref, o_ref, xs_ref, lhs_ref, acc_ref):
    n_pp, half_q, spectra = o_ref.shape[0], o_ref.shape[1], o_ref.shape[2]
    width = o_ref.shape[3]
    frames = spectra + TAPS - 1
    per_frame = t_ref.shape[0] // 128
    stride = per_frame * half_q
    for pp in range(n_pp):
        xs_ref[pp] = x_ref[pp].astype(jnp.float32)
    lhs_ref[...] = jnp.zeros_like(lhs_ref)
    for jp in range(per_frame // 2):
        for pp in range(n_pp):
            for q in range(half_q):
                base = (pp * half_q + q) * F_PAD
                for half in range(2):
                    j = 2 * jp + half
                    lhs_ref[pl.ds(base, frames), pl.ds(half * 128, 128)] = xs_ref[
                        pp, pl.ds(j * half_q + q, frames, stride=stride), :
                    ]
        d = jnp.dot(
            lhs_ref[...].astype(jnp.bfloat16),
            t_ref[pl.ds(jp * 256, 256), :],
            preferred_element_type=jnp.float32,
        )
        if jp == 0:
            acc_ref[...] = d
        else:
            acc_ref[...] += d
    for pp in range(n_pp):
        for q in range(half_q):
            base = (pp * half_q + q) * F_PAD
            tap = None
            for m in range(TAPS):
                col = (m * width) // 128
                v = acc_ref[pl.ds(base + m, spectra), pl.ds(col * 128, 128)]
                shift = (m * width) % 128
                if shift:
                    v = pltpu.roll(v, 128 - shift, 1)
                v = v[:, :width]
                tap = v if tap is None else tap + v
            o_ref[pp, q] = tap.astype(o_ref.dtype)


def filter_bank(native, table, half_q):
    n_p, rows, lanes = native.shape
    n_k = table.shape[1]
    width = n_k // TAPS
    m_rows = P_STEP * half_q * F_PAD
    return pl.pallas_call(
        _fb_kernel,
        grid=(n_p // P_STEP,),
        out_shape=jax.ShapeDtypeStruct((n_p, half_q, SPECTRA, width), jnp.bfloat16),
        in_specs=[
            pl.BlockSpec((P_STEP, rows, lanes), lambda i: (i, 0, 0)),
            pl.BlockSpec(table.shape, lambda i: (0, 0)),
        ],
        out_specs=pl.BlockSpec((P_STEP, half_q, SPECTRA, width), lambda i: (i, 0, 0, 0)),
        scratch_shapes=[
            pltpu.VMEM((P_STEP, rows, lanes), jnp.float32),
            pltpu.VMEM((m_rows, 256), jnp.float32),
            pltpu.VMEM((m_rows, n_k), jnp.float32),
        ],
    )(native, table)


N_CHUNK = 2


def _gather_plan(nz, nx):
    keys = []
    last = nz // 2
    for s in range(1, last + 1):
        for h in range(N_CHUNK):
            if s < last or nz % 2 or h < N_CHUNK // 2:
                keys.append(("rf", s, h))
            if s < last or (nz % 2 == 0 and h >= N_CHUNK // 2) or (nz % 2 and s <= (nz - 1) // 2):
                keys.append(("rb", s, h))
    for off in range(nz):
        for h in range(N_CHUNK):
            keys.append(("sib", off, h))
    for h in range(N_CHUNK):
        for kind in ("cf1", "cb1", "y0", "cf2", "y1", "of", "ob"):
            keys.append((kind, 0, h))
    return {k: i for i, k in enumerate(keys)}


def _gather_kernel(plan, x_ref, rowg_ref, colg_ref, send_sems, recv_sems, local_sems):
    nrow = lax.axis_size("row")
    ncol = lax.axis_size("col")
    r = lax.axis_index("row")
    c = lax.axis_index("col")
    ch = lax.axis_index("chan")
    nz = nrow // 2
    z = r // 2
    core = r % 2
    nx = ncol // 2
    yl = c // nx
    xx = c % nx
    cs = x_ref.shape[0] // N_CHUNK
    mesh_ids = pl.DeviceIdType.MESH

    def row_slot(zz, cc):
        return ((zz + nz) % nz) * 2 + cc

    def col_slot(yy, xv):
        return yy * nx + (xv + nx) % nx

    z_up = (row_slot(z + 1, core), c, ch)
    z_down = (row_slot(z - 1, core), c, ch)
    sibling = (row_slot(z, 1 - core), c, ch)
    x_up = (r, col_slot(yl, xx + 1), ch)
    x_down = (r, col_slot(yl, xx - 1), ch)
    y_other = (r, col_slot(1 - yl, xx), ch)

    barrier = pltpu.get_barrier_semaphore()
    for dev in (z_up, z_down, sibling, x_up, x_down, y_other):
        pl.semaphore_signal(barrier, inc=1, device_id=dev, device_id_type=mesh_ids)
    pl.semaphore_wait(barrier, 6)

    def chunk(ref, slot, h):
        return ref.at[slot, pl.ds(h * cs, cs)]

    def desc(src, dst, key, dev):
        i = plan[key]
        return pltpu.make_async_remote_copy(
            src_ref=src, dst_ref=dst, send_sem=send_sems.at[i],
            recv_sem=recv_sems.at[i], device_id=dev, device_id_type=mesh_ids)

    started = []

    def send(ref, slot, h, key, dev, from_input=False):
        src = x_ref.at[pl.ds(h * cs, cs)] if from_input else chunk(ref, slot, h)
        d = desc(src, chunk(ref, slot, h), key, dev)
        d.start()
        started.append(d)

    def wait_in(ref, slot, h, key):
        if key in plan:
            desc(chunk(ref, slot, h), chunk(ref, slot, h), key, z_up).wait_recv()

    local_row = pltpu.make_async_copy(x_ref, rowg_ref.at[r], local_sems.at[0])
    local_col = pltpu.make_async_copy(x_ref, colg_ref.at[c], local_sems.at[1])
    local_row.start()
    local_col.start()

    own_r = row_slot(z, core)
    own_c = col_slot(yl, xx)
    for h in range(N_CHUNK):
        if ("rf", 1, h) in plan:
            send(rowg_ref, own_r, h, ("rf", 1, h), z_up, True)
        if ("rb", 1, h) in plan:
            send(rowg_ref, own_r, h, ("rb", 1, h), z_down, True)
        send(rowg_ref, own_r, h, ("sib", 0, h), sibling, True)
        send(colg_ref, own_c, h, ("cf1", 0, h), x_up, True)
        send(colg_ref, own_c, h, ("cb1", 0, h), x_down, True)
        send(colg_ref, own_c, h, ("y0", 0, h), y_other, True)

    last = nz // 2
    for s in range(1, last + 1):
        for h in range(N_CHUNK):
            if ("rf", s, h) in plan:
                slot = row_slot(z - s, core)
                wait_in(rowg_ref, slot, h, ("rf", s, h))
                if ("rf", s + 1, h) in plan:
                    send(rowg_ref, slot, h, ("rf", s + 1, h), z_up)
                send(rowg_ref, slot, h, ("sib", (nz - s) % nz, h), sibling)
            if ("rb", s, h) in plan:
                slot = row_slot(z + s, core)
                wait_in(rowg_ref, slot, h, ("rb", s, h))
                if ("rb", s + 1, h) in plan:
                    send(rowg_ref, slot, h, ("rb", s + 1, h), z_down)
                send(rowg_ref, slot, h, ("sib", s, h), sibling)
            if s == 1:
                slot = col_slot(yl, xx - 1)
                wait_in(colg_ref, slot, h, ("cf1", 0, h))
                send(colg_ref, slot, h, ("cf2", 0, h), x_up)
                send(colg_ref, slot, h, ("y1", 0, h), y_other)
                slot = col_slot(1 - yl, xx)
                wait_in(colg_ref, slot, h, ("y0", 0, h))
                send(colg_ref, slot, h, ("ob", 0, h), x_down)
            if s == 2:
                slot = col_slot(1 - yl, xx - 1)
                wait_in(colg_ref, slot, h, ("y1", 0, h))
                send(colg_ref, slot, h, ("of", 0, h), x_up)

    for h in range(N_CHUNK):
        wait_in(colg_ref, col_slot(yl, xx + 1), h, ("cb1", 0, h))
        wait_in(colg_ref, col_slot(yl, xx - 2), h, ("cf2", 0, h))
        wait_in(colg_ref, col_slot(1 - yl, xx + 1), h, ("ob", 0, h))
        wait_in(colg_ref, col_slot(1 - yl, xx - 2), h, ("of", 0, h))
    for off in range(nz):
        for h in range(N_CHUNK):
            wait_in(rowg_ref, row_slot(z + off, 1 - core), h, ("sib", off, h))
    for d in started:
        d.wait_send()
    local_row.wait()
    local_col.wait()


def gather_both(x):
    nrow = lax.axis_size("row")
    ncol = lax.axis_size("col")
    assert ncol == 8 and nrow % 2 == 0 and x.shape[0] % N_CHUNK == 0
    plan = _gather_plan(nrow // 2, ncol // 2)
    any_spec = pl.BlockSpec(memory_space=pl.ANY)
    return pl.pallas_call(
        functools.partial(_gather_kernel, plan),
        out_shape=(
            jax.ShapeDtypeStruct((nrow,) + x.shape, x.dtype),
            jax.ShapeDtypeStruct((ncol,) + x.shape, x.dtype),
        ),
        in_specs=[any_spec],
        out_specs=(any_spec, any_spec),
        scratch_shapes=[
            pltpu.SemaphoreType.DMA((len(plan),)),
            pltpu.SemaphoreType.DMA((len(plan),)),
            pltpu.SemaphoreType.DMA((2,)),
        ],
        compiler_params=pltpu.CompilerParams(collective_id=0, has_side_effects=True),
    )(x)


def _chan_kernel(f_ref, o_ref, sems):
    me = lax.axis_index("chan")
    other = 1 - me
    mesh_ids = pl.DeviceIdType.MESH
    dev = (lax.axis_index("row"), lax.axis_index("col"), other)
    barrier = pltpu.get_barrier_semaphore()
    pl.semaphore_signal(barrier, inc=1, device_id=dev, device_id_type=mesh_ids)
    pl.semaphore_wait(barrier, 1)
    remote = pltpu.make_async_remote_copy(
        src_ref=f_ref.at[other], dst_ref=o_ref.at[me], send_sem=sems.at[0],
        recv_sem=sems.at[1], device_id=dev, device_id_type=mesh_ids)
    remote.start()
    local = pltpu.make_async_copy(f_ref.at[me], o_ref.at[me], sems.at[2])
    local.start()
    local.wait()
    remote.wait()


def chan_exchange(halves):
    assert halves.shape[0] == 2
    any_spec = pl.BlockSpec(memory_space=pl.ANY)
    return pl.pallas_call(
        _chan_kernel,
        out_shape=jax.ShapeDtypeStruct(halves.shape, halves.dtype),
        in_specs=[any_spec],
        out_specs=any_spec,
        scratch_shapes=[pltpu.SemaphoreType.DMA((3,))],
        compiler_params=pltpu.CompilerParams(collective_id=1, has_side_effects=True),
    )(halves)


def per_device(voltages, lane_map, input_flags):
    n_chan = lax.axis_size("chan")
    all_chans = CH_DEV * n_chan
    half_q = voltages.shape[1]
    table_rows = kernel_table(NFFT, TAPS, all_chans)
    lane_chunks = voltages.shape[2] // 128
    native = (
        voltages.reshape(P_DEV, half_q, lane_chunks, 128)
        .transpose(0, 2, 1, 3)
        .reshape(P_DEV, lane_chunks * half_q, 128)
    )
    filtered = filter_bank(native, table_rows, half_q)
    filtered = filtered.reshape(P_DEV, half_q, SPECTRA, all_chans, 2)
    filtered = filtered.transpose(3, 0, 1, 4, 2).reshape(all_chans, P_DEV, half_q, 2 * SPECTRA)
    halves = filtered.reshape(n_chan, CH_DEV, P_DEV, half_q, 2 * SPECTRA)
    turned_over = (
        chan_exchange(halves).transpose(1, 2, 0, 3, 4).reshape(CH_DEV, P_DEV, n_chan * half_q, 2 * SPECTRA)
    )
    lane_rows = turned_over.reshape(CH_DEV, LANES, 2 * SPECTRA)
    lane_index = lane_map.reshape(LANES)
    selector = (lane_index[:, None] == jnp.arange(LANES, dtype=jnp.int32)[None, :]).astype(
        jnp.bfloat16
    )
    reordered = jnp.einsum("kl,clz->ckz", selector, lane_rows, preferred_element_type=jnp.float32)
    weights = input_flags.reshape(LANES).astype(jnp.float32)[None, :, None]
    channelised = (
        (reordered * weights).astype(jnp.bfloat16).reshape(CH_DEV, P_DEV, Q_DEV, 2 * SPECTRA)
    )
    by_row, by_col = gather_both(channelised.reshape(CH_DEV, P_DEV * Q_DEV, 2 * SPECTRA))
    n_row = by_row.shape[0]
    grid_cols = by_col.shape[0] * Q_DEV
    products = correlate(by_col, by_row)
    return products.reshape(CH_DEV, 2, P_DEV, grid_cols, Q_DEV, n_row * P_DEV)


CH_STEP = 2


def _corr_kernel(c_ref, g_ref, out_ref, cf_ref, lf_ref, rf_ref, acc_ref):
    n_i, blk_i, width = c_ref.shape[0], c_ref.shape[2], c_ref.shape[3]
    n_j, blk = g_ref.shape[0], g_ref.shape[2]
    n_q = Q_DEV
    n_pl = blk_i // n_q
    rows = n_i * blk_i
    n_p2 = n_j * blk // n_q
    lane = lax.broadcasted_iota(jnp.int32, (rows, width), 1)
    for cc in range(c_ref.shape[1]):
        for i in range(n_i):
            cf_ref[pl.ds(i * blk_i, blk_i), :] = c_ref[i, cc].astype(jnp.float32)
        for p in range(n_pl):
            for q in range(n_q):
                lf_ref[pl.ds(p * n_i * n_q + q, n_i, stride=n_q), :] = cf_ref[
                    pl.ds(p * n_q + q, n_i, stride=blk_i), :
                ]
        a32 = lf_ref[...]
        a = a32.astype(out_ref.dtype)
        rolled = pltpu.roll(a32, width // 2, 1)
        a_rot = jnp.where(lane >= width // 2, -rolled, rolled).astype(out_ref.dtype)
        for j in range(n_j):
            rf_ref[pl.ds(j * blk, blk), :] = g_ref[j, cc].astype(jnp.float32)
        for q2 in range(n_q):
            b = rf_ref[pl.ds(q2, n_p2, stride=n_q), :].astype(out_ref.dtype)
            for part, lhs in enumerate((a, a_rot)):
                acc_ref[pl.ds(part * rows * n_q + q2, rows, stride=n_q), :] = lax.dot_general(
                    lhs, b, (((1,), (1,)), ((), ())), preferred_element_type=jnp.float32
                )
        out_ref[cc] = (acc_ref[...] * (1.0 / SPECTRA)).astype(out_ref.dtype).reshape(out_ref.shape[1:])


def correlate(by_col, by_row):
    n_i, n_c, blk_i, k = by_col.shape
    n_j, _, blk, _ = by_row.shape
    rows = n_i * blk_i
    n_p2 = n_j * blk // Q_DEV
    out_rows = rows * Q_DEV // P_DEV
    return pl.pallas_call(
        _corr_kernel,
        grid=(n_c // CH_STEP,),
        out_shape=jax.ShapeDtypeStruct((n_c, 2, P_DEV, out_rows, n_p2), jnp.bfloat16),
        in_specs=[
            pl.BlockSpec((n_i, CH_STEP, blk_i, k), lambda i: (0, i, 0, 0)),
            pl.BlockSpec((n_j, CH_STEP, blk, k), lambda i: (0, i, 0, 0)),
        ],
        out_specs=pl.BlockSpec((CH_STEP, 2, P_DEV, out_rows, n_p2), lambda i: (i, 0, 0, 0, 0)),
        scratch_shapes=[
            pltpu.VMEM((rows, k), jnp.float32),
            pltpu.VMEM((rows, k), jnp.float32),
            pltpu.VMEM((n_j * blk, k), jnp.float32),
            pltpu.VMEM((2 * rows * Q_DEV, n_p2), jnp.float32),
        ],
    )(by_col, by_row)


def solution(mesh):
    return jax.shard_map(
        per_device,
        mesh=mesh,
        in_specs=(P("row", ("col", "chan"), None), P("row", "col", None), P("row", "col")),
        out_specs=P("chan", None, "row", None, "col", None),
        check_vma=False,
    )
```

```python
import functools

import jax
import ml_dtypes
import numpy as np
import jax.numpy as jnp
from jax import lax
from jax.sharding import PartitionSpec as P
from jax.experimental import pallas as pl
from jax.experimental.pallas import tpu as pltpu

NFFT = 2048
TAPS = 4
P_DEV = 8
Q_DEV = 4
CH_DEV = 16
SPECTRA = 64
LANES = 32
FRAMES = 67


def kernel_table(nfft, taps, chans):
    length = taps * nfft
    position = np.arange(length, dtype=np.float64)
    centre = (position - length / 2 + 0.5) / nfft
    window = np.sinc(centre) * (0.5 - 0.5 * np.cos(2.0 * np.pi * (position + 0.5) / length))
    window = window * np.sqrt(2.0 / np.sum(window * window))
    window = window.reshape(taps, nfft)
    sample = np.arange(nfft, dtype=np.int64)
    bin_index = nfft // 4 + np.arange(chans, dtype=np.int64)
    phase_index = bin_index[:, None] * sample[None, :] % nfft
    phases = phase_index.astype(np.float64) * (2.0 * np.pi / nfft)
    both_parts = np.stack([np.cos(phases).T, -np.sin(phases).T], -1)
    built = window.T[:, :, None, None] * both_parts[:, None, :, :]
    return jnp.asarray(built.reshape(nfft, taps * chans * 2).astype(ml_dtypes.bfloat16))


P_STEP = 2
F_PAD = 72


def _fb_kernel(x_ref, t_ref, o_ref, xs_ref, lhs_ref, acc_ref):
    n_pp, half_q, spectra = o_ref.shape[0], o_ref.shape[1], o_ref.shape[2]
    width = o_ref.shape[3]
    frames = spectra + TAPS - 1
    per_frame = t_ref.shape[0] // 128
    stride = per_frame * half_q
    for pp in range(n_pp):
        xs_ref[pp] = x_ref[pp].astype(jnp.float32)
    lhs_ref[...] = jnp.zeros_like(lhs_ref)
    for jp in range(per_frame // 2):
        for pp in range(n_pp):
            for q in range(half_q):
                base = (pp * half_q + q) * F_PAD
                for half in range(2):
                    j = 2 * jp + half
                    lhs_ref[pl.ds(base, frames), pl.ds(half * 128, 128)] = xs_ref[
                        pp, pl.ds(j * half_q + q, frames, stride=stride), :
                    ]
        d = jnp.dot(
            lhs_ref[...].astype(jnp.bfloat16),
            t_ref[pl.ds(jp * 256, 256), :],
            preferred_element_type=jnp.float32,
        )
        if jp == 0:
            acc_ref[...] = d
        else:
            acc_ref[...] += d
    for pp in range(n_pp):
        for q in range(half_q):
            base = (pp * half_q + q) * F_PAD
            tap = None
            for m in range(TAPS):
                col = (m * width) // 128
                v = acc_ref[pl.ds(base + m, spectra), pl.ds(col * 128, 128)]
                shift = (m * width) % 128
                if shift:
                    v = pltpu.roll(v, 128 - shift, 1)
                v = v[:, :width]
                tap = v if tap is None else tap + v
            o_ref[pp, q] = tap.astype(o_ref.dtype)


def filter_bank(native, table, half_q):
    n_p, rows, lanes = native.shape
    n_k = table.shape[1]
    width = n_k // TAPS
    m_rows = P_STEP * half_q * F_PAD
    return pl.pallas_call(
        _fb_kernel,
        grid=(n_p // P_STEP,),
        out_shape=jax.ShapeDtypeStruct((n_p, half_q, SPECTRA, width), jnp.bfloat16),
        in_specs=[
            pl.BlockSpec((P_STEP, rows, lanes), lambda i: (i, 0, 0)),
            pl.BlockSpec(table.shape, lambda i: (0, 0)),
        ],
        out_specs=pl.BlockSpec((P_STEP, half_q, SPECTRA, width), lambda i: (i, 0, 0, 0)),
        scratch_shapes=[
            pltpu.VMEM((P_STEP, rows, lanes), jnp.float32),
            pltpu.VMEM((m_rows, 256), jnp.float32),
            pltpu.VMEM((m_rows, n_k), jnp.float32),
        ],
    )(native, table)


N_CHUNK = 2


def _gather_plan(nz, nx):
    keys = []
    last = nz // 2
    for s in range(1, last + 1):
        for h in range(N_CHUNK):
            if s < last or nz % 2 or h < N_CHUNK // 2:
                keys.append(("rf", s, h))
            if s < last or (nz % 2 == 0 and h >= N_CHUNK // 2) or (nz % 2 and s <= (nz - 1) // 2):
                keys.append(("rb", s, h))
    for h in range(N_CHUNK):
        keys.append(("rf2" if h < N_CHUNK // 2 else "rb2", last, h))
    for off in range(nz):
        for h in range(N_CHUNK):
            if off != last:
                keys.append(("sib", off, h))
    for h in range(N_CHUNK):
        for kind in ("cf1", "cb1", "y0", "cf2", "y1", "of", "ob"):
            keys.append((kind, 0, h))
    return {k: i for i, k in enumerate(keys)}


def _gather_kernel(plan, x_ref, rowg_ref, colg_ref, send_sems, recv_sems, local_sems):
    nrow = lax.axis_size("row")
    ncol = lax.axis_size("col")
    r = lax.axis_index("row")
    c = lax.axis_index("col")
    ch = lax.axis_index("chan")
    nz = nrow // 2
    z = r // 2
    core = r % 2
    nx = ncol // 2
    yl = c // nx
    xx = c % nx
    cs = x_ref.shape[0] // N_CHUNK
    mesh_ids = pl.DeviceIdType.MESH

    def row_slot(zz, cc):
        return ((zz + nz) % nz) * 2 + cc

    def col_slot(yy, xv):
        return yy * nx + (xv + nx) % nx

    z_up = (row_slot(z + 1, core), c, ch)
    z_down = (row_slot(z - 1, core), c, ch)
    sibling = (row_slot(z, 1 - core), c, ch)
    z_up_x = (row_slot(z + 1, 1 - core), c, ch)
    z_down_x = (row_slot(z - 1, 1 - core), c, ch)
    x_up = (r, col_slot(yl, xx + 1), ch)
    x_down = (r, col_slot(yl, xx - 1), ch)
    y_other = (r, col_slot(1 - yl, xx), ch)

    barrier = pltpu.get_barrier_semaphore()
    neighbours = (z_up, z_down, z_up_x, z_down_x, sibling, x_up, x_down, y_other)
    for dev in neighbours:
        pl.semaphore_signal(barrier, inc=1, device_id=dev, device_id_type=mesh_ids)
    pl.semaphore_wait(barrier, len(neighbours))

    def chunk(ref, slot, h):
        return ref.at[slot, pl.ds(h * cs, cs)]

    def desc(src, dst, key, dev):
        i = plan[key]
        return pltpu.make_async_remote_copy(
            src_ref=src, dst_ref=dst, send_sem=send_sems.at[i],
            recv_sem=recv_sems.at[i], device_id=dev, device_id_type=mesh_ids)

    started = []

    def send(ref, slot, h, key, dev, from_input=False):
        src = x_ref.at[pl.ds(h * cs, cs)] if from_input else chunk(ref, slot, h)
        d = desc(src, chunk(ref, slot, h), key, dev)
        d.start()
        started.append(d)

    def wait_in(ref, slot, h, key):
        if key in plan:
            desc(chunk(ref, slot, h), chunk(ref, slot, h), key, z_up).wait_recv()

    local_row = pltpu.make_async_copy(x_ref, rowg_ref.at[r], local_sems.at[0])
    local_col = pltpu.make_async_copy(x_ref, colg_ref.at[c], local_sems.at[1])
    local_row.start()
    local_col.start()

    own_r = row_slot(z, core)
    own_c = col_slot(yl, xx)
    for h in range(N_CHUNK):
        if ("rf", 1, h) in plan:
            send(rowg_ref, own_r, h, ("rf", 1, h), z_up, True)
        if ("rb", 1, h) in plan:
            send(rowg_ref, own_r, h, ("rb", 1, h), z_down, True)
        send(rowg_ref, own_r, h, ("sib", 0, h), sibling, True)
        send(colg_ref, own_c, h, ("cf1", 0, h), x_up, True)
        send(colg_ref, own_c, h, ("cb1", 0, h), x_down, True)
        send(colg_ref, own_c, h, ("y0", 0, h), y_other, True)

    last = nz // 2
    for s in range(1, last + 1):
        for h in range(N_CHUNK):
            if ("rf", s, h) in plan:
                slot = row_slot(z - s, core)
                wait_in(rowg_ref, slot, h, ("rf", s, h))
                if ("rf", s + 1, h) in plan:
                    send(rowg_ref, slot, h, ("rf", s + 1, h), z_up)
                if ("rf2", s + 1, h) in plan:
                    send(rowg_ref, slot, h, ("rf2", s + 1, h), z_up_x)
                if ("sib", (nz - s) % nz, h) in plan:
                    send(rowg_ref, slot, h, ("sib", (nz - s) % nz, h), sibling)
            if ("rb", s, h) in plan:
                slot = row_slot(z + s, core)
                wait_in(rowg_ref, slot, h, ("rb", s, h))
                if ("rb", s + 1, h) in plan:
                    send(rowg_ref, slot, h, ("rb", s + 1, h), z_down)
                if ("rb2", s + 1, h) in plan:
                    send(rowg_ref, slot, h, ("rb2", s + 1, h), z_down_x)
                if ("sib", s, h) in plan:
                    send(rowg_ref, slot, h, ("sib", s, h), sibling)
            if s == 1:
                slot = col_slot(yl, xx - 1)
                wait_in(colg_ref, slot, h, ("cf1", 0, h))
                send(colg_ref, slot, h, ("cf2", 0, h), x_up)
                send(colg_ref, slot, h, ("y1", 0, h), y_other)
                slot = col_slot(1 - yl, xx)
                wait_in(colg_ref, slot, h, ("y0", 0, h))
                send(colg_ref, slot, h, ("ob", 0, h), x_down)
            if s == 2:
                slot = col_slot(1 - yl, xx - 1)
                wait_in(colg_ref, slot, h, ("y1", 0, h))
                send(colg_ref, slot, h, ("of", 0, h), x_up)

    for h in range(N_CHUNK):
        wait_in(colg_ref, col_slot(yl, xx + 1), h, ("cb1", 0, h))
        wait_in(colg_ref, col_slot(yl, xx - 2), h, ("cf2", 0, h))
        wait_in(colg_ref, col_slot(1 - yl, xx + 1), h, ("ob", 0, h))
        wait_in(colg_ref, col_slot(1 - yl, xx - 2), h, ("of", 0, h))
    for off in range(nz):
        for h in range(N_CHUNK):
            wait_in(rowg_ref, row_slot(z + off, 1 - core), h, ("sib", off, h))
    for h in range(N_CHUNK):
        wait_in(rowg_ref, row_slot(z - last, 1 - core), h, ("rf2", last, h))
        wait_in(rowg_ref, row_slot(z + last, 1 - core), h, ("rb2", last, h))
    for d in started:
        d.wait_send()
    local_row.wait()
    local_col.wait()


def gather_both(x):
    nrow = lax.axis_size("row")
    ncol = lax.axis_size("col")
    assert ncol == 8 and nrow % 4 == 0 and nrow >= 8 and x.shape[0] % N_CHUNK == 0
    plan = _gather_plan(nrow // 2, ncol // 2)
    any_spec = pl.BlockSpec(memory_space=pl.ANY)
    return pl.pallas_call(
        functools.partial(_gather_kernel, plan),
        out_shape=(
            jax.ShapeDtypeStruct((nrow,) + x.shape, x.dtype),
            jax.ShapeDtypeStruct((ncol,) + x.shape, x.dtype),
        ),
        in_specs=[any_spec],
        out_specs=(any_spec, any_spec),
        scratch_shapes=[
            pltpu.SemaphoreType.DMA((len(plan),)),
            pltpu.SemaphoreType.DMA((len(plan),)),
            pltpu.SemaphoreType.DMA((2,)),
        ],
        compiler_params=pltpu.CompilerParams(collective_id=0, has_side_effects=True),
    )(x)


def per_device(voltages, lane_map, input_flags):
    n_chan = lax.axis_size("chan")
    all_chans = CH_DEV * n_chan
    half_q = voltages.shape[1]
    table_rows = kernel_table(NFFT, TAPS, all_chans)
    lane_chunks = voltages.shape[2] // 128
    native = (
        voltages.reshape(P_DEV, half_q, lane_chunks, 128)
        .transpose(0, 2, 1, 3)
        .reshape(P_DEV, lane_chunks * half_q, 128)
    )
    filtered = filter_bank(native, table_rows, half_q)
    filtered = filtered.reshape(P_DEV, half_q, SPECTRA, all_chans, 2)
    filtered = filtered.transpose(3, 0, 1, 4, 2).reshape(all_chans, P_DEV, half_q, 2 * SPECTRA)
    me_chan = lax.axis_index("chan")
    halves = filtered.reshape(n_chan, CH_DEV, P_DEV, half_q, 2 * SPECTRA)
    kept = jnp.where(me_chan == 0, halves[0], halves[1])
    sent = jnp.where(me_chan == 0, halves[1], halves[0])
    received = lax.ppermute(sent, "chan", [(0, 1), (1, 0)])
    first = jnp.where(me_chan == 0, kept, received)
    second = jnp.where(me_chan == 0, received, kept)
    turned_over = jnp.concatenate([first, second], axis=2)
    lane_rows = turned_over.reshape(CH_DEV, LANES, 2 * SPECTRA)
    lane_index = lane_map.reshape(LANES)
    selector = (lane_index[:, None] == jnp.arange(LANES, dtype=jnp.int32)[None, :]).astype(
        jnp.bfloat16
    )
    reordered = jnp.einsum("kl,clz->ckz", selector, lane_rows, preferred_element_type=jnp.float32)
    weights = input_flags.reshape(LANES).astype(jnp.float32)[None, :, None]
    channelised = (
        (reordered * weights).astype(jnp.bfloat16).reshape(CH_DEV, P_DEV, Q_DEV, 2 * SPECTRA)
    )
    by_row, by_col = gather_both(channelised.reshape(CH_DEV, P_DEV * Q_DEV, 2 * SPECTRA))
    n_row = by_row.shape[0]
    grid_cols = by_col.shape[0] * Q_DEV
    products = correlate(by_col, by_row)
    return products.reshape(CH_DEV, 2, P_DEV, grid_cols, Q_DEV, n_row * P_DEV)


CH_STEP = 2


def _corr_kernel(c_ref, g_ref, out_ref, cf_ref, lf_ref, rf_ref, acc_ref):
    n_i, blk_i, width = c_ref.shape[0], c_ref.shape[2], c_ref.shape[3]
    n_j, blk = g_ref.shape[0], g_ref.shape[2]
    n_q = Q_DEV
    n_pl = blk_i // n_q
    rows = n_i * blk_i
    n_p2 = n_j * blk // n_q
    lane = lax.broadcasted_iota(jnp.int32, (rows, width), 1)
    for cc in range(c_ref.shape[1]):
        for i in range(n_i):
            cf_ref[pl.ds(i * blk_i, blk_i), :] = c_ref[i, cc].astype(jnp.float32)
        for p in range(n_pl):
            for q in range(n_q):
                lf_ref[pl.ds(p * n_i * n_q + q, n_i, stride=n_q), :] = cf_ref[
                    pl.ds(p * n_q + q, n_i, stride=blk_i), :
                ]
        a32 = lf_ref[...]
        a = a32.astype(out_ref.dtype)
        rolled = pltpu.roll(a32, width // 2, 1)
        a_rot = jnp.where(lane >= width // 2, -rolled, rolled).astype(out_ref.dtype)
        for j in range(n_j):
            rf_ref[pl.ds(j * blk, blk), :] = g_ref[j, cc].astype(jnp.float32)
        for q2 in range(n_q):
            b = rf_ref[pl.ds(q2, n_p2, stride=n_q), :].astype(out_ref.dtype)
            for part, lhs in enumerate((a, a_rot)):
                acc_ref[pl.ds(part * rows * n_q + q2, rows, stride=n_q), :] = lax.dot_general(
                    lhs, b, (((1,), (1,)), ((), ())), preferred_element_type=jnp.float32
                )
        out_ref[cc] = (acc_ref[...] * (1.0 / SPECTRA)).astype(out_ref.dtype).reshape(out_ref.shape[1:])


def correlate(by_col, by_row):
    n_i, n_c, blk_i, k = by_col.shape
    n_j, _, blk, _ = by_row.shape
    rows = n_i * blk_i
    n_p2 = n_j * blk // Q_DEV
    out_rows = rows * Q_DEV // P_DEV
    return pl.pallas_call(
        _corr_kernel,
        grid=(n_c // CH_STEP,),
        out_shape=jax.ShapeDtypeStruct((n_c, 2, P_DEV, out_rows, n_p2), jnp.bfloat16),
        in_specs=[
            pl.BlockSpec((n_i, CH_STEP, blk_i, k), lambda i: (0, i, 0, 0)),
            pl.BlockSpec((n_j, CH_STEP, blk, k), lambda i: (0, i, 0, 0)),
        ],
        out_specs=pl.BlockSpec((CH_STEP, 2, P_DEV, out_rows, n_p2), lambda i: (i, 0, 0, 0, 0)),
        scratch_shapes=[
            pltpu.VMEM((rows, k), jnp.float32),
            pltpu.VMEM((rows, k), jnp.float32),
            pltpu.VMEM((n_j * blk, k), jnp.float32),
            pltpu.VMEM((2 * rows * Q_DEV, n_p2), jnp.float32),
        ],
    )(by_col, by_row)


def solution(mesh):
    return jax.shard_map(
        per_device,
        mesh=mesh,
        in_specs=(P("row", ("col", "chan"), None), P("row", "col", None), P("row", "col")),
        out_specs=P("chan", None, "row", None, "col", None),
        check_vma=False,
    )
```

```python
import functools

import jax
import ml_dtypes
import numpy as np
import jax.numpy as jnp
from jax import lax
from jax.sharding import PartitionSpec as P
from jax.experimental import pallas as pl
from jax.experimental.pallas import tpu as pltpu

NFFT = 2048
TAPS = 4
P_DEV = 8
Q_DEV = 4
CH_DEV = 16
SPECTRA = 64
LANES = 32
FRAMES = 67


def kernel_table(nfft, taps, chans):
    length = taps * nfft
    position = np.arange(length, dtype=np.float64)
    centre = (position - length / 2 + 0.5) / nfft
    window = np.sinc(centre) * (0.5 - 0.5 * np.cos(2.0 * np.pi * (position + 0.5) / length))
    window = window * np.sqrt(2.0 / np.sum(window * window))
    window = window.reshape(taps, nfft)
    sample = np.arange(nfft, dtype=np.int64)
    bin_index = nfft // 4 + np.arange(chans, dtype=np.int64)
    phase_index = bin_index[:, None] * sample[None, :] % nfft
    phases = phase_index.astype(np.float64) * (2.0 * np.pi / nfft)
    both_parts = np.stack([np.cos(phases).T, -np.sin(phases).T], -1)
    built = window.T[:, :, None, None] * both_parts[:, None, :, :]
    return jnp.asarray(built.reshape(nfft, taps * chans * 2).astype(ml_dtypes.bfloat16))


P_STEP = 2
F_PAD = 72


def _fb_kernel(x_ref, t_ref, o_ref, xs_ref, lhs_ref, acc_ref):
    n_pp, half_q, spectra = o_ref.shape[0], o_ref.shape[1], o_ref.shape[2]
    width = o_ref.shape[3]
    frames = spectra + TAPS - 1
    per_frame = t_ref.shape[0] // 128
    stride = per_frame * half_q
    for pp in range(n_pp):
        xs_ref[pp] = x_ref[pp].astype(jnp.float32)
    lhs_ref[...] = jnp.zeros_like(lhs_ref)
    for jp in range(per_frame // 2):
        for pp in range(n_pp):
            for q in range(half_q):
                base = (pp * half_q + q) * F_PAD
                for half in range(2):
                    j = 2 * jp + half
                    lhs_ref[pl.ds(base, frames), pl.ds(half * 128, 128)] = xs_ref[
                        pp, pl.ds(j * half_q + q, frames, stride=stride), :
                    ]
        d = jnp.dot(
            lhs_ref[...].astype(jnp.bfloat16),
            t_ref[pl.ds(jp * 256, 256), :],
            preferred_element_type=jnp.float32,
        )
        if jp == 0:
            acc_ref[...] = d
        else:
            acc_ref[...] += d
    for pp in range(n_pp):
        for q in range(half_q):
            base = (pp * half_q + q) * F_PAD
            tap = None
            for m in range(TAPS):
                col = (m * width) // 128
                v = acc_ref[pl.ds(base + m, spectra), pl.ds(col * 128, 128)]
                shift = (m * width) % 128
                if shift:
                    v = pltpu.roll(v, 128 - shift, 1)
                v = v[:, :width]
                tap = v if tap is None else tap + v
            o_ref[pp, q] = tap.astype(o_ref.dtype)


def filter_bank(native, table, half_q):
    n_p, rows, lanes = native.shape
    n_k = table.shape[1]
    width = n_k // TAPS
    m_rows = P_STEP * half_q * F_PAD
    return pl.pallas_call(
        _fb_kernel,
        grid=(n_p // P_STEP,),
        out_shape=jax.ShapeDtypeStruct((n_p, half_q, SPECTRA, width), jnp.bfloat16),
        in_specs=[
            pl.BlockSpec((P_STEP, rows, lanes), lambda i: (i, 0, 0)),
            pl.BlockSpec(table.shape, lambda i: (0, 0)),
        ],
        out_specs=pl.BlockSpec((P_STEP, half_q, SPECTRA, width), lambda i: (i, 0, 0, 0)),
        scratch_shapes=[
            pltpu.VMEM((P_STEP, rows, lanes), jnp.float32),
            pltpu.VMEM((m_rows, 256), jnp.float32),
            pltpu.VMEM((m_rows, n_k), jnp.float32),
        ],
    )(native, table)


N_CHUNK = 2


def _gather_plan(nz, nx):
    keys = []
    last = nz // 2
    for s in range(1, last + 1):
        for h in range(N_CHUNK):
            if s < last or nz % 2 or h < N_CHUNK // 2:
                keys.append(("rf", s, h))
            if s < last or (nz % 2 == 0 and h >= N_CHUNK // 2) or (nz % 2 and s <= (nz - 1) // 2):
                keys.append(("rb", s, h))
    for h in range(N_CHUNK):
        keys.append(("rf2" if h < N_CHUNK // 2 else "rb2", last, h))
    for off in range(nz):
        for h in range(N_CHUNK):
            if off != last:
                keys.append(("sib", off, h))
    for h in range(N_CHUNK):
        for kind in ("cf1", "cb1", "y0", "cf2", "y1", "of", "ob"):
            keys.append((kind, 0, h))
    return {k: i for i, k in enumerate(keys)}


def _gather_kernel(plan, x_ref, rowg_ref, colg_ref, send_sems, recv_sems, local_sems):
    nrow = lax.axis_size("row")
    ncol = lax.axis_size("col")
    r = lax.axis_index("row")
    c = lax.axis_index("col")
    ch = lax.axis_index("chan")
    nz = nrow // 2
    z = r // 2
    core = r % 2
    nx = ncol // 2
    yl = c // nx
    xx = c % nx
    cs = x_ref.shape[0] // N_CHUNK
    mesh_ids = pl.DeviceIdType.MESH

    def row_slot(zz, cc):
        return ((zz + nz) % nz) * 2 + cc

    def col_slot(yy, xv):
        return yy * nx + (xv + nx) % nx

    z_up = (row_slot(z + 1, core), c, ch)
    z_down = (row_slot(z - 1, core), c, ch)
    sibling = (row_slot(z, 1 - core), c, ch)
    z_up_x = (row_slot(z + 1, 1 - core), c, ch)
    z_down_x = (row_slot(z - 1, 1 - core), c, ch)
    x_up = (r, col_slot(yl, xx + 1), ch)
    x_down = (r, col_slot(yl, xx - 1), ch)
    y_other = (r, col_slot(1 - yl, xx), ch)

    barrier = pltpu.get_barrier_semaphore()
    neighbours = (z_up, z_down, z_up_x, z_down_x, sibling, x_up, x_down, y_other)
    for dev in neighbours:
        pl.semaphore_signal(barrier, inc=1, device_id=dev, device_id_type=mesh_ids)
    pl.semaphore_wait(barrier, len(neighbours))

    def chunk(ref, slot, h):
        return ref.at[slot, pl.ds(h * cs, cs)]

    def desc(src, dst, key, dev):
        i = plan[key]
        return pltpu.make_async_remote_copy(
            src_ref=src, dst_ref=dst, send_sem=send_sems.at[i],
            recv_sem=recv_sems.at[i], device_id=dev, device_id_type=mesh_ids)

    started = []

    def send(ref, slot, h, key, dev, from_input=False):
        src = x_ref.at[pl.ds(h * cs, cs)] if from_input else chunk(ref, slot, h)
        d = desc(src, chunk(ref, slot, h), key, dev)
        d.start()
        started.append(d)

    def wait_in(ref, slot, h, key):
        if key in plan:
            desc(chunk(ref, slot, h), chunk(ref, slot, h), key, z_up).wait_recv()

    local_row = pltpu.make_async_copy(x_ref, rowg_ref.at[r], local_sems.at[0])
    local_col = pltpu.make_async_copy(x_ref, colg_ref.at[c], local_sems.at[1])
    local_row.start()
    local_col.start()

    own_r = row_slot(z, core)
    own_c = col_slot(yl, xx)
    for h in range(N_CHUNK):
        if ("rf", 1, h) in plan:
            send(rowg_ref, own_r, h, ("rf", 1, h), z_up, True)
        if ("rb", 1, h) in plan:
            send(rowg_ref, own_r, h, ("rb", 1, h), z_down, True)
        send(rowg_ref, own_r, h, ("sib", 0, h), sibling, True)
        send(colg_ref, own_c, h, ("cf1", 0, h), x_up, True)
        send(colg_ref, own_c, h, ("cb1", 0, h), x_down, True)
        send(colg_ref, own_c, h, ("y0", 0, h), y_other, True)

    last = nz // 2
    for s in range(1, last + 1):
        for h in range(N_CHUNK):
            if ("rf", s, h) in plan:
                slot = row_slot(z - s, core)
                wait_in(rowg_ref, slot, h, ("rf", s, h))
                if ("rf", s + 1, h) in plan:
                    send(rowg_ref, slot, h, ("rf", s + 1, h), z_up)
                if ("rf2", s + 1, h) in plan:
                    send(rowg_ref, slot, h, ("rf2", s + 1, h), z_up_x)
                if ("sib", (nz - s) % nz, h) in plan:
                    send(rowg_ref, slot, h, ("sib", (nz - s) % nz, h), sibling)
            if ("rb", s, h) in plan:
                slot = row_slot(z + s, core)
                wait_in(rowg_ref, slot, h, ("rb", s, h))
                if ("rb", s + 1, h) in plan:
                    send(rowg_ref, slot, h, ("rb", s + 1, h), z_down)
                if ("rb2", s + 1, h) in plan:
                    send(rowg_ref, slot, h, ("rb2", s + 1, h), z_down_x)
                if ("sib", s, h) in plan:
                    send(rowg_ref, slot, h, ("sib", s, h), sibling)
            if s == 1:
                slot = col_slot(yl, xx - 1)
                wait_in(colg_ref, slot, h, ("cf1", 0, h))
                send(colg_ref, slot, h, ("cf2", 0, h), x_up)
                send(colg_ref, slot, h, ("y1", 0, h), y_other)
                slot = col_slot(1 - yl, xx)
                wait_in(colg_ref, slot, h, ("y0", 0, h))
                send(colg_ref, slot, h, ("ob", 0, h), x_down)
            if s == 2:
                slot = col_slot(1 - yl, xx - 1)
                wait_in(colg_ref, slot, h, ("y1", 0, h))
                send(colg_ref, slot, h, ("of", 0, h), x_up)

    for h in range(N_CHUNK):
        wait_in(colg_ref, col_slot(yl, xx + 1), h, ("cb1", 0, h))
        wait_in(colg_ref, col_slot(yl, xx - 2), h, ("cf2", 0, h))
        wait_in(colg_ref, col_slot(1 - yl, xx + 1), h, ("ob", 0, h))
        wait_in(colg_ref, col_slot(1 - yl, xx - 2), h, ("of", 0, h))
    for off in range(nz):
        for h in range(N_CHUNK):
            wait_in(rowg_ref, row_slot(z + off, 1 - core), h, ("sib", off, h))
    for h in range(N_CHUNK):
        wait_in(rowg_ref, row_slot(z - last, 1 - core), h, ("rf2", last, h))
        wait_in(rowg_ref, row_slot(z + last, 1 - core), h, ("rb2", last, h))
    for d in started:
        d.wait_send()
    local_row.wait()
    local_col.wait()


def gather_both(x):
    nrow = lax.axis_size("row")
    ncol = lax.axis_size("col")
    assert ncol == 8 and nrow % 4 == 0 and nrow >= 8 and x.shape[0] % N_CHUNK == 0
    plan = _gather_plan(nrow // 2, ncol // 2)
    any_spec = pl.BlockSpec(memory_space=pl.ANY)
    return pl.pallas_call(
        functools.partial(_gather_kernel, plan),
        out_shape=(
            jax.ShapeDtypeStruct((nrow,) + x.shape, x.dtype),
            jax.ShapeDtypeStruct((ncol,) + x.shape, x.dtype),
        ),
        in_specs=[any_spec],
        out_specs=(any_spec, any_spec),
        scratch_shapes=[
            pltpu.SemaphoreType.DMA((len(plan),)),
            pltpu.SemaphoreType.DMA((len(plan),)),
            pltpu.SemaphoreType.DMA((2,)),
        ],
        compiler_params=pltpu.CompilerParams(collective_id=0, has_side_effects=True),
    )(x)


def per_device(voltages, lane_map, input_flags):
    n_chan = lax.axis_size("chan")
    all_chans = CH_DEV * n_chan
    half_q = voltages.shape[1]
    table_rows = kernel_table(NFFT, TAPS, all_chans)
    lane_chunks = voltages.shape[2] // 128
    native = (
        voltages.reshape(P_DEV, half_q, lane_chunks, 128)
        .transpose(0, 2, 1, 3)
        .reshape(P_DEV, lane_chunks * half_q, 128)
    )
    filtered = filter_bank(native, table_rows, half_q)
    filtered = filtered.reshape(P_DEV, half_q, SPECTRA, all_chans, 2)
    filtered = filtered.transpose(3, 0, 1, 4, 2).reshape(all_chans, P_DEV, half_q, 2 * SPECTRA)
    me_chan = lax.axis_index("chan")
    halves = filtered.reshape(n_chan, CH_DEV, P_DEV, half_q, 2 * SPECTRA)
    kept = jnp.where(me_chan == 0, halves[0], halves[1])
    sent = jnp.where(me_chan == 0, halves[1], halves[0])
    received = lax.ppermute(sent, "chan", [(0, 1), (1, 0)])
    first = jnp.where(me_chan == 0, kept, received)
    second = jnp.where(me_chan == 0, received, kept)
    turned_over = jnp.concatenate([first, second], axis=2)
    lane_rows = turned_over.reshape(CH_DEV, LANES, 2 * SPECTRA)
    lane_index = lane_map.reshape(LANES)
    selector = (lane_index[:, None] == jnp.arange(LANES, dtype=jnp.int32)[None, :]).astype(
        jnp.bfloat16
    )
    reordered = jnp.einsum("kl,clz->ckz", selector, lane_rows, preferred_element_type=jnp.float32)
    weights = input_flags.reshape(LANES).astype(jnp.float32)[None, :, None]
    channelised = (
        (reordered * weights).astype(jnp.bfloat16).reshape(CH_DEV, P_DEV, Q_DEV, 2 * SPECTRA)
    )
    by_row, by_col = gather_both(channelised.reshape(CH_DEV, P_DEV * Q_DEV, 2 * SPECTRA))
    n_row = by_row.shape[0]
    grid_cols = by_col.shape[0] * Q_DEV
    products = correlate(by_col, by_row)
    return products.reshape(CH_DEV, 2, P_DEV, grid_cols, Q_DEV, n_row * P_DEV)


CH_STEP = 4


def _corr_kernel(c_ref, g_ref, out_ref, cf_ref, lf_ref, rf_ref, acc_ref):
    n_i, blk_i, width = c_ref.shape[0], c_ref.shape[2], c_ref.shape[3]
    n_j, blk = g_ref.shape[0], g_ref.shape[2]
    n_q = Q_DEV
    n_pl = blk_i // n_q
    rows = n_i * blk_i
    n_p2 = n_j * blk // n_q
    lane = lax.broadcasted_iota(jnp.int32, (rows, width), 1)
    for cc in range(c_ref.shape[1]):
        for i in range(n_i):
            cf_ref[pl.ds(i * blk_i, blk_i), :] = c_ref[i, cc].astype(jnp.float32)
        for p in range(n_pl):
            for q in range(n_q):
                lf_ref[pl.ds(p * n_i * n_q + q, n_i, stride=n_q), :] = cf_ref[
                    pl.ds(p * n_q + q, n_i, stride=blk_i), :
                ]
        a32 = lf_ref[...]
        rolled = pltpu.roll(a32, width // 2, 1)
        a_rot = jnp.where(lane >= width // 2, -rolled, rolled)
        both = jnp.concatenate([a32, a_rot], axis=0).astype(out_ref.dtype)
        for j in range(n_j):
            rf_ref[pl.ds(j * blk, blk), :] = g_ref[j, cc].astype(jnp.float32)
        for q2 in range(n_q):
            b = rf_ref[pl.ds(q2, n_p2, stride=n_q), :].astype(out_ref.dtype)
            acc_ref[pl.ds(q2, 2 * rows, stride=n_q), :] = lax.dot_general(
                both, b, (((1,), (1,)), ((), ())), preferred_element_type=jnp.float32
            )
        out_ref[cc] = (acc_ref[...] * (1.0 / SPECTRA)).astype(out_ref.dtype).reshape(out_ref.shape[1:])


def correlate(by_col, by_row):
    n_i, n_c, blk_i, k = by_col.shape
    n_j, _, blk, _ = by_row.shape
    rows = n_i * blk_i
    n_p2 = n_j * blk // Q_DEV
    out_rows = rows * Q_DEV // P_DEV
    return pl.pallas_call(
        _corr_kernel,
        grid=(n_c // CH_STEP,),
        out_shape=jax.ShapeDtypeStruct((n_c, 2, P_DEV, out_rows, n_p2), jnp.bfloat16),
        in_specs=[
            pl.BlockSpec((n_i, CH_STEP, blk_i, k), lambda i: (0, i, 0, 0)),
            pl.BlockSpec((n_j, CH_STEP, blk, k), lambda i: (0, i, 0, 0)),
        ],
        out_specs=pl.BlockSpec((CH_STEP, 2, P_DEV, out_rows, n_p2), lambda i: (i, 0, 0, 0, 0)),
        scratch_shapes=[
            pltpu.VMEM((rows, k), jnp.float32),
            pltpu.VMEM((rows, k), jnp.float32),
            pltpu.VMEM((n_j * blk, k), jnp.float32),
            pltpu.VMEM((2 * rows * Q_DEV, n_p2), jnp.float32),
        ],
    )(by_col, by_row)


def solution(mesh):
    return jax.shard_map(
        per_device,
        mesh=mesh,
        in_specs=(P("row", ("col", "chan"), None), P("row", "col", None), P("row", "col")),
        out_specs=P("chan", None, "row", None, "col", None),
        check_vma=False,
    )
```

```python
import functools

import jax
import ml_dtypes
import numpy as np
import jax.numpy as jnp
from jax import lax
from jax.sharding import PartitionSpec as P
from jax.experimental import pallas as pl
from jax.experimental.pallas import tpu as pltpu

NFFT = 2048
TAPS = 4
P_DEV = 8
Q_DEV = 4
CH_DEV = 16
SPECTRA = 64
LANES = 32
FRAMES = 67


def kernel_table(nfft, taps, chans):
    length = taps * nfft
    position = np.arange(length, dtype=np.float64)
    centre = (position - length / 2 + 0.5) / nfft
    window = np.sinc(centre) * (0.5 - 0.5 * np.cos(2.0 * np.pi * (position + 0.5) / length))
    window = window * np.sqrt(2.0 / np.sum(window * window))
    window = window.reshape(taps, nfft)
    sample = np.arange(nfft, dtype=np.int64)
    bin_index = nfft // 4 + np.arange(chans, dtype=np.int64)
    phase_index = bin_index[:, None] * sample[None, :] % nfft
    phases = phase_index.astype(np.float64) * (2.0 * np.pi / nfft)
    both_parts = np.stack([np.cos(phases).T, -np.sin(phases).T], -1)
    built = window.T[:, :, None, None] * both_parts[:, None, :, :]
    return jnp.asarray(built.reshape(nfft, taps * chans * 2).astype(ml_dtypes.bfloat16))


P_STEP = 2
F_PAD = 72


def _fb_kernel(x_ref, t_ref, o_ref, xs_ref, lhs_ref, acc_ref):
    n_pp, half_q, spectra = o_ref.shape[0], o_ref.shape[1], o_ref.shape[2]
    width = o_ref.shape[3]
    frames = spectra + TAPS - 1
    per_frame = t_ref.shape[0] // 128
    stride = per_frame * half_q
    for pp in range(n_pp):
        xs_ref[pp] = x_ref[pp].astype(jnp.float32)
    lhs_ref[...] = jnp.zeros_like(lhs_ref)
    for jp in range(per_frame // 2):
        for pp in range(n_pp):
            for q in range(half_q):
                base = (pp * half_q + q) * F_PAD
                for half in range(2):
                    j = 2 * jp + half
                    lhs_ref[pl.ds(base, frames), pl.ds(half * 128, 128)] = xs_ref[
                        pp, pl.ds(j * half_q + q, frames, stride=stride), :
                    ]
        d = jnp.dot(
            lhs_ref[...].astype(jnp.bfloat16),
            t_ref[pl.ds(jp * 256, 256), :],
            preferred_element_type=jnp.float32,
        )
        if jp == 0:
            acc_ref[...] = d
        else:
            acc_ref[...] += d
    for pp in range(n_pp):
        for q in range(half_q):
            base = (pp * half_q + q) * F_PAD
            tap = None
            for m in range(TAPS):
                col = (m * width) // 128
                v = acc_ref[pl.ds(base + m, spectra), pl.ds(col * 128, 128)]
                shift = (m * width) % 128
                if shift:
                    v = pltpu.roll(v, 128 - shift, 1)
                v = v[:, :width]
                tap = v if tap is None else tap + v
            o_ref[pp, q] = tap.astype(o_ref.dtype)


def filter_bank(native, table, half_q):
    n_p, rows, lanes = native.shape
    n_k = table.shape[1]
    width = n_k // TAPS
    m_rows = P_STEP * half_q * F_PAD
    return pl.pallas_call(
        _fb_kernel,
        grid=(n_p // P_STEP,),
        out_shape=jax.ShapeDtypeStruct((n_p, half_q, SPECTRA, width), jnp.bfloat16),
        in_specs=[
            pl.BlockSpec((P_STEP, rows, lanes), lambda i: (i, 0, 0)),
            pl.BlockSpec(table.shape, lambda i: (0, 0)),
        ],
        out_specs=pl.BlockSpec((P_STEP, half_q, SPECTRA, width), lambda i: (i, 0, 0, 0)),
        scratch_shapes=[
            pltpu.VMEM((P_STEP, rows, lanes), jnp.float32),
            pltpu.VMEM((m_rows, 256), jnp.float32),
            pltpu.VMEM((m_rows, n_k), jnp.float32),
        ],
    )(native, table)


N_CHUNK = 4


def _gather_plan(nz, nx):
    keys = []
    last = nz // 2
    for s in range(1, last + 1):
        for h in range(N_CHUNK):
            if s < last or nz % 2 or h < N_CHUNK // 2:
                keys.append(("rf", s, h))
            if s < last or (nz % 2 == 0 and h >= N_CHUNK // 2) or (nz % 2 and s <= (nz - 1) // 2):
                keys.append(("rb", s, h))
    for h in range(N_CHUNK):
        keys.append(("rf2" if h < N_CHUNK // 2 else "rb2", last, h))
    for off in range(nz):
        for h in range(N_CHUNK):
            if off != last:
                keys.append(("sib", off, h))
    for h in range(N_CHUNK):
        for kind in ("cf1", "cb1", "y0", "cf2", "y1", "of", "ob"):
            keys.append((kind, 0, h))
    return {k: i for i, k in enumerate(keys)}


def _gather_kernel(plan, x_ref, rowg_ref, colg_ref, send_sems, recv_sems, local_sems):
    nrow = lax.axis_size("row")
    ncol = lax.axis_size("col")
    r = lax.axis_index("row")
    c = lax.axis_index("col")
    ch = lax.axis_index("chan")
    nz = nrow // 2
    z = r // 2
    core = r % 2
    nx = ncol // 2
    yl = c // nx
    xx = c % nx
    cs = x_ref.shape[0] // N_CHUNK
    mesh_ids = pl.DeviceIdType.MESH

    def row_slot(zz, cc):
        return ((zz + nz) % nz) * 2 + cc

    def col_slot(yy, xv):
        return yy * nx + (xv + nx) % nx

    z_up = (row_slot(z + 1, core), c, ch)
    z_down = (row_slot(z - 1, core), c, ch)
    sibling = (row_slot(z, 1 - core), c, ch)
    z_up_x = (row_slot(z + 1, 1 - core), c, ch)
    z_down_x = (row_slot(z - 1, 1 - core), c, ch)
    x_up = (r, col_slot(yl, xx + 1), ch)
    x_down = (r, col_slot(yl, xx - 1), ch)
    y_other = (r, col_slot(1 - yl, xx), ch)

    barrier = pltpu.get_barrier_semaphore()
    neighbours = (z_up, z_down, z_up_x, z_down_x, sibling, x_up, x_down, y_other)
    for dev in neighbours:
        pl.semaphore_signal(barrier, inc=1, device_id=dev, device_id_type=mesh_ids)
    pl.semaphore_wait(barrier, len(neighbours))

    def chunk(ref, slot, h):
        return ref.at[slot, pl.ds(h * cs, cs)]

    def desc(src, dst, key, dev):
        i = plan[key]
        return pltpu.make_async_remote_copy(
            src_ref=src, dst_ref=dst, send_sem=send_sems.at[i],
            recv_sem=recv_sems.at[i], device_id=dev, device_id_type=mesh_ids)

    started = []

    def send(ref, slot, h, key, dev, from_input=False):
        src = x_ref.at[pl.ds(h * cs, cs)] if from_input else chunk(ref, slot, h)
        d = desc(src, chunk(ref, slot, h), key, dev)
        d.start()
        started.append(d)

    def wait_in(ref, slot, h, key):
        if key in plan:
            desc(chunk(ref, slot, h), chunk(ref, slot, h), key, z_up).wait_recv()

    local_row = pltpu.make_async_copy(x_ref, rowg_ref.at[r], local_sems.at[0])
    local_col = pltpu.make_async_copy(x_ref, colg_ref.at[c], local_sems.at[1])
    local_row.start()
    local_col.start()

    own_r = row_slot(z, core)
    own_c = col_slot(yl, xx)
    for h in range(N_CHUNK):
        if ("rf", 1, h) in plan:
            send(rowg_ref, own_r, h, ("rf", 1, h), z_up, True)
        if ("rb", 1, h) in plan:
            send(rowg_ref, own_r, h, ("rb", 1, h), z_down, True)
        send(rowg_ref, own_r, h, ("sib", 0, h), sibling, True)
        send(colg_ref, own_c, h, ("cf1", 0, h), x_up, True)
        send(colg_ref, own_c, h, ("cb1", 0, h), x_down, True)
        send(colg_ref, own_c, h, ("y0", 0, h), y_other, True)

    last = nz // 2
    for s in range(1, last + 1):
        for h in range(N_CHUNK):
            if ("rf", s, h) in plan:
                slot = row_slot(z - s, core)
                wait_in(rowg_ref, slot, h, ("rf", s, h))
                if ("rf", s + 1, h) in plan:
                    send(rowg_ref, slot, h, ("rf", s + 1, h), z_up)
                if ("rf2", s + 1, h) in plan:
                    send(rowg_ref, slot, h, ("rf2", s + 1, h), z_up_x)
                if ("sib", (nz - s) % nz, h) in plan:
                    send(rowg_ref, slot, h, ("sib", (nz - s) % nz, h), sibling)
            if ("rb", s, h) in plan:
                slot = row_slot(z + s, core)
                wait_in(rowg_ref, slot, h, ("rb", s, h))
                if ("rb", s + 1, h) in plan:
                    send(rowg_ref, slot, h, ("rb", s + 1, h), z_down)
                if ("rb2", s + 1, h) in plan:
                    send(rowg_ref, slot, h, ("rb2", s + 1, h), z_down_x)
                if ("sib", s, h) in plan:
                    send(rowg_ref, slot, h, ("sib", s, h), sibling)
            if s == 1:
                slot = col_slot(yl, xx - 1)
                wait_in(colg_ref, slot, h, ("cf1", 0, h))
                send(colg_ref, slot, h, ("cf2", 0, h), x_up)
                send(colg_ref, slot, h, ("y1", 0, h), y_other)
                slot = col_slot(1 - yl, xx)
                wait_in(colg_ref, slot, h, ("y0", 0, h))
                send(colg_ref, slot, h, ("ob", 0, h), x_down)
            if s == 2:
                slot = col_slot(1 - yl, xx - 1)
                wait_in(colg_ref, slot, h, ("y1", 0, h))
                send(colg_ref, slot, h, ("of", 0, h), x_up)

    for h in range(N_CHUNK):
        wait_in(colg_ref, col_slot(yl, xx + 1), h, ("cb1", 0, h))
        wait_in(colg_ref, col_slot(yl, xx - 2), h, ("cf2", 0, h))
        wait_in(colg_ref, col_slot(1 - yl, xx + 1), h, ("ob", 0, h))
        wait_in(colg_ref, col_slot(1 - yl, xx - 2), h, ("of", 0, h))
    for off in range(nz):
        for h in range(N_CHUNK):
            wait_in(rowg_ref, row_slot(z + off, 1 - core), h, ("sib", off, h))
    for h in range(N_CHUNK):
        wait_in(rowg_ref, row_slot(z - last, 1 - core), h, ("rf2", last, h))
        wait_in(rowg_ref, row_slot(z + last, 1 - core), h, ("rb2", last, h))
    for d in started:
        d.wait_send()
    local_row.wait()
    local_col.wait()


def gather_both(x):
    nrow = lax.axis_size("row")
    ncol = lax.axis_size("col")
    assert ncol == 8 and nrow % 4 == 0 and nrow >= 8 and x.shape[0] % N_CHUNK == 0
    plan = _gather_plan(nrow // 2, ncol // 2)
    any_spec = pl.BlockSpec(memory_space=pl.ANY)
    return pl.pallas_call(
        functools.partial(_gather_kernel, plan),
        out_shape=(
            jax.ShapeDtypeStruct((nrow,) + x.shape, x.dtype),
            jax.ShapeDtypeStruct((ncol,) + x.shape, x.dtype),
        ),
        in_specs=[any_spec],
        out_specs=(any_spec, any_spec),
        scratch_shapes=[
            pltpu.SemaphoreType.DMA((len(plan),)),
            pltpu.SemaphoreType.DMA((len(plan),)),
            pltpu.SemaphoreType.DMA((2,)),
        ],
        compiler_params=pltpu.CompilerParams(collective_id=0, has_side_effects=True),
    )(x)


def per_device(voltages, lane_map, input_flags):
    n_chan = lax.axis_size("chan")
    all_chans = CH_DEV * n_chan
    half_q = voltages.shape[1]
    table_rows = kernel_table(NFFT, TAPS, all_chans)
    lane_chunks = voltages.shape[2] // 128
    native = (
        voltages.reshape(P_DEV, half_q, lane_chunks, 128)
        .transpose(0, 2, 1, 3)
        .reshape(P_DEV, lane_chunks * half_q, 128)
    )
    filtered = filter_bank(native, table_rows, half_q)
    filtered = filtered.reshape(P_DEV, half_q, SPECTRA, all_chans, 2)
    filtered = filtered.transpose(3, 0, 1, 4, 2).reshape(all_chans, P_DEV, half_q, 2 * SPECTRA)
    me_chan = lax.axis_index("chan")
    halves = filtered.reshape(n_chan, CH_DEV, P_DEV, half_q, 2 * SPECTRA)
    kept = jnp.where(me_chan == 0, halves[0], halves[1])
    sent = jnp.where(me_chan == 0, halves[1], halves[0])
    received = lax.ppermute(sent, "chan", [(0, 1), (1, 0)])
    first = jnp.where(me_chan == 0, kept, received)
    second = jnp.where(me_chan == 0, received, kept)
    turned_over = jnp.concatenate([first, second], axis=2)
    lane_rows = turned_over.reshape(CH_DEV, LANES, 2 * SPECTRA)
    lane_index = lane_map.reshape(LANES)
    selector = (lane_index[:, None] == jnp.arange(LANES, dtype=jnp.int32)[None, :]).astype(
        jnp.bfloat16
    )
    reordered = jnp.einsum("kl,clz->ckz", selector, lane_rows, preferred_element_type=jnp.float32)
    weights = input_flags.reshape(LANES).astype(jnp.float32)[None, :, None]
    channelised = (
        (reordered * weights).astype(jnp.bfloat16).reshape(CH_DEV, P_DEV, Q_DEV, 2 * SPECTRA)
    )
    by_row, by_col = gather_both(channelised.reshape(CH_DEV, P_DEV * Q_DEV, 2 * SPECTRA))
    n_row = by_row.shape[0]
    grid_cols = by_col.shape[0] * Q_DEV
    products = correlate(by_col, by_row)
    return products.reshape(CH_DEV, 2, P_DEV, grid_cols, Q_DEV, n_row * P_DEV)


CH_STEP = 4


def _corr_kernel(c_ref, g_ref, out_ref, cf_ref, lf_ref, rf_ref, acc_ref):
    n_i, blk_i, width = c_ref.shape[0], c_ref.shape[2], c_ref.shape[3]
    n_j, blk = g_ref.shape[0], g_ref.shape[2]
    n_q = Q_DEV
    n_pl = blk_i // n_q
    rows = n_i * blk_i
    n_p2 = n_j * blk // n_q
    lane = lax.broadcasted_iota(jnp.int32, (rows, width), 1)
    for cc in range(c_ref.shape[1]):
        for i in range(n_i):
            cf_ref[pl.ds(i * blk_i, blk_i), :] = c_ref[i, cc].astype(jnp.float32)
        for p in range(n_pl):
            for q in range(n_q):
                lf_ref[pl.ds(p * n_i * n_q + q, n_i, stride=n_q), :] = cf_ref[
                    pl.ds(p * n_q + q, n_i, stride=blk_i), :
                ]
        a32 = lf_ref[...]
        rolled = pltpu.roll(a32, width // 2, 1)
        a_rot = jnp.where(lane >= width // 2, -rolled, rolled)
        both = jnp.concatenate([a32, a_rot], axis=0).astype(out_ref.dtype)
        for j in range(n_j):
            rf_ref[pl.ds(j * blk, blk), :] = g_ref[j, cc].astype(jnp.float32)
        for q2 in range(n_q):
            b = rf_ref[pl.ds(q2, n_p2, stride=n_q), :].astype(out_ref.dtype)
            acc_ref[pl.ds(q2, 2 * rows, stride=n_q), :] = lax.dot_general(
                both, b, (((1,), (1,)), ((), ())), preferred_element_type=jnp.float32
            )
        out_ref[cc] = (acc_ref[...] * (1.0 / SPECTRA)).astype(out_ref.dtype).reshape(out_ref.shape[1:])


def correlate(by_col, by_row):
    n_i, n_c, blk_i, k = by_col.shape
    n_j, _, blk, _ = by_row.shape
    rows = n_i * blk_i
    n_p2 = n_j * blk // Q_DEV
    out_rows = rows * Q_DEV // P_DEV
    return pl.pallas_call(
        _corr_kernel,
        grid=(n_c // CH_STEP,),
        out_shape=jax.ShapeDtypeStruct((n_c, 2, P_DEV, out_rows, n_p2), jnp.bfloat16),
        in_specs=[
            pl.BlockSpec((n_i, CH_STEP, blk_i, k), lambda i: (0, i, 0, 0)),
            pl.BlockSpec((n_j, CH_STEP, blk, k), lambda i: (0, i, 0, 0)),
        ],
        out_specs=pl.BlockSpec((CH_STEP, 2, P_DEV, out_rows, n_p2), lambda i: (i, 0, 0, 0, 0)),
        scratch_shapes=[
            pltpu.VMEM((rows, k), jnp.float32),
            pltpu.VMEM((rows, k), jnp.float32),
            pltpu.VMEM((n_j * blk, k), jnp.float32),
            pltpu.VMEM((2 * rows * Q_DEV, n_p2), jnp.float32),
        ],
    )(by_col, by_row)


def solution(mesh):
    return jax.shard_map(
        per_device,
        mesh=mesh,
        in_specs=(P("row", ("col", "chan"), None), P("row", "col", None), P("row", "col")),
        out_specs=P("chan", None, "row", None, "col", None),
        check_vma=False,
    )
```

```python
import functools

import jax
import ml_dtypes
import numpy as np
import jax.numpy as jnp
from jax import lax
from jax.sharding import PartitionSpec as P
from jax.experimental import pallas as pl
from jax.experimental.pallas import tpu as pltpu

NFFT = 2048
TAPS = 4
P_DEV = 8
Q_DEV = 4
CH_DEV = 16
SPECTRA = 64
LANES = 32
FRAMES = 67


def kernel_table(nfft, taps, chans):
    length = taps * nfft
    position = np.arange(length, dtype=np.float64)
    centre = (position - length / 2 + 0.5) / nfft
    window = np.sinc(centre) * (0.5 - 0.5 * np.cos(2.0 * np.pi * (position + 0.5) / length))
    window = window * np.sqrt(2.0 / np.sum(window * window))
    window = window.reshape(taps, nfft)
    sample = np.arange(nfft, dtype=np.int64)
    bin_index = nfft // 4 + np.arange(chans, dtype=np.int64)
    phase_index = bin_index[:, None] * sample[None, :] % nfft
    phases = phase_index.astype(np.float64) * (2.0 * np.pi / nfft)
    both_parts = np.stack([np.cos(phases).T, -np.sin(phases).T], -1)
    built = window.T[:, :, None, None] * both_parts[:, None, :, :]
    return jnp.asarray(built.reshape(nfft, taps * chans * 2).astype(ml_dtypes.bfloat16))


P_STEP = 2
F_PAD = 72


def _fb_kernel(x_ref, t_ref, o_ref, xs_ref, lhs_ref, acc_ref):
    n_pp, half_q, spectra = o_ref.shape[0], o_ref.shape[1], o_ref.shape[2]
    width = o_ref.shape[3]
    frames = spectra + TAPS - 1
    per_frame = t_ref.shape[0] // 128
    stride = per_frame * half_q
    for pp in range(n_pp):
        xs_ref[pp] = x_ref[pp].astype(jnp.float32)
    for pp in range(n_pp):
        for q in range(half_q):
            base = (pp * half_q + q) * F_PAD
            lhs_ref[pl.ds(base + frames, F_PAD - frames), :] = jnp.zeros(
                (F_PAD - frames, lhs_ref.shape[1]), jnp.float32
            )
            for j in range(per_frame):
                lhs_ref[pl.ds(base, frames), pl.ds(j * 128, 128)] = xs_ref[
                    pp, pl.ds(j * half_q + q, frames, stride=stride), :
                ]
    acc_ref[...] = jnp.dot(
        lhs_ref[...].astype(jnp.bfloat16), t_ref[...], preferred_element_type=jnp.float32
    )
    for pp in range(n_pp):
        for q in range(half_q):
            base = (pp * half_q + q) * F_PAD
            tap = None
            for m in range(TAPS):
                col = (m * width) // 128
                v = acc_ref[pl.ds(base + m, spectra), pl.ds(col * 128, 128)]
                shift = (m * width) % 128
                if shift:
                    v = pltpu.roll(v, 128 - shift, 1)
                v = v[:, :width]
                tap = v if tap is None else tap + v
            o_ref[pp, q] = tap.astype(o_ref.dtype)


def filter_bank(native, table, half_q):
    n_p, rows, lanes = native.shape
    n_k = table.shape[1]
    width = n_k // TAPS
    m_rows = P_STEP * half_q * F_PAD
    return pl.pallas_call(
        _fb_kernel,
        grid=(n_p // P_STEP,),
        out_shape=jax.ShapeDtypeStruct((n_p, half_q, SPECTRA, width), jnp.bfloat16),
        in_specs=[
            pl.BlockSpec((P_STEP, rows, lanes), lambda i: (i, 0, 0)),
            pl.BlockSpec(table.shape, lambda i: (0, 0)),
        ],
        out_specs=pl.BlockSpec((P_STEP, half_q, SPECTRA, width), lambda i: (i, 0, 0, 0)),
        scratch_shapes=[
            pltpu.VMEM((P_STEP, rows, lanes), jnp.float32),
            pltpu.VMEM((m_rows, table.shape[0]), jnp.float32),
            pltpu.VMEM((m_rows, n_k), jnp.float32),
        ],
    )(native, table)


N_CHUNK = 4


def _gather_plan(nz, nx):
    keys = []
    last = nz // 2
    for s in range(1, last + 1):
        for h in range(N_CHUNK):
            if s < last or nz % 2 or h < N_CHUNK // 2:
                keys.append(("rf", s, h))
            if s < last or (nz % 2 == 0 and h >= N_CHUNK // 2) or (nz % 2 and s <= (nz - 1) // 2):
                keys.append(("rb", s, h))
    for h in range(N_CHUNK):
        keys.append(("rf2" if h < N_CHUNK // 2 else "rb2", last, h))
    for off in range(nz):
        for h in range(N_CHUNK):
            if off != last:
                keys.append(("sib", off, h))
    for h in range(N_CHUNK):
        for kind in ("cf1", "cb1", "y0", "cf2", "y1", "of", "ob"):
            keys.append((kind, 0, h))
    return {k: i for i, k in enumerate(keys)}


def _gather_kernel(plan, x_ref, rowg_ref, colg_ref, send_sems, recv_sems, local_sems):
    nrow = lax.axis_size("row")
    ncol = lax.axis_size("col")
    r = lax.axis_index("row")
    c = lax.axis_index("col")
    ch = lax.axis_index("chan")
    nz = nrow // 2
    z = r // 2
    core = r % 2
    nx = ncol // 2
    yl = c // nx
    xx = c % nx
    cs = x_ref.shape[0] // N_CHUNK
    mesh_ids = pl.DeviceIdType.MESH

    def row_slot(zz, cc):
        return ((zz + nz) % nz) * 2 + cc

    def col_slot(yy, xv):
        return yy * nx + (xv + nx) % nx

    z_up = (row_slot(z + 1, core), c, ch)
    z_down = (row_slot(z - 1, core), c, ch)
    sibling = (row_slot(z, 1 - core), c, ch)
    z_up_x = (row_slot(z + 1, 1 - core), c, ch)
    z_down_x = (row_slot(z - 1, 1 - core), c, ch)
    x_up = (r, col_slot(yl, xx + 1), ch)
    x_down = (r, col_slot(yl, xx - 1), ch)
    y_other = (r, col_slot(1 - yl, xx), ch)

    barrier = pltpu.get_barrier_semaphore()
    neighbours = (z_up, z_down, z_up_x, z_down_x, sibling, x_up, x_down, y_other)
    for dev in neighbours:
        pl.semaphore_signal(barrier, inc=1, device_id=dev, device_id_type=mesh_ids)
    pl.semaphore_wait(barrier, len(neighbours))

    def chunk(ref, slot, h):
        return ref.at[slot, pl.ds(h * cs, cs)]

    def desc(src, dst, key, dev):
        i = plan[key]
        return pltpu.make_async_remote_copy(
            src_ref=src, dst_ref=dst, send_sem=send_sems.at[i],
            recv_sem=recv_sems.at[i], device_id=dev, device_id_type=mesh_ids)

    started = []

    def send(ref, slot, h, key, dev, from_input=False):
        src = x_ref.at[pl.ds(h * cs, cs)] if from_input else chunk(ref, slot, h)
        d = desc(src, chunk(ref, slot, h), key, dev)
        d.start()
        started.append(d)

    def wait_in(ref, slot, h, key):
        if key in plan:
            desc(chunk(ref, slot, h), chunk(ref, slot, h), key, z_up).wait_recv()

    local_row = pltpu.make_async_copy(x_ref, rowg_ref.at[r], local_sems.at[0])
    local_col = pltpu.make_async_copy(x_ref, colg_ref.at[c], local_sems.at[1])
    local_row.start()
    local_col.start()

    own_r = row_slot(z, core)
    own_c = col_slot(yl, xx)
    for h in range(N_CHUNK):
        if ("rf", 1, h) in plan:
            send(rowg_ref, own_r, h, ("rf", 1, h), z_up, True)
        if ("rb", 1, h) in plan:
            send(rowg_ref, own_r, h, ("rb", 1, h), z_down, True)
        send(rowg_ref, own_r, h, ("sib", 0, h), sibling, True)
        send(colg_ref, own_c, h, ("cf1", 0, h), x_up, True)
        send(colg_ref, own_c, h, ("cb1", 0, h), x_down, True)
        send(colg_ref, own_c, h, ("y0", 0, h), y_other, True)

    last = nz // 2
    for s in range(1, last + 1):
        for h in range(N_CHUNK):
            if ("rf", s, h) in plan:
                slot = row_slot(z - s, core)
                wait_in(rowg_ref, slot, h, ("rf", s, h))
                if ("rf", s + 1, h) in plan:
                    send(rowg_ref, slot, h, ("rf", s + 1, h), z_up)
                if ("rf2", s + 1, h) in plan:
                    send(rowg_ref, slot, h, ("rf2", s + 1, h), z_up_x)
                if ("sib", (nz - s) % nz, h) in plan:
                    send(rowg_ref, slot, h, ("sib", (nz - s) % nz, h), sibling)
            if ("rb", s, h) in plan:
                slot = row_slot(z + s, core)
                wait_in(rowg_ref, slot, h, ("rb", s, h))
                if ("rb", s + 1, h) in plan:
                    send(rowg_ref, slot, h, ("rb", s + 1, h), z_down)
                if ("rb2", s + 1, h) in plan:
                    send(rowg_ref, slot, h, ("rb2", s + 1, h), z_down_x)
                if ("sib", s, h) in plan:
                    send(rowg_ref, slot, h, ("sib", s, h), sibling)
            if s == 1:
                slot = col_slot(yl, xx - 1)
                wait_in(colg_ref, slot, h, ("cf1", 0, h))
                send(colg_ref, slot, h, ("cf2", 0, h), x_up)
                send(colg_ref, slot, h, ("y1", 0, h), y_other)
                slot = col_slot(1 - yl, xx)
                wait_in(colg_ref, slot, h, ("y0", 0, h))
                send(colg_ref, slot, h, ("ob", 0, h), x_down)
            if s == 2:
                slot = col_slot(1 - yl, xx - 1)
                wait_in(colg_ref, slot, h, ("y1", 0, h))
                send(colg_ref, slot, h, ("of", 0, h), x_up)

    for h in range(N_CHUNK):
        wait_in(colg_ref, col_slot(yl, xx + 1), h, ("cb1", 0, h))
        wait_in(colg_ref, col_slot(yl, xx - 2), h, ("cf2", 0, h))
        wait_in(colg_ref, col_slot(1 - yl, xx + 1), h, ("ob", 0, h))
        wait_in(colg_ref, col_slot(1 - yl, xx - 2), h, ("of", 0, h))
    for off in range(nz):
        for h in range(N_CHUNK):
            wait_in(rowg_ref, row_slot(z + off, 1 - core), h, ("sib", off, h))
    for h in range(N_CHUNK):
        wait_in(rowg_ref, row_slot(z - last, 1 - core), h, ("rf2", last, h))
        wait_in(rowg_ref, row_slot(z + last, 1 - core), h, ("rb2", last, h))
    for d in started:
        d.wait_send()
    local_row.wait()
    local_col.wait()


def gather_both(x):
    nrow = lax.axis_size("row")
    ncol = lax.axis_size("col")
    assert ncol == 8 and nrow % 4 == 0 and nrow >= 8 and x.shape[0] % N_CHUNK == 0
    plan = _gather_plan(nrow // 2, ncol // 2)
    any_spec = pl.BlockSpec(memory_space=pl.ANY)
    return pl.pallas_call(
        functools.partial(_gather_kernel, plan),
        out_shape=(
            jax.ShapeDtypeStruct((nrow,) + x.shape, x.dtype),
            jax.ShapeDtypeStruct((ncol,) + x.shape, x.dtype),
        ),
        in_specs=[any_spec],
        out_specs=(any_spec, any_spec),
        scratch_shapes=[
            pltpu.SemaphoreType.DMA((len(plan),)),
            pltpu.SemaphoreType.DMA((len(plan),)),
            pltpu.SemaphoreType.DMA((2,)),
        ],
        compiler_params=pltpu.CompilerParams(collective_id=0, has_side_effects=True),
    )(x)


def per_device(voltages, lane_map, input_flags):
    n_chan = lax.axis_size("chan")
    all_chans = CH_DEV * n_chan
    half_q = voltages.shape[1]
    table_rows = kernel_table(NFFT, TAPS, all_chans)
    lane_chunks = voltages.shape[2] // 128
    native = (
        voltages.reshape(P_DEV, half_q, lane_chunks, 128)
        .transpose(0, 2, 1, 3)
        .reshape(P_DEV, lane_chunks * half_q, 128)
    )
    filtered = filter_bank(native, table_rows, half_q)
    filtered = filtered.reshape(P_DEV, half_q, SPECTRA, all_chans, 2)
    filtered = filtered.transpose(3, 0, 1, 4, 2).reshape(all_chans, P_DEV, half_q, 2 * SPECTRA)
    me_chan = lax.axis_index("chan")
    halves = filtered.reshape(n_chan, CH_DEV, P_DEV, half_q, 2 * SPECTRA)
    kept = jnp.where(me_chan == 0, halves[0], halves[1])
    sent = jnp.where(me_chan == 0, halves[1], halves[0])
    received = lax.ppermute(sent, "chan", [(0, 1), (1, 0)])
    first = jnp.where(me_chan == 0, kept, received)
    second = jnp.where(me_chan == 0, received, kept)
    turned_over = jnp.concatenate([first, second], axis=2)
    lane_rows = turned_over.reshape(CH_DEV, LANES, 2 * SPECTRA)
    lane_index = lane_map.reshape(LANES)
    selector = (lane_index[:, None] == jnp.arange(LANES, dtype=jnp.int32)[None, :]).astype(
        jnp.bfloat16
    )
    reordered = jnp.einsum("kl,clz->ckz", selector, lane_rows, preferred_element_type=jnp.float32)
    weights = input_flags.reshape(LANES).astype(jnp.float32)[None, :, None]
    channelised = (
        (reordered * weights).astype(jnp.bfloat16).reshape(CH_DEV, P_DEV, Q_DEV, 2 * SPECTRA)
    )
    by_row, by_col = gather_both(channelised.reshape(CH_DEV, P_DEV * Q_DEV, 2 * SPECTRA))
    n_row = by_row.shape[0]
    grid_cols = by_col.shape[0] * Q_DEV
    products = correlate(by_col, by_row)
    return products.reshape(CH_DEV, 2, P_DEV, grid_cols, Q_DEV, n_row * P_DEV)


CH_STEP = 4


def _corr_kernel(c_ref, g_ref, out_ref, cf_ref, lf_ref, rf_ref, acc_ref):
    n_i, blk_i, width = c_ref.shape[0], c_ref.shape[2], c_ref.shape[3]
    n_j, blk = g_ref.shape[0], g_ref.shape[2]
    n_q = Q_DEV
    n_pl = blk_i // n_q
    rows = n_i * blk_i
    n_p2 = n_j * blk // n_q
    lane = lax.broadcasted_iota(jnp.int32, (rows, width), 1)
    for cc in range(c_ref.shape[1]):
        for i in range(n_i):
            cf_ref[pl.ds(i * blk_i, blk_i), :] = c_ref[i, cc].astype(jnp.float32)
        for p in range(n_pl):
            for q in range(n_q):
                lf_ref[pl.ds(p * n_i * n_q + q, n_i, stride=n_q), :] = cf_ref[
                    pl.ds(p * n_q + q, n_i, stride=blk_i), :
                ]
        a32 = lf_ref[...]
        rolled = pltpu.roll(a32, width // 2, 1)
        a_rot = jnp.where(lane >= width // 2, -rolled, rolled)
        both = jnp.concatenate([a32, a_rot], axis=0).astype(out_ref.dtype)
        for j in range(n_j):
            rf_ref[pl.ds(j * blk, blk), :] = g_ref[j, cc].astype(jnp.float32)
        for q2 in range(n_q):
            b = rf_ref[pl.ds(q2, n_p2, stride=n_q), :].astype(out_ref.dtype)
            acc_ref[pl.ds(q2, 2 * rows, stride=n_q), :] = lax.dot_general(
                both, b, (((1,), (1,)), ((), ())), preferred_element_type=jnp.float32
            )
        out_ref[cc] = (acc_ref[...] * (1.0 / SPECTRA)).astype(out_ref.dtype).reshape(out_ref.shape[1:])


def correlate(by_col, by_row):
    n_i, n_c, blk_i, k = by_col.shape
    n_j, _, blk, _ = by_row.shape
    rows = n_i * blk_i
    n_p2 = n_j * blk // Q_DEV
    out_rows = rows * Q_DEV // P_DEV
    return pl.pallas_call(
        _corr_kernel,
        grid=(n_c // CH_STEP,),
        out_shape=jax.ShapeDtypeStruct((n_c, 2, P_DEV, out_rows, n_p2), jnp.bfloat16),
        in_specs=[
            pl.BlockSpec((n_i, CH_STEP, blk_i, k), lambda i: (0, i, 0, 0)),
            pl.BlockSpec((n_j, CH_STEP, blk, k), lambda i: (0, i, 0, 0)),
        ],
        out_specs=pl.BlockSpec((CH_STEP, 2, P_DEV, out_rows, n_p2), lambda i: (i, 0, 0, 0, 0)),
        scratch_shapes=[
            pltpu.VMEM((rows, k), jnp.float32),
            pltpu.VMEM((rows, k), jnp.float32),
            pltpu.VMEM((n_j * blk, k), jnp.float32),
            pltpu.VMEM((2 * rows * Q_DEV, n_p2), jnp.float32),
        ],
    )(by_col, by_row)


def solution(mesh):
    return jax.shard_map(
        per_device,
        mesh=mesh,
        in_specs=(P("row", ("col", "chan"), None), P("row", "col", None), P("row", "col")),
        out_specs=P("chan", None, "row", None, "col", None),
        check_vma=False,
    )
```

```python
import functools

import jax
import ml_dtypes
import numpy as np
import jax.numpy as jnp
from jax import lax
from jax.sharding import PartitionSpec as P
from jax.experimental import pallas as pl
from jax.experimental.pallas import tpu as pltpu

NFFT = 2048
TAPS = 4
P_DEV = 8
Q_DEV = 4
CH_DEV = 16
SPECTRA = 64
LANES = 32
FRAMES = 67


def kernel_table(nfft, taps, chans):
    length = taps * nfft
    position = np.arange(length, dtype=np.float64)
    centre = (position - length / 2 + 0.5) / nfft
    window = np.sinc(centre) * (0.5 - 0.5 * np.cos(2.0 * np.pi * (position + 0.5) / length))
    window = window * np.sqrt(2.0 / np.sum(window * window))
    window = window.reshape(taps, nfft)
    sample = np.arange(nfft, dtype=np.int64)
    bin_index = nfft // 4 + np.arange(chans, dtype=np.int64)
    phase_index = bin_index[:, None] * sample[None, :] % nfft
    phases = phase_index.astype(np.float64) * (2.0 * np.pi / nfft)
    both_parts = np.stack([np.cos(phases).T, -np.sin(phases).T], -1)
    built = window.T[:, :, None, None] * both_parts[:, None, :, :]
    return jnp.asarray(built.reshape(nfft, taps * chans * 2).astype(ml_dtypes.bfloat16))


P_STEP = 4
F_PAD = 72


def _fb_kernel(x_ref, t_ref, o_ref, xs_ref, lhs_ref, acc_ref):
    n_pp, half_q, spectra = o_ref.shape[0], o_ref.shape[1], o_ref.shape[2]
    width = o_ref.shape[3]
    frames = spectra + TAPS - 1
    per_frame = t_ref.shape[0] // 128
    stride = per_frame * half_q
    for pp in range(n_pp):
        xs_ref[pp] = x_ref[pp].astype(jnp.float32)
    for pp in range(n_pp):
        for q in range(half_q):
            base = (pp * half_q + q) * F_PAD
            lhs_ref[pl.ds(base + frames, F_PAD - frames), :] = jnp.zeros(
                (F_PAD - frames, lhs_ref.shape[1]), jnp.float32
            )
            for j in range(per_frame):
                lhs_ref[pl.ds(base, frames), pl.ds(j * 128, 128)] = xs_ref[
                    pp, pl.ds(j * half_q + q, frames, stride=stride), :
                ]
    acc_ref[...] = jnp.dot(
        lhs_ref[...].astype(jnp.bfloat16), t_ref[...], preferred_element_type=jnp.float32
    )
    for pp in range(n_pp):
        for q in range(half_q):
            base = (pp * half_q + q) * F_PAD
            tap = None
            for m in range(TAPS):
                col = (m * width) // 128
                v = acc_ref[pl.ds(base + m, spectra), pl.ds(col * 128, 128)]
                shift = (m * width) % 128
                if shift:
                    v = pltpu.roll(v, 128 - shift, 1)
                v = v[:, :width]
                tap = v if tap is None else tap + v
            o_ref[pp, q] = tap.astype(o_ref.dtype)


def filter_bank(native, table, half_q):
    n_p, rows, lanes = native.shape
    n_k = table.shape[1]
    width = n_k // TAPS
    m_rows = P_STEP * half_q * F_PAD
    return pl.pallas_call(
        _fb_kernel,
        grid=(n_p // P_STEP,),
        out_shape=jax.ShapeDtypeStruct((n_p, half_q, SPECTRA, width), jnp.bfloat16),
        in_specs=[
            pl.BlockSpec((P_STEP, rows, lanes), lambda i: (i, 0, 0)),
            pl.BlockSpec(table.shape, lambda i: (0, 0)),
        ],
        out_specs=pl.BlockSpec((P_STEP, half_q, SPECTRA, width), lambda i: (i, 0, 0, 0)),
        scratch_shapes=[
            pltpu.VMEM((P_STEP, rows, lanes), jnp.float32),
            pltpu.VMEM((m_rows, table.shape[0]), jnp.float32),
            pltpu.VMEM((m_rows, n_k), jnp.float32),
        ],
    )(native, table)


N_CHUNK = 4


def _gather_plan(nz, nx):
    keys = []
    last = nz // 2
    for s in range(1, last + 1):
        for h in range(N_CHUNK):
            if s < last or nz % 2 or h < N_CHUNK // 2:
                keys.append(("rf", s, h))
            if s < last or (nz % 2 == 0 and h >= N_CHUNK // 2) or (nz % 2 and s <= (nz - 1) // 2):
                keys.append(("rb", s, h))
    for h in range(N_CHUNK):
        keys.append(("rf2" if h < N_CHUNK // 2 else "rb2", last, h))
    for off in range(nz):
        for h in range(N_CHUNK):
            if off != last:
                keys.append(("sib", off, h))
    for h in range(N_CHUNK):
        for kind in ("cf1", "cb1", "y0", "cf2", "y1", "of", "ob"):
            keys.append((kind, 0, h))
    return {k: i for i, k in enumerate(keys)}


def _gather_kernel(plan, x_ref, rowg_ref, colg_ref, send_sems, recv_sems, local_sems):
    nrow = lax.axis_size("row")
    ncol = lax.axis_size("col")
    r = lax.axis_index("row")
    c = lax.axis_index("col")
    ch = lax.axis_index("chan")
    nz = nrow // 2
    z = r // 2
    core = r % 2
    nx = ncol // 2
    yl = c // nx
    xx = c % nx
    cs = x_ref.shape[0] // N_CHUNK
    mesh_ids = pl.DeviceIdType.MESH

    def row_slot(zz, cc):
        return ((zz + nz) % nz) * 2 + cc

    def col_slot(yy, xv):
        return yy * nx + (xv + nx) % nx

    z_up = (row_slot(z + 1, core), c, ch)
    z_down = (row_slot(z - 1, core), c, ch)
    sibling = (row_slot(z, 1 - core), c, ch)
    z_up_x = (row_slot(z + 1, 1 - core), c, ch)
    z_down_x = (row_slot(z - 1, 1 - core), c, ch)
    x_up = (r, col_slot(yl, xx + 1), ch)
    x_down = (r, col_slot(yl, xx - 1), ch)
    y_other = (r, col_slot(1 - yl, xx), ch)

    barrier = pltpu.get_barrier_semaphore()
    neighbours = (z_up, z_down, z_up_x, z_down_x, sibling, x_up, x_down, y_other)
    for dev in neighbours:
        pl.semaphore_signal(barrier, inc=1, device_id=dev, device_id_type=mesh_ids)
    pl.semaphore_wait(barrier, len(neighbours))

    def chunk(ref, slot, h):
        return ref.at[slot, pl.ds(h * cs, cs)]

    def desc(src, dst, key, dev):
        i = plan[key]
        return pltpu.make_async_remote_copy(
            src_ref=src, dst_ref=dst, send_sem=send_sems.at[i],
            recv_sem=recv_sems.at[i], device_id=dev, device_id_type=mesh_ids)

    started = []

    def send(ref, slot, h, key, dev, from_input=False):
        src = x_ref.at[pl.ds(h * cs, cs)] if from_input else chunk(ref, slot, h)
        d = desc(src, chunk(ref, slot, h), key, dev)
        d.start()
        started.append(d)

    def wait_in(ref, slot, h, key):
        if key in plan:
            desc(chunk(ref, slot, h), chunk(ref, slot, h), key, z_up).wait_recv()

    local_row = pltpu.make_async_copy(x_ref, rowg_ref.at[r], local_sems.at[0])
    local_col = pltpu.make_async_copy(x_ref, colg_ref.at[c], local_sems.at[1])
    local_row.start()
    local_col.start()

    own_r = row_slot(z, core)
    own_c = col_slot(yl, xx)
    for h in range(N_CHUNK):
        if ("rf", 1, h) in plan:
            send(rowg_ref, own_r, h, ("rf", 1, h), z_up, True)
        if ("rb", 1, h) in plan:
            send(rowg_ref, own_r, h, ("rb", 1, h), z_down, True)
        send(rowg_ref, own_r, h, ("sib", 0, h), sibling, True)
        send(colg_ref, own_c, h, ("cf1", 0, h), x_up, True)
        send(colg_ref, own_c, h, ("cb1", 0, h), x_down, True)
        send(colg_ref, own_c, h, ("y0", 0, h), y_other, True)

    last = nz // 2
    for s in range(1, last + 1):
        for h in range(N_CHUNK):
            if ("rf", s, h) in plan:
                slot = row_slot(z - s, core)
                wait_in(rowg_ref, slot, h, ("rf", s, h))
                if ("rf", s + 1, h) in plan:
                    send(rowg_ref, slot, h, ("rf", s + 1, h), z_up)
                if ("rf2", s + 1, h) in plan:
                    send(rowg_ref, slot, h, ("rf2", s + 1, h), z_up_x)
                if ("sib", (nz - s) % nz, h) in plan:
                    send(rowg_ref, slot, h, ("sib", (nz - s) % nz, h), sibling)
            if ("rb", s, h) in plan:
                slot = row_slot(z + s, core)
                wait_in(rowg_ref, slot, h, ("rb", s, h))
                if ("rb", s + 1, h) in plan:
                    send(rowg_ref, slot, h, ("rb", s + 1, h), z_down)
                if ("rb2", s + 1, h) in plan:
                    send(rowg_ref, slot, h, ("rb2", s + 1, h), z_down_x)
                if ("sib", s, h) in plan:
                    send(rowg_ref, slot, h, ("sib", s, h), sibling)
            if s == 1:
                slot = col_slot(yl, xx - 1)
                wait_in(colg_ref, slot, h, ("cf1", 0, h))
                send(colg_ref, slot, h, ("cf2", 0, h), x_up)
                send(colg_ref, slot, h, ("y1", 0, h), y_other)
                slot = col_slot(1 - yl, xx)
                wait_in(colg_ref, slot, h, ("y0", 0, h))
                send(colg_ref, slot, h, ("ob", 0, h), x_down)
            if s == 2:
                slot = col_slot(1 - yl, xx - 1)
                wait_in(colg_ref, slot, h, ("y1", 0, h))
                send(colg_ref, slot, h, ("of", 0, h), x_up)

    for h in range(N_CHUNK):
        wait_in(colg_ref, col_slot(yl, xx + 1), h, ("cb1", 0, h))
        wait_in(colg_ref, col_slot(yl, xx - 2), h, ("cf2", 0, h))
        wait_in(colg_ref, col_slot(1 - yl, xx + 1), h, ("ob", 0, h))
        wait_in(colg_ref, col_slot(1 - yl, xx - 2), h, ("of", 0, h))
    for off in range(nz):
        for h in range(N_CHUNK):
            wait_in(rowg_ref, row_slot(z + off, 1 - core), h, ("sib", off, h))
    for h in range(N_CHUNK):
        wait_in(rowg_ref, row_slot(z - last, 1 - core), h, ("rf2", last, h))
        wait_in(rowg_ref, row_slot(z + last, 1 - core), h, ("rb2", last, h))
    for d in started:
        d.wait_send()
    local_row.wait()
    local_col.wait()


def gather_both(x):
    nrow = lax.axis_size("row")
    ncol = lax.axis_size("col")
    assert ncol == 8 and nrow % 4 == 0 and nrow >= 8 and x.shape[0] % N_CHUNK == 0
    plan = _gather_plan(nrow // 2, ncol // 2)
    any_spec = pl.BlockSpec(memory_space=pl.ANY)
    return pl.pallas_call(
        functools.partial(_gather_kernel, plan),
        out_shape=(
            jax.ShapeDtypeStruct((nrow,) + x.shape, x.dtype),
            jax.ShapeDtypeStruct((ncol,) + x.shape, x.dtype),
        ),
        in_specs=[any_spec],
        out_specs=(any_spec, any_spec),
        scratch_shapes=[
            pltpu.SemaphoreType.DMA((len(plan),)),
            pltpu.SemaphoreType.DMA((len(plan),)),
            pltpu.SemaphoreType.DMA((2,)),
        ],
        compiler_params=pltpu.CompilerParams(collective_id=0, has_side_effects=True),
    )(x)


def per_device(voltages, lane_map, input_flags):
    n_chan = lax.axis_size("chan")
    all_chans = CH_DEV * n_chan
    half_q = voltages.shape[1]
    table_rows = kernel_table(NFFT, TAPS, all_chans)
    lane_chunks = voltages.shape[2] // 128
    native = (
        voltages.reshape(P_DEV, half_q, lane_chunks, 128)
        .transpose(0, 2, 1, 3)
        .reshape(P_DEV, lane_chunks * half_q, 128)
    )
    filtered = filter_bank(native, table_rows, half_q)
    filtered = filtered.reshape(P_DEV, half_q, SPECTRA, all_chans, 2)
    filtered = filtered.transpose(3, 0, 1, 4, 2).reshape(all_chans, P_DEV, half_q, 2 * SPECTRA)
    me_chan = lax.axis_index("chan")
    halves = filtered.reshape(n_chan, CH_DEV, P_DEV, half_q, 2 * SPECTRA)
    kept = jnp.where(me_chan == 0, halves[0], halves[1])
    sent = jnp.where(me_chan == 0, halves[1], halves[0])
    received = lax.ppermute(sent, "chan", [(0, 1), (1, 0)])
    first = jnp.where(me_chan == 0, kept, received)
    second = jnp.where(me_chan == 0, received, kept)
    turned_over = jnp.concatenate([first, second], axis=2)
    lane_rows = turned_over.reshape(CH_DEV, LANES, 2 * SPECTRA)
    lane_index = lane_map.reshape(LANES)
    selector = (lane_index[:, None] == jnp.arange(LANES, dtype=jnp.int32)[None, :]).astype(
        jnp.bfloat16
    )
    reordered = jnp.einsum("kl,clz->ckz", selector, lane_rows, preferred_element_type=jnp.float32)
    weights = input_flags.reshape(LANES).astype(jnp.float32)[None, :, None]
    channelised = (
        (reordered * weights).astype(jnp.bfloat16).reshape(CH_DEV, P_DEV, Q_DEV, 2 * SPECTRA)
    )
    by_row, by_col = gather_both(channelised.reshape(CH_DEV, P_DEV * Q_DEV, 2 * SPECTRA))
    n_row = by_row.shape[0]
    grid_cols = by_col.shape[0] * Q_DEV
    products = correlate(by_col, by_row)
    return products.reshape(CH_DEV, 2, P_DEV, grid_cols, Q_DEV, n_row * P_DEV)


CH_STEP = 4


def _corr_kernel(c_ref, g_ref, out_ref, cf_ref, lf_ref, rf_ref, acc_ref):
    n_i, blk_i, width = c_ref.shape[0], c_ref.shape[2], c_ref.shape[3]
    n_j, blk = g_ref.shape[0], g_ref.shape[2]
    n_q = Q_DEV
    n_pl = blk_i // n_q
    rows = n_i * blk_i
    n_p2 = n_j * blk // n_q
    lane = lax.broadcasted_iota(jnp.int32, (rows, width), 1)
    for cc in range(c_ref.shape[1]):
        for i in range(n_i):
            cf_ref[pl.ds(i * blk_i, blk_i), :] = c_ref[i, cc].astype(jnp.float32)
        for p in range(n_pl):
            for q in range(n_q):
                lf_ref[pl.ds(p * n_i * n_q + q, n_i, stride=n_q), :] = cf_ref[
                    pl.ds(p * n_q + q, n_i, stride=blk_i), :
                ]
        a32 = lf_ref[...]
        rolled = pltpu.roll(a32, width // 2, 1)
        a_rot = jnp.where(lane >= width // 2, -rolled, rolled)
        both = jnp.concatenate([a32, a_rot], axis=0).astype(out_ref.dtype)
        for j in range(n_j):
            rf_ref[pl.ds(j * blk, blk), :] = g_ref[j, cc].astype(jnp.float32)
        for q2 in range(n_q):
            b = rf_ref[pl.ds(q2, n_p2, stride=n_q), :].astype(out_ref.dtype)
            acc_ref[pl.ds(q2, 2 * rows, stride=n_q), :] = lax.dot_general(
                both, b, (((1,), (1,)), ((), ())), preferred_element_type=jnp.float32
            )
        out_ref[cc] = (acc_ref[...] * (1.0 / SPECTRA)).astype(out_ref.dtype).reshape(out_ref.shape[1:])


def correlate(by_col, by_row):
    n_i, n_c, blk_i, k = by_col.shape
    n_j, _, blk, _ = by_row.shape
    rows = n_i * blk_i
    n_p2 = n_j * blk // Q_DEV
    out_rows = rows * Q_DEV // P_DEV
    return pl.pallas_call(
        _corr_kernel,
        grid=(n_c // CH_STEP,),
        out_shape=jax.ShapeDtypeStruct((n_c, 2, P_DEV, out_rows, n_p2), jnp.bfloat16),
        in_specs=[
            pl.BlockSpec((n_i, CH_STEP, blk_i, k), lambda i: (0, i, 0, 0)),
            pl.BlockSpec((n_j, CH_STEP, blk, k), lambda i: (0, i, 0, 0)),
        ],
        out_specs=pl.BlockSpec((CH_STEP, 2, P_DEV, out_rows, n_p2), lambda i: (i, 0, 0, 0, 0)),
        scratch_shapes=[
            pltpu.VMEM((rows, k), jnp.float32),
            pltpu.VMEM((rows, k), jnp.float32),
            pltpu.VMEM((n_j * blk, k), jnp.float32),
            pltpu.VMEM((2 * rows * Q_DEV, n_p2), jnp.float32),
        ],
    )(by_col, by_row)


def solution(mesh):
    return jax.shard_map(
        per_device,
        mesh=mesh,
        in_specs=(P("row", ("col", "chan"), None), P("row", "col", None), P("row", "col")),
        out_specs=P("chan", None, "row", None, "col", None),
        check_vma=False,
    )
```

```python
import functools

import jax
import ml_dtypes
import numpy as np
import jax.numpy as jnp
from jax import lax
from jax.sharding import PartitionSpec as P
from jax.experimental import pallas as pl
from jax.experimental.pallas import tpu as pltpu

NFFT = 2048
TAPS = 4
P_DEV = 8
Q_DEV = 4
CH_DEV = 16
SPECTRA = 64
LANES = 32
FRAMES = 67


def kernel_table(nfft, taps, chans):
    length = taps * nfft
    position = np.arange(length, dtype=np.float64)
    centre = (position - length / 2 + 0.5) / nfft
    window = np.sinc(centre) * (0.5 - 0.5 * np.cos(2.0 * np.pi * (position + 0.5) / length))
    window = window * np.sqrt(2.0 / np.sum(window * window))
    window = window.reshape(taps, nfft)
    sample = np.arange(nfft, dtype=np.int64)
    bin_index = nfft // 4 + np.arange(chans, dtype=np.int64)
    phase_index = bin_index[:, None] * sample[None, :] % nfft
    phases = phase_index.astype(np.float64) * (2.0 * np.pi / nfft)
    both_parts = np.stack([np.cos(phases).T, -np.sin(phases).T], -1)
    built = window.T[:, :, None, None] * both_parts[:, None, :, :]
    return jnp.asarray(built.reshape(nfft, taps * chans * 2).astype(ml_dtypes.bfloat16))


P_STEP = 2
F_PAD = 72


def _fb_kernel(x_ref, t_ref, o_ref, xs_ref, lhs_ref, acc_ref):
    n_pp, half_q, spectra = o_ref.shape[0], o_ref.shape[1], o_ref.shape[2]
    width = o_ref.shape[3]
    frames = spectra + TAPS - 1
    per_frame = t_ref.shape[0] // 128
    stride = per_frame * half_q
    for pp in range(n_pp):
        xs_ref[pp] = x_ref[pp].astype(jnp.float32)
    for pp in range(n_pp):
        for q in range(half_q):
            base = (pp * half_q + q) * F_PAD
            lhs_ref[pl.ds(base + frames, F_PAD - frames), :] = jnp.zeros(
                (F_PAD - frames, lhs_ref.shape[1]), jnp.float32
            )
            for j in range(per_frame):
                lhs_ref[pl.ds(base, frames), pl.ds(j * 128, 128)] = xs_ref[
                    pp, pl.ds(j * half_q + q, frames, stride=stride), :
                ]
    acc_ref[...] = jnp.dot(
        lhs_ref[...].astype(jnp.bfloat16), t_ref[...], preferred_element_type=jnp.float32
    )
    for pp in range(n_pp):
        for q in range(half_q):
            base = (pp * half_q + q) * F_PAD
            tap = None
            for m in range(TAPS):
                col = (m * width) // 128
                v = acc_ref[pl.ds(base + m, spectra), pl.ds(col * 128, 128)]
                shift = (m * width) % 128
                if shift:
                    v = pltpu.roll(v, 128 - shift, 1)
                v = v[:, :width]
                tap = v if tap is None else tap + v
            o_ref[pp, q] = tap.astype(o_ref.dtype)


def filter_bank(native, table, half_q):
    n_p, rows, lanes = native.shape
    n_k = table.shape[1]
    width = n_k // TAPS
    m_rows = P_STEP * half_q * F_PAD
    return pl.pallas_call(
        _fb_kernel,
        grid=(n_p // P_STEP,),
        out_shape=jax.ShapeDtypeStruct((n_p, half_q, SPECTRA, width), jnp.bfloat16),
        in_specs=[
            pl.BlockSpec((P_STEP, rows, lanes), lambda i: (i, 0, 0)),
            pl.BlockSpec(table.shape, lambda i: (0, 0)),
        ],
        out_specs=pl.BlockSpec((P_STEP, half_q, SPECTRA, width), lambda i: (i, 0, 0, 0)),
        scratch_shapes=[
            pltpu.VMEM((P_STEP, rows, lanes), jnp.float32),
            pltpu.VMEM((m_rows, table.shape[0]), jnp.float32),
            pltpu.VMEM((m_rows, n_k), jnp.float32),
        ],
    )(native, table)


N_CHUNK = 8


def _gather_plan(nz, nx):
    keys = []
    last = nz // 2
    for s in range(1, last + 1):
        for h in range(N_CHUNK):
            if s < last or nz % 2 or h < N_CHUNK // 2:
                keys.append(("rf", s, h))
            if s < last or (nz % 2 == 0 and h >= N_CHUNK // 2) or (nz % 2 and s <= (nz - 1) // 2):
                keys.append(("rb", s, h))
    for h in range(N_CHUNK):
        keys.append(("rf2" if h < N_CHUNK // 2 else "rb2", last, h))
    for off in range(nz):
        for h in range(N_CHUNK):
            if off != last:
                keys.append(("sib", off, h))
    for h in range(N_CHUNK):
        for kind in ("cf1", "cb1", "y0", "cf2", "y1", "of", "ob"):
            keys.append((kind, 0, h))
    return {k: i for i, k in enumerate(keys)}


def _gather_kernel(plan, x_ref, rowg_ref, colg_ref, send_sems, recv_sems, local_sems):
    nrow = lax.axis_size("row")
    ncol = lax.axis_size("col")
    r = lax.axis_index("row")
    c = lax.axis_index("col")
    ch = lax.axis_index("chan")
    nz = nrow // 2
    z = r // 2
    core = r % 2
    nx = ncol // 2
    yl = c // nx
    xx = c % nx
    cs = x_ref.shape[0] // N_CHUNK
    mesh_ids = pl.DeviceIdType.MESH

    def row_slot(zz, cc):
        return ((zz + nz) % nz) * 2 + cc

    def col_slot(yy, xv):
        return yy * nx + (xv + nx) % nx

    z_up = (row_slot(z + 1, core), c, ch)
    z_down = (row_slot(z - 1, core), c, ch)
    sibling = (row_slot(z, 1 - core), c, ch)
    z_up_x = (row_slot(z + 1, 1 - core), c, ch)
    z_down_x = (row_slot(z - 1, 1 - core), c, ch)
    x_up = (r, col_slot(yl, xx + 1), ch)
    x_down = (r, col_slot(yl, xx - 1), ch)
    y_other = (r, col_slot(1 - yl, xx), ch)

    barrier = pltpu.get_barrier_semaphore()
    neighbours = (z_up, z_down, z_up_x, z_down_x, sibling, x_up, x_down, y_other)
    for dev in neighbours:
        pl.semaphore_signal(barrier, inc=1, device_id=dev, device_id_type=mesh_ids)
    pl.semaphore_wait(barrier, len(neighbours))

    def chunk(ref, slot, h):
        return ref.at[slot, pl.ds(h * cs, cs)]

    def desc(src, dst, key, dev):
        i = plan[key]
        return pltpu.make_async_remote_copy(
            src_ref=src, dst_ref=dst, send_sem=send_sems.at[i],
            recv_sem=recv_sems.at[i], device_id=dev, device_id_type=mesh_ids)

    started = []

    def send(ref, slot, h, key, dev, from_input=False):
        src = x_ref.at[pl.ds(h * cs, cs)] if from_input else chunk(ref, slot, h)
        d = desc(src, chunk(ref, slot, h), key, dev)
        d.start()
        started.append(d)

    def wait_in(ref, slot, h, key):
        if key in plan:
            desc(chunk(ref, slot, h), chunk(ref, slot, h), key, z_up).wait_recv()

    local_row = pltpu.make_async_copy(x_ref, rowg_ref.at[r], local_sems.at[0])
    local_col = pltpu.make_async_copy(x_ref, colg_ref.at[c], local_sems.at[1])
    local_row.start()
    local_col.start()

    own_r = row_slot(z, core)
    own_c = col_slot(yl, xx)
    for h in range(N_CHUNK):
        if ("rf", 1, h) in plan:
            send(rowg_ref, own_r, h, ("rf", 1, h), z_up, True)
        if ("rb", 1, h) in plan:
            send(rowg_ref, own_r, h, ("rb", 1, h), z_down, True)
        send(rowg_ref, own_r, h, ("sib", 0, h), sibling, True)
        send(colg_ref, own_c, h, ("cf1", 0, h), x_up, True)
        send(colg_ref, own_c, h, ("cb1", 0, h), x_down, True)
        send(colg_ref, own_c, h, ("y0", 0, h), y_other, True)

    last = nz // 2
    for s in range(1, last + 1):
        for h in range(N_CHUNK):
            if ("rf", s, h) in plan:
                slot = row_slot(z - s, core)
                wait_in(rowg_ref, slot, h, ("rf", s, h))
                if ("rf", s + 1, h) in plan:
                    send(rowg_ref, slot, h, ("rf", s + 1, h), z_up)
                if ("rf2", s + 1, h) in plan:
                    send(rowg_ref, slot, h, ("rf2", s + 1, h), z_up_x)
                if ("sib", (nz - s) % nz, h) in plan:
                    send(rowg_ref, slot, h, ("sib", (nz - s) % nz, h), sibling)
            if ("rb", s, h) in plan:
                slot = row_slot(z + s, core)
                wait_in(rowg_ref, slot, h, ("rb", s, h))
                if ("rb", s + 1, h) in plan:
                    send(rowg_ref, slot, h, ("rb", s + 1, h), z_down)
                if ("rb2", s + 1, h) in plan:
                    send(rowg_ref, slot, h, ("rb2", s + 1, h), z_down_x)
                if ("sib", s, h) in plan:
                    send(rowg_ref, slot, h, ("sib", s, h), sibling)
            if s == 1:
                slot = col_slot(yl, xx - 1)
                wait_in(colg_ref, slot, h, ("cf1", 0, h))
                send(colg_ref, slot, h, ("cf2", 0, h), x_up)
                send(colg_ref, slot, h, ("y1", 0, h), y_other)
                slot = col_slot(1 - yl, xx)
                wait_in(colg_ref, slot, h, ("y0", 0, h))
                send(colg_ref, slot, h, ("ob", 0, h), x_down)
            if s == 2:
                slot = col_slot(1 - yl, xx - 1)
                wait_in(colg_ref, slot, h, ("y1", 0, h))
                send(colg_ref, slot, h, ("of", 0, h), x_up)

    for h in range(N_CHUNK):
        wait_in(colg_ref, col_slot(yl, xx + 1), h, ("cb1", 0, h))
        wait_in(colg_ref, col_slot(yl, xx - 2), h, ("cf2", 0, h))
        wait_in(colg_ref, col_slot(1 - yl, xx + 1), h, ("ob", 0, h))
        wait_in(colg_ref, col_slot(1 - yl, xx - 2), h, ("of", 0, h))
    for off in range(nz):
        for h in range(N_CHUNK):
            wait_in(rowg_ref, row_slot(z + off, 1 - core), h, ("sib", off, h))
    for h in range(N_CHUNK):
        wait_in(rowg_ref, row_slot(z - last, 1 - core), h, ("rf2", last, h))
        wait_in(rowg_ref, row_slot(z + last, 1 - core), h, ("rb2", last, h))
    for d in started:
        d.wait_send()
    local_row.wait()
    local_col.wait()


def gather_both(x):
    nrow = lax.axis_size("row")
    ncol = lax.axis_size("col")
    assert ncol == 8 and nrow % 4 == 0 and nrow >= 8 and x.shape[0] % N_CHUNK == 0
    plan = _gather_plan(nrow // 2, ncol // 2)
    any_spec = pl.BlockSpec(memory_space=pl.ANY)
    return pl.pallas_call(
        functools.partial(_gather_kernel, plan),
        out_shape=(
            jax.ShapeDtypeStruct((nrow,) + x.shape, x.dtype),
            jax.ShapeDtypeStruct((ncol,) + x.shape, x.dtype),
        ),
        in_specs=[any_spec],
        out_specs=(any_spec, any_spec),
        scratch_shapes=[
            pltpu.SemaphoreType.DMA((len(plan),)),
            pltpu.SemaphoreType.DMA((len(plan),)),
            pltpu.SemaphoreType.DMA((2,)),
        ],
        compiler_params=pltpu.CompilerParams(collective_id=0, has_side_effects=True),
    )(x)


def per_device(voltages, lane_map, input_flags):
    n_chan = lax.axis_size("chan")
    all_chans = CH_DEV * n_chan
    half_q = voltages.shape[1]
    table_rows = kernel_table(NFFT, TAPS, all_chans)
    lane_chunks = voltages.shape[2] // 128
    native = (
        voltages.reshape(P_DEV, half_q, lane_chunks, 128)
        .transpose(0, 2, 1, 3)
        .reshape(P_DEV, lane_chunks * half_q, 128)
    )
    filtered = filter_bank(native, table_rows, half_q)
    filtered = filtered.reshape(P_DEV, half_q, SPECTRA, all_chans, 2)
    filtered = filtered.transpose(3, 0, 1, 4, 2).reshape(all_chans, P_DEV, half_q, 2 * SPECTRA)
    me_chan = lax.axis_index("chan")
    halves = filtered.reshape(n_chan, CH_DEV, P_DEV, half_q, 2 * SPECTRA)
    kept = jnp.where(me_chan == 0, halves[0], halves[1])
    sent = jnp.where(me_chan == 0, halves[1], halves[0])
    received = lax.ppermute(sent, "chan", [(0, 1), (1, 0)])
    first = jnp.where(me_chan == 0, kept, received)
    second = jnp.where(me_chan == 0, received, kept)
    turned_over = jnp.concatenate([first, second], axis=2)
    lane_rows = turned_over.reshape(CH_DEV, LANES, 2 * SPECTRA)
    lane_index = lane_map.reshape(LANES)
    selector = (lane_index[:, None] == jnp.arange(LANES, dtype=jnp.int32)[None, :]).astype(
        jnp.bfloat16
    )
    reordered = jnp.einsum("kl,clz->ckz", selector, lane_rows, preferred_element_type=jnp.float32)
    weights = input_flags.reshape(LANES).astype(jnp.float32)[None, :, None]
    channelised = (
        (reordered * weights).astype(jnp.bfloat16).reshape(CH_DEV, P_DEV, Q_DEV, 2 * SPECTRA)
    )
    by_row, by_col = gather_both(channelised.reshape(CH_DEV, P_DEV * Q_DEV, 2 * SPECTRA))
    n_row = by_row.shape[0]
    grid_cols = by_col.shape[0] * Q_DEV
    products = correlate(by_col, by_row)
    return products.reshape(CH_DEV, 2, P_DEV, grid_cols, Q_DEV, n_row * P_DEV)


CH_STEP = 4


def _corr_kernel(c_ref, g_ref, out_ref, cf_ref, lf_ref, rf_ref, acc_ref):
    n_i, blk_i, width = c_ref.shape[0], c_ref.shape[2], c_ref.shape[3]
    n_j, blk = g_ref.shape[0], g_ref.shape[2]
    n_q = Q_DEV
    n_pl = blk_i // n_q
    rows = n_i * blk_i
    n_p2 = n_j * blk // n_q
    lane = lax.broadcasted_iota(jnp.int32, (rows, width), 1)
    for cc in range(c_ref.shape[1]):
        for i in range(n_i):
            cf_ref[pl.ds(i * blk_i, blk_i), :] = c_ref[i, cc].astype(jnp.float32)
        for p in range(n_pl):
            for q in range(n_q):
                lf_ref[pl.ds(p * n_i * n_q + q, n_i, stride=n_q), :] = cf_ref[
                    pl.ds(p * n_q + q, n_i, stride=blk_i), :
                ]
        a32 = lf_ref[...]
        rolled = pltpu.roll(a32, width // 2, 1)
        a_rot = jnp.where(lane >= width // 2, -rolled, rolled)
        both = jnp.concatenate([a32, a_rot], axis=0).astype(out_ref.dtype)
        for j in range(n_j):
            rf_ref[pl.ds(j * blk, blk), :] = g_ref[j, cc].astype(jnp.float32)
        for q2 in range(n_q):
            b = rf_ref[pl.ds(q2, n_p2, stride=n_q), :].astype(out_ref.dtype)
            acc_ref[pl.ds(q2, 2 * rows, stride=n_q), :] = lax.dot_general(
                both, b, (((1,), (1,)), ((), ())), preferred_element_type=jnp.float32
            )
        out_ref[cc] = (acc_ref[...] * (1.0 / SPECTRA)).astype(out_ref.dtype).reshape(out_ref.shape[1:])


def correlate(by_col, by_row):
    n_i, n_c, blk_i, k = by_col.shape
    n_j, _, blk, _ = by_row.shape
    rows = n_i * blk_i
    n_p2 = n_j * blk // Q_DEV
    out_rows = rows * Q_DEV // P_DEV
    return pl.pallas_call(
        _corr_kernel,
        grid=(n_c // CH_STEP,),
        out_shape=jax.ShapeDtypeStruct((n_c, 2, P_DEV, out_rows, n_p2), jnp.bfloat16),
        in_specs=[
            pl.BlockSpec((n_i, CH_STEP, blk_i, k), lambda i: (0, i, 0, 0)),
            pl.BlockSpec((n_j, CH_STEP, blk, k), lambda i: (0, i, 0, 0)),
        ],
        out_specs=pl.BlockSpec((CH_STEP, 2, P_DEV, out_rows, n_p2), lambda i: (i, 0, 0, 0, 0)),
        scratch_shapes=[
            pltpu.VMEM((rows, k), jnp.float32),
            pltpu.VMEM((rows, k), jnp.float32),
            pltpu.VMEM((n_j * blk, k), jnp.float32),
            pltpu.VMEM((2 * rows * Q_DEV, n_p2), jnp.float32),
        ],
    )(by_col, by_row)


def solution(mesh):
    return jax.shard_map(
        per_device,
        mesh=mesh,
        in_specs=(P("row", ("col", "chan"), None), P("row", "col", None), P("row", "col")),
        out_specs=P("chan", None, "row", None, "col", None),
        check_vma=False,
    )
```

```python
import functools

import jax
import ml_dtypes
import numpy as np
import jax.numpy as jnp
from jax import lax
from jax.sharding import PartitionSpec as P
from jax.experimental import pallas as pl
from jax.experimental.pallas import tpu as pltpu

NFFT = 2048
TAPS = 4
P_DEV = 8
Q_DEV = 4
CH_DEV = 16
SPECTRA = 64
LANES = 32
FRAMES = 67


def kernel_table(nfft, taps, chans):
    length = taps * nfft
    position = np.arange(length, dtype=np.float64)
    centre = (position - length / 2 + 0.5) / nfft
    window = np.sinc(centre) * (0.5 - 0.5 * np.cos(2.0 * np.pi * (position + 0.5) / length))
    window = window * np.sqrt(2.0 / np.sum(window * window))
    window = window.reshape(taps, nfft)
    sample = np.arange(nfft, dtype=np.int64)
    bin_index = nfft // 4 + np.arange(chans, dtype=np.int64)
    phase_index = bin_index[:, None] * sample[None, :] % nfft
    phases = phase_index.astype(np.float64) * (2.0 * np.pi / nfft)
    both_parts = np.stack([np.cos(phases).T, -np.sin(phases).T], -1)
    built = window.T[:, :, None, None] * both_parts[:, None, :, :]
    return jnp.asarray(built.reshape(nfft, taps * chans * 2).astype(ml_dtypes.bfloat16))


P_STEP = 2
F_PAD = 72


def _fb_kernel(x_ref, t_ref, o_ref, xs_ref, lhs_ref, acc_ref):
    n_pp, half_q, spectra = o_ref.shape[0], o_ref.shape[1], o_ref.shape[2]
    width = o_ref.shape[3]
    frames = spectra + TAPS - 1
    per_frame = t_ref.shape[0] // 128
    stride = per_frame * half_q
    for pp in range(n_pp):
        xs_ref[pp] = x_ref[pp].astype(jnp.float32)
    for pp in range(n_pp):
        for q in range(half_q):
            base = (pp * half_q + q) * F_PAD
            lhs_ref[pl.ds(base + frames, F_PAD - frames), :] = jnp.zeros(
                (F_PAD - frames, lhs_ref.shape[1]), jnp.float32
            )
            for j in range(per_frame):
                lhs_ref[pl.ds(base, frames), pl.ds(j * 128, 128)] = xs_ref[
                    pp, pl.ds(j * half_q + q, frames, stride=stride), :
                ]
    acc_ref[...] = jnp.dot(
        lhs_ref[...].astype(jnp.bfloat16), t_ref[...], preferred_element_type=jnp.float32
    )
    for pp in range(n_pp):
        for q in range(half_q):
            base = (pp * half_q + q) * F_PAD
            tap = None
            for m in range(TAPS):
                col = (m * width) // 128
                v = acc_ref[pl.ds(base + m, spectra), pl.ds(col * 128, 128)]
                shift = (m * width) % 128
                if shift:
                    v = pltpu.roll(v, 128 - shift, 1)
                v = v[:, :width]
                tap = v if tap is None else tap + v
            o_ref[pp, q] = tap.astype(o_ref.dtype)


def filter_bank(native, table, half_q):
    n_p, rows, lanes = native.shape
    n_k = table.shape[1]
    width = n_k // TAPS
    m_rows = P_STEP * half_q * F_PAD
    return pl.pallas_call(
        _fb_kernel,
        grid=(n_p // P_STEP,),
        out_shape=jax.ShapeDtypeStruct((n_p, half_q, SPECTRA, width), jnp.bfloat16),
        in_specs=[
            pl.BlockSpec((P_STEP, rows, lanes), lambda i: (i, 0, 0)),
            pl.BlockSpec(table.shape, lambda i: (0, 0)),
        ],
        out_specs=pl.BlockSpec((P_STEP, half_q, SPECTRA, width), lambda i: (i, 0, 0, 0)),
        scratch_shapes=[
            pltpu.VMEM((P_STEP, rows, lanes), jnp.float32),
            pltpu.VMEM((m_rows, table.shape[0]), jnp.float32),
            pltpu.VMEM((m_rows, n_k), jnp.float32),
        ],
    )(native, table)


N_CHUNK = 4


def _gather_plan(nz, nx):
    keys = []
    last = nz // 2
    for s in range(1, last + 1):
        for h in range(N_CHUNK):
            if s < last or nz % 2 or h < N_CHUNK // 2:
                keys.append(("rf", s, h))
            if s < last or (nz % 2 == 0 and h >= N_CHUNK // 2) or (nz % 2 and s <= (nz - 1) // 2):
                keys.append(("rb", s, h))
    for h in range(N_CHUNK):
        keys.append(("rf2" if h < N_CHUNK // 2 else "rb2", last, h))
    for off in range(nz):
        for h in range(N_CHUNK):
            if off != last:
                keys.append(("sib", off, h))
    for h in range(N_CHUNK):
        for kind in ("cf1", "cb1", "y0", "cf2", "y1", "of", "ob"):
            keys.append((kind, 0, h))
    return {k: i for i, k in enumerate(keys)}


def _gather_kernel(plan, x_ref, rowg_ref, colg_ref, send_sems, recv_sems, local_sems):
    nrow = lax.axis_size("row")
    ncol = lax.axis_size("col")
    r = lax.axis_index("row")
    c = lax.axis_index("col")
    ch = lax.axis_index("chan")
    nz = nrow // 2
    z = r // 2
    core = r % 2
    nx = ncol // 2
    yl = c // nx
    xx = c % nx
    cs = x_ref.shape[0] // N_CHUNK
    mesh_ids = pl.DeviceIdType.MESH

    def row_slot(zz, cc):
        return ((zz + nz) % nz) * 2 + cc

    def col_slot(yy, xv):
        return yy * nx + (xv + nx) % nx

    z_up = (row_slot(z + 1, core), c, ch)
    z_down = (row_slot(z - 1, core), c, ch)
    sibling = (row_slot(z, 1 - core), c, ch)
    z_up_x = (row_slot(z + 1, 1 - core), c, ch)
    z_down_x = (row_slot(z - 1, 1 - core), c, ch)
    x_up = (r, col_slot(yl, xx + 1), ch)
    x_down = (r, col_slot(yl, xx - 1), ch)
    y_other = (r, col_slot(1 - yl, xx), ch)

    barrier = pltpu.get_barrier_semaphore()
    neighbours = (z_up, z_down, z_up_x, z_down_x, sibling, x_up, x_down, y_other)
    for dev in neighbours:
        pl.semaphore_signal(barrier, inc=1, device_id=dev, device_id_type=mesh_ids)
    pl.semaphore_wait(barrier, len(neighbours))

    def chunk(ref, slot, h):
        return ref.at[slot, pl.ds(h * cs, cs)]

    def desc(src, dst, key, dev):
        i = plan[key]
        return pltpu.make_async_remote_copy(
            src_ref=src, dst_ref=dst, send_sem=send_sems.at[i],
            recv_sem=recv_sems.at[i], device_id=dev, device_id_type=mesh_ids)

    started = []

    def send(ref, slot, h, key, dev, from_input=False):
        src = x_ref.at[pl.ds(h * cs, cs)] if from_input else chunk(ref, slot, h)
        d = desc(src, chunk(ref, slot, h), key, dev)
        d.start()
        started.append(d)

    def wait_in(ref, slot, h, key):
        if key in plan:
            desc(chunk(ref, slot, h), chunk(ref, slot, h), key, z_up).wait_recv()

    local_row = pltpu.make_async_copy(x_ref, rowg_ref.at[r], local_sems.at[0])
    local_col = pltpu.make_async_copy(x_ref, colg_ref.at[c], local_sems.at[1])
    local_row.start()
    local_col.start()

    own_r = row_slot(z, core)
    own_c = col_slot(yl, xx)
    for h in range(N_CHUNK):
        if ("rf", 1, h) in plan:
            send(rowg_ref, own_r, h, ("rf", 1, h), z_up, True)
        if ("rb", 1, h) in plan:
            send(rowg_ref, own_r, h, ("rb", 1, h), z_down, True)
        send(rowg_ref, own_r, h, ("sib", 0, h), sibling, True)
        send(colg_ref, own_c, h, ("cf1", 0, h), x_up, True)
        send(colg_ref, own_c, h, ("cb1", 0, h), x_down, True)
        send(colg_ref, own_c, h, ("y0", 0, h), y_other, True)

    last = nz // 2
    for s in range(1, last + 1):
        for h in range(N_CHUNK):
            if ("rf", s, h) in plan:
                slot = row_slot(z - s, core)
                wait_in(rowg_ref, slot, h, ("rf", s, h))
                if ("rf", s + 1, h) in plan:
                    send(rowg_ref, slot, h, ("rf", s + 1, h), z_up)
                if ("rf2", s + 1, h) in plan:
                    send(rowg_ref, slot, h, ("rf2", s + 1, h), z_up_x)
                if ("sib", (nz - s) % nz, h) in plan:
                    send(rowg_ref, slot, h, ("sib", (nz - s) % nz, h), sibling)
            if ("rb", s, h) in plan:
                slot = row_slot(z + s, core)
                wait_in(rowg_ref, slot, h, ("rb", s, h))
                if ("rb", s + 1, h) in plan:
                    send(rowg_ref, slot, h, ("rb", s + 1, h), z_down)
                if ("rb2", s + 1, h) in plan:
                    send(rowg_ref, slot, h, ("rb2", s + 1, h), z_down_x)
                if ("sib", s, h) in plan:
                    send(rowg_ref, slot, h, ("sib", s, h), sibling)
            if s == 1:
                slot = col_slot(yl, xx - 1)
                wait_in(colg_ref, slot, h, ("cf1", 0, h))
                send(colg_ref, slot, h, ("cf2", 0, h), x_up)
                send(colg_ref, slot, h, ("y1", 0, h), y_other)
                slot = col_slot(1 - yl, xx)
                wait_in(colg_ref, slot, h, ("y0", 0, h))
                send(colg_ref, slot, h, ("ob", 0, h), x_down)
            if s == 2:
                slot = col_slot(1 - yl, xx - 1)
                wait_in(colg_ref, slot, h, ("y1", 0, h))
                send(colg_ref, slot, h, ("of", 0, h), x_up)

    for h in range(N_CHUNK):
        wait_in(colg_ref, col_slot(yl, xx + 1), h, ("cb1", 0, h))
        wait_in(colg_ref, col_slot(yl, xx - 2), h, ("cf2", 0, h))
        wait_in(colg_ref, col_slot(1 - yl, xx + 1), h, ("ob", 0, h))
        wait_in(colg_ref, col_slot(1 - yl, xx - 2), h, ("of", 0, h))
    for off in range(nz):
        for h in range(N_CHUNK):
            wait_in(rowg_ref, row_slot(z + off, 1 - core), h, ("sib", off, h))
    for h in range(N_CHUNK):
        wait_in(rowg_ref, row_slot(z - last, 1 - core), h, ("rf2", last, h))
        wait_in(rowg_ref, row_slot(z + last, 1 - core), h, ("rb2", last, h))
    for d in started:
        d.wait_send()
    local_row.wait()
    local_col.wait()


def gather_both(x):
    nrow = lax.axis_size("row")
    ncol = lax.axis_size("col")
    assert ncol == 8 and nrow % 4 == 0 and nrow >= 8 and x.shape[0] % N_CHUNK == 0
    plan = _gather_plan(nrow // 2, ncol // 2)
    any_spec = pl.BlockSpec(memory_space=pl.ANY)
    return pl.pallas_call(
        functools.partial(_gather_kernel, plan),
        out_shape=(
            jax.ShapeDtypeStruct((nrow,) + x.shape, x.dtype),
            jax.ShapeDtypeStruct((ncol,) + x.shape, x.dtype),
        ),
        in_specs=[any_spec],
        out_specs=(any_spec, any_spec),
        scratch_shapes=[
            pltpu.SemaphoreType.DMA((len(plan),)),
            pltpu.SemaphoreType.DMA((len(plan),)),
            pltpu.SemaphoreType.DMA((2,)),
        ],
        compiler_params=pltpu.CompilerParams(collective_id=0, has_side_effects=True),
    )(x)


def per_device(voltages, lane_map, input_flags):
    n_chan = lax.axis_size("chan")
    all_chans = CH_DEV * n_chan
    half_q = voltages.shape[1]
    table_rows = kernel_table(NFFT, TAPS, all_chans)
    lane_chunks = voltages.shape[2] // 128
    native = (
        voltages.reshape(P_DEV, half_q, lane_chunks, 128)
        .transpose(0, 2, 1, 3)
        .reshape(P_DEV, lane_chunks * half_q, 128)
    )
    filtered = filter_bank(native, table_rows, half_q)
    filtered = filtered.reshape(P_DEV, half_q, SPECTRA, all_chans, 2)
    filtered = filtered.transpose(3, 0, 1, 4, 2).reshape(all_chans, P_DEV, half_q, 2 * SPECTRA)
    me_chan = lax.axis_index("chan")
    halves = filtered.reshape(n_chan, CH_DEV, P_DEV, half_q, 2 * SPECTRA)
    kept = jnp.where(me_chan == 0, halves[0], halves[1])
    sent = jnp.where(me_chan == 0, halves[1], halves[0])
    received = lax.ppermute(sent, "chan", [(0, 1), (1, 0)])
    first = jnp.where(me_chan == 0, kept, received)
    second = jnp.where(me_chan == 0, received, kept)
    turned_over = jnp.concatenate([first, second], axis=2)
    lane_rows = turned_over.reshape(CH_DEV, LANES, 2 * SPECTRA)
    lane_index = lane_map.reshape(LANES)
    selector = (lane_index[:, None] == jnp.arange(LANES, dtype=jnp.int32)[None, :]).astype(
        jnp.bfloat16
    )
    reordered = jnp.einsum("kl,clz->ckz", selector, lane_rows, preferred_element_type=jnp.float32)
    weights = input_flags.reshape(LANES).astype(jnp.float32)[None, :, None]
    channelised = (
        (reordered * weights).astype(jnp.bfloat16).reshape(CH_DEV, P_DEV, Q_DEV, 2 * SPECTRA)
    )
    by_row, by_col = gather_both(channelised.reshape(CH_DEV, P_DEV * Q_DEV, 2 * SPECTRA))
    n_row = by_row.shape[0]
    grid_cols = by_col.shape[0] * Q_DEV
    products = correlate(by_col, by_row)
    return products.reshape(CH_DEV, 2, P_DEV, grid_cols, Q_DEV, n_row * P_DEV)


CH_STEP = 8


def _corr_kernel(c_ref, g_ref, out_ref, cf_ref, lf_ref, rf_ref, acc_ref):
    n_i, blk_i, width = c_ref.shape[0], c_ref.shape[2], c_ref.shape[3]
    n_j, blk = g_ref.shape[0], g_ref.shape[2]
    n_q = Q_DEV
    n_pl = blk_i // n_q
    rows = n_i * blk_i
    n_p2 = n_j * blk // n_q
    lane = lax.broadcasted_iota(jnp.int32, (rows, width), 1)
    for cc in range(c_ref.shape[1]):
        for i in range(n_i):
            cf_ref[pl.ds(i * blk_i, blk_i), :] = c_ref[i, cc].astype(jnp.float32)
        for p in range(n_pl):
            for q in range(n_q):
                lf_ref[pl.ds(p * n_i * n_q + q, n_i, stride=n_q), :] = cf_ref[
                    pl.ds(p * n_q + q, n_i, stride=blk_i), :
                ]
        a32 = lf_ref[...]
        rolled = pltpu.roll(a32, width // 2, 1)
        a_rot = jnp.where(lane >= width // 2, -rolled, rolled)
        both = jnp.concatenate([a32, a_rot], axis=0).astype(out_ref.dtype)
        for j in range(n_j):
            rf_ref[pl.ds(j * blk, blk), :] = g_ref[j, cc].astype(jnp.float32)
        for q2 in range(n_q):
            b = rf_ref[pl.ds(q2, n_p2, stride=n_q), :].astype(out_ref.dtype)
            acc_ref[pl.ds(q2, 2 * rows, stride=n_q), :] = lax.dot_general(
                both, b, (((1,), (1,)), ((), ())), preferred_element_type=jnp.float32
            )
        out_ref[cc] = (acc_ref[...] * (1.0 / SPECTRA)).astype(out_ref.dtype).reshape(out_ref.shape[1:])


def correlate(by_col, by_row):
    n_i, n_c, blk_i, k = by_col.shape
    n_j, _, blk, _ = by_row.shape
    rows = n_i * blk_i
    n_p2 = n_j * blk // Q_DEV
    out_rows = rows * Q_DEV // P_DEV
    return pl.pallas_call(
        _corr_kernel,
        grid=(n_c // CH_STEP,),
        out_shape=jax.ShapeDtypeStruct((n_c, 2, P_DEV, out_rows, n_p2), jnp.bfloat16),
        in_specs=[
            pl.BlockSpec((n_i, CH_STEP, blk_i, k), lambda i: (0, i, 0, 0)),
            pl.BlockSpec((n_j, CH_STEP, blk, k), lambda i: (0, i, 0, 0)),
        ],
        out_specs=pl.BlockSpec((CH_STEP, 2, P_DEV, out_rows, n_p2), lambda i: (i, 0, 0, 0, 0)),
        scratch_shapes=[
            pltpu.VMEM((rows, k), jnp.float32),
            pltpu.VMEM((rows, k), jnp.float32),
            pltpu.VMEM((n_j * blk, k), jnp.float32),
            pltpu.VMEM((2 * rows * Q_DEV, n_p2), jnp.float32),
        ],
    )(by_col, by_row)


def solution(mesh):
    return jax.shard_map(
        per_device,
        mesh=mesh,
        in_specs=(P("row", ("col", "chan"), None), P("row", "col", None), P("row", "col")),
        out_specs=P("chan", None, "row", None, "col", None),
        check_vma=False,
    )
```

```python
import functools

import jax
import ml_dtypes
import numpy as np
import jax.numpy as jnp
from jax import lax
from jax.sharding import PartitionSpec as P
from jax.experimental import pallas as pl
from jax.experimental.pallas import tpu as pltpu

NFFT = 2048
TAPS = 4
P_DEV = 8
Q_DEV = 4
CH_DEV = 16
SPECTRA = 64
LANES = 32
FRAMES = 67


def kernel_table(nfft, taps, chans):
    length = taps * nfft
    position = np.arange(length, dtype=np.float64)
    centre = (position - length / 2 + 0.5) / nfft
    window = np.sinc(centre) * (0.5 - 0.5 * np.cos(2.0 * np.pi * (position + 0.5) / length))
    window = window * np.sqrt(2.0 / np.sum(window * window))
    window = window.reshape(taps, nfft)
    sample = np.arange(nfft, dtype=np.int64)
    bin_index = nfft // 4 + np.arange(chans, dtype=np.int64)
    phase_index = bin_index[:, None] * sample[None, :] % nfft
    phases = phase_index.astype(np.float64) * (2.0 * np.pi / nfft)
    both_parts = np.stack([np.cos(phases).T, -np.sin(phases).T], 1)
    built = window.T[:, :, None, None] * both_parts[:, None, :, :]
    return jnp.asarray(built.reshape(nfft, taps * chans * 2).astype(ml_dtypes.bfloat16))


P_STEP = 2
F_PAD = 72


def _fb_kernel(x_ref, t_ref, o_ref, xs_ref, lhs_ref, acc_ref):
    n_pp = o_ref.shape[0]
    width = 2 * o_ref.shape[1]
    spectra = SPECTRA
    half_q = o_ref.shape[2] // (2 * spectra)
    frames = spectra + TAPS - 1
    per_frame = t_ref.shape[0] // 128
    stride = per_frame * half_q
    for pp in range(n_pp):
        xs_ref[pp] = x_ref[pp].astype(jnp.float32)
    for pp in range(n_pp):
        for q in range(half_q):
            base = (pp * half_q + q) * F_PAD
            lhs_ref[pl.ds(base + frames, F_PAD - frames), :] = jnp.zeros(
                (F_PAD - frames, lhs_ref.shape[1]), jnp.float32
            )
            for j in range(per_frame):
                lhs_ref[pl.ds(base, frames), pl.ds(j * 128, 128)] = xs_ref[
                    pp, pl.ds(j * half_q + q, frames, stride=stride), :
                ]
    acc_ref[...] = jnp.dot(
        lhs_ref[...].astype(jnp.bfloat16), t_ref[...], preferred_element_type=jnp.float32
    )
    for pp in range(n_pp):
        for q in range(half_q):
            base = (pp * half_q + q) * F_PAD
            tap = None
            for m in range(TAPS):
                col = (m * width) // 128
                v = acc_ref[pl.ds(base + m, spectra), pl.ds(col * 128, 128)]
                shift = (m * width) % 128
                if shift:
                    v = pltpu.roll(v, 128 - shift, 1)
                v = v[:, :width]
                tap = v if tap is None else tap + v
            tap_t = tap.T
            half = width // 2
            row = jnp.concatenate([tap_t[:half], tap_t[half:]], axis=1)
            o_ref[pp, :, pl.ds(q * 2 * spectra, 2 * spectra)] = row.astype(o_ref.dtype)


def filter_bank(native, table, half_q):
    n_p, rows, lanes = native.shape
    n_k = table.shape[1]
    width = n_k // TAPS
    m_rows = P_STEP * half_q * F_PAD
    return pl.pallas_call(
        _fb_kernel,
        grid=(n_p // P_STEP,),
        out_shape=jax.ShapeDtypeStruct((n_p, width // 2, half_q * 2 * SPECTRA), jnp.bfloat16),
        in_specs=[
            pl.BlockSpec((P_STEP, rows, lanes), lambda i: (i, 0, 0)),
            pl.BlockSpec(table.shape, lambda i: (0, 0)),
        ],
        out_specs=pl.BlockSpec((P_STEP, width // 2, half_q * 2 * SPECTRA), lambda i: (i, 0, 0)),
        scratch_shapes=[
            pltpu.VMEM((P_STEP, rows, lanes), jnp.float32),
            pltpu.VMEM((m_rows, table.shape[0]), jnp.float32),
            pltpu.VMEM((m_rows, n_k), jnp.float32),
        ],
    )(native, table)


N_CHUNK = 4


def _gather_plan(nz, nx):
    keys = []
    last = nz // 2
    for s in range(1, last + 1):
        for h in range(N_CHUNK):
            if s < last or nz % 2 or h < N_CHUNK // 2:
                keys.append(("rf", s, h))
            if s < last or (nz % 2 == 0 and h >= N_CHUNK // 2) or (nz % 2 and s <= (nz - 1) // 2):
                keys.append(("rb", s, h))
    for h in range(N_CHUNK):
        keys.append(("rf2" if h < N_CHUNK // 2 else "rb2", last, h))
    for off in range(nz):
        for h in range(N_CHUNK):
            if off != last:
                keys.append(("sib", off, h))
    for h in range(N_CHUNK):
        for kind in ("cf1", "cb1", "y0", "cf2", "y1", "of", "ob"):
            keys.append((kind, 0, h))
    return {k: i for i, k in enumerate(keys)}


def _gather_kernel(plan, x_ref, rowg_ref, colg_ref, send_sems, recv_sems, local_sems):
    nrow = lax.axis_size("row")
    ncol = lax.axis_size("col")
    r = lax.axis_index("row")
    c = lax.axis_index("col")
    ch = lax.axis_index("chan")
    nz = nrow // 2
    z = r // 2
    core = r % 2
    nx = ncol // 2
    yl = c // nx
    xx = c % nx
    cs = x_ref.shape[0] // N_CHUNK
    mesh_ids = pl.DeviceIdType.MESH

    def row_slot(zz, cc):
        return ((zz + nz) % nz) * 2 + cc

    def col_slot(yy, xv):
        return yy * nx + (xv + nx) % nx

    z_up = (row_slot(z + 1, core), c, ch)
    z_down = (row_slot(z - 1, core), c, ch)
    sibling = (row_slot(z, 1 - core), c, ch)
    z_up_x = (row_slot(z + 1, 1 - core), c, ch)
    z_down_x = (row_slot(z - 1, 1 - core), c, ch)
    x_up = (r, col_slot(yl, xx + 1), ch)
    x_down = (r, col_slot(yl, xx - 1), ch)
    y_other = (r, col_slot(1 - yl, xx), ch)

    barrier = pltpu.get_barrier_semaphore()
    neighbours = (z_up, z_down, z_up_x, z_down_x, sibling, x_up, x_down, y_other)
    for dev in neighbours:
        pl.semaphore_signal(barrier, inc=1, device_id=dev, device_id_type=mesh_ids)
    pl.semaphore_wait(barrier, len(neighbours))

    def chunk(ref, slot, h):
        return ref.at[slot, pl.ds(h * cs, cs)]

    def desc(src, dst, key, dev):
        i = plan[key]
        return pltpu.make_async_remote_copy(
            src_ref=src, dst_ref=dst, send_sem=send_sems.at[i],
            recv_sem=recv_sems.at[i], device_id=dev, device_id_type=mesh_ids)

    started = []

    def send(ref, slot, h, key, dev, from_input=False):
        src = x_ref.at[pl.ds(h * cs, cs)] if from_input else chunk(ref, slot, h)
        d = desc(src, chunk(ref, slot, h), key, dev)
        d.start()
        started.append(d)

    def wait_in(ref, slot, h, key):
        if key in plan:
            desc(chunk(ref, slot, h), chunk(ref, slot, h), key, z_up).wait_recv()

    local_row = pltpu.make_async_copy(x_ref, rowg_ref.at[r], local_sems.at[0])
    local_col = pltpu.make_async_copy(x_ref, colg_ref.at[c], local_sems.at[1])
    local_row.start()
    local_col.start()

    own_r = row_slot(z, core)
    own_c = col_slot(yl, xx)
    for h in range(N_CHUNK):
        if ("rf", 1, h) in plan:
            send(rowg_ref, own_r, h, ("rf", 1, h), z_up, True)
        if ("rb", 1, h) in plan:
            send(rowg_ref, own_r, h, ("rb", 1, h), z_down, True)
        send(rowg_ref, own_r, h, ("sib", 0, h), sibling, True)
        send(colg_ref, own_c, h, ("cf1", 0, h), x_up, True)
        send(colg_ref, own_c, h, ("cb1", 0, h), x_down, True)
        send(colg_ref, own_c, h, ("y0", 0, h), y_other, True)

    last = nz // 2
    for s in range(1, last + 1):
        for h in range(N_CHUNK):
            if ("rf", s, h) in plan:
                slot = row_slot(z - s, core)
                wait_in(rowg_ref, slot, h, ("rf", s, h))
                if ("rf", s + 1, h) in plan:
                    send(rowg_ref, slot, h, ("rf", s + 1, h), z_up)
                if ("rf2", s + 1, h) in plan:
                    send(rowg_ref, slot, h, ("rf2", s + 1, h), z_up_x)
                if ("sib", (nz - s) % nz, h) in plan:
                    send(rowg_ref, slot, h, ("sib", (nz - s) % nz, h), sibling)
            if ("rb", s, h) in plan:
                slot = row_slot(z + s, core)
                wait_in(rowg_ref, slot, h, ("rb", s, h))
                if ("rb", s + 1, h) in plan:
                    send(rowg_ref, slot, h, ("rb", s + 1, h), z_down)
                if ("rb2", s + 1, h) in plan:
                    send(rowg_ref, slot, h, ("rb2", s + 1, h), z_down_x)
                if ("sib", s, h) in plan:
                    send(rowg_ref, slot, h, ("sib", s, h), sibling)
            if s == 1:
                slot = col_slot(yl, xx - 1)
                wait_in(colg_ref, slot, h, ("cf1", 0, h))
                send(colg_ref, slot, h, ("cf2", 0, h), x_up)
                send(colg_ref, slot, h, ("y1", 0, h), y_other)
                slot = col_slot(1 - yl, xx)
                wait_in(colg_ref, slot, h, ("y0", 0, h))
                send(colg_ref, slot, h, ("ob", 0, h), x_down)
            if s == 2:
                slot = col_slot(1 - yl, xx - 1)
                wait_in(colg_ref, slot, h, ("y1", 0, h))
                send(colg_ref, slot, h, ("of", 0, h), x_up)

    for h in range(N_CHUNK):
        wait_in(colg_ref, col_slot(yl, xx + 1), h, ("cb1", 0, h))
        wait_in(colg_ref, col_slot(yl, xx - 2), h, ("cf2", 0, h))
        wait_in(colg_ref, col_slot(1 - yl, xx + 1), h, ("ob", 0, h))
        wait_in(colg_ref, col_slot(1 - yl, xx - 2), h, ("of", 0, h))
    for off in range(nz):
        for h in range(N_CHUNK):
            wait_in(rowg_ref, row_slot(z + off, 1 - core), h, ("sib", off, h))
    for h in range(N_CHUNK):
        wait_in(rowg_ref, row_slot(z - last, 1 - core), h, ("rf2", last, h))
        wait_in(rowg_ref, row_slot(z + last, 1 - core), h, ("rb2", last, h))
    for d in started:
        d.wait_send()
    local_row.wait()
    local_col.wait()


def gather_both(x):
    nrow = lax.axis_size("row")
    ncol = lax.axis_size("col")
    assert ncol == 8 and nrow % 4 == 0 and nrow >= 8 and x.shape[0] % N_CHUNK == 0
    plan = _gather_plan(nrow // 2, ncol // 2)
    any_spec = pl.BlockSpec(memory_space=pl.ANY)
    return pl.pallas_call(
        functools.partial(_gather_kernel, plan),
        out_shape=(
            jax.ShapeDtypeStruct((nrow,) + x.shape, x.dtype),
            jax.ShapeDtypeStruct((ncol,) + x.shape, x.dtype),
        ),
        in_specs=[any_spec],
        out_specs=(any_spec, any_spec),
        scratch_shapes=[
            pltpu.SemaphoreType.DMA((len(plan),)),
            pltpu.SemaphoreType.DMA((len(plan),)),
            pltpu.SemaphoreType.DMA((2,)),
        ],
        compiler_params=pltpu.CompilerParams(collective_id=0, has_side_effects=True),
    )(x)


def per_device(voltages, lane_map, input_flags):
    n_chan = lax.axis_size("chan")
    all_chans = CH_DEV * n_chan
    half_q = voltages.shape[1]
    table_rows = kernel_table(NFFT, TAPS, all_chans)
    lane_chunks = voltages.shape[2] // 128
    native = (
        voltages.reshape(P_DEV, half_q, lane_chunks, 128)
        .transpose(0, 2, 1, 3)
        .reshape(P_DEV, lane_chunks * half_q, 128)
    )
    filtered = filter_bank(native, table_rows, half_q)
    filtered = filtered.reshape(P_DEV, all_chans, half_q, 2 * SPECTRA).transpose(1, 0, 2, 3)
    me_chan = lax.axis_index("chan")
    halves = filtered.reshape(n_chan, CH_DEV, P_DEV, half_q, 2 * SPECTRA)
    kept = jnp.where(me_chan == 0, halves[0], halves[1])
    sent = jnp.where(me_chan == 0, halves[1], halves[0])
    received = lax.ppermute(sent, "chan", [(0, 1), (1, 0)])
    first = jnp.where(me_chan == 0, kept, received)
    second = jnp.where(me_chan == 0, received, kept)
    turned_over = jnp.concatenate([first, second], axis=2)
    lane_rows = turned_over.reshape(CH_DEV, LANES, 2 * SPECTRA)
    lane_index = lane_map.reshape(LANES)
    selector = (lane_index[:, None] == jnp.arange(LANES, dtype=jnp.int32)[None, :]).astype(
        jnp.bfloat16
    )
    reordered = jnp.einsum("kl,clz->ckz", selector, lane_rows, preferred_element_type=jnp.float32)
    weights = input_flags.reshape(LANES).astype(jnp.float32)[None, :, None]
    channelised = (
        (reordered * weights).astype(jnp.bfloat16).reshape(CH_DEV, P_DEV, Q_DEV, 2 * SPECTRA)
    )
    by_row, by_col = gather_both(channelised.reshape(CH_DEV, P_DEV * Q_DEV, 2 * SPECTRA))
    n_row = by_row.shape[0]
    grid_cols = by_col.shape[0] * Q_DEV
    products = correlate(by_col, by_row)
    return products.reshape(CH_DEV, 2, P_DEV, grid_cols, Q_DEV, n_row * P_DEV)


CH_STEP = 4


def _corr_kernel(c_ref, g_ref, out_ref, cf_ref, lf_ref, rf_ref, acc_ref):
    n_i, blk_i, width = c_ref.shape[0], c_ref.shape[2], c_ref.shape[3]
    n_j, blk = g_ref.shape[0], g_ref.shape[2]
    n_q = Q_DEV
    n_pl = blk_i // n_q
    rows = n_i * blk_i
    n_p2 = n_j * blk // n_q
    lane = lax.broadcasted_iota(jnp.int32, (rows, width), 1)
    for cc in range(c_ref.shape[1]):
        for i in range(n_i):
            cf_ref[pl.ds(i * blk_i, blk_i), :] = c_ref[i, cc].astype(jnp.float32)
        for p in range(n_pl):
            for q in range(n_q):
                lf_ref[pl.ds(p * n_i * n_q + q, n_i, stride=n_q), :] = cf_ref[
                    pl.ds(p * n_q + q, n_i, stride=blk_i), :
                ]
        a32 = lf_ref[...]
        rolled = pltpu.roll(a32, width // 2, 1)
        a_rot = jnp.where(lane >= width // 2, -rolled, rolled)
        both = jnp.concatenate([a32, a_rot], axis=0).astype(out_ref.dtype)
        for j in range(n_j):
            rf_ref[pl.ds(j * blk, blk), :] = g_ref[j, cc].astype(jnp.float32)
        for q2 in range(n_q):
            b = rf_ref[pl.ds(q2, n_p2, stride=n_q), :].astype(out_ref.dtype)
            acc_ref[pl.ds(q2, 2 * rows, stride=n_q), :] = lax.dot_general(
                both, b, (((1,), (1,)), ((), ())), preferred_element_type=jnp.float32
            )
        out_ref[cc] = (acc_ref[...] * (1.0 / SPECTRA)).astype(out_ref.dtype).reshape(out_ref.shape[1:])


def correlate(by_col, by_row):
    n_i, n_c, blk_i, k = by_col.shape
    n_j, _, blk, _ = by_row.shape
    rows = n_i * blk_i
    n_p2 = n_j * blk // Q_DEV
    out_rows = rows * Q_DEV // P_DEV
    return pl.pallas_call(
        _corr_kernel,
        grid=(n_c // CH_STEP,),
        out_shape=jax.ShapeDtypeStruct((n_c, 2, P_DEV, out_rows, n_p2), jnp.bfloat16),
        in_specs=[
            pl.BlockSpec((n_i, CH_STEP, blk_i, k), lambda i: (0, i, 0, 0)),
            pl.BlockSpec((n_j, CH_STEP, blk, k), lambda i: (0, i, 0, 0)),
        ],
        out_specs=pl.BlockSpec((CH_STEP, 2, P_DEV, out_rows, n_p2), lambda i: (i, 0, 0, 0, 0)),
        scratch_shapes=[
            pltpu.VMEM((rows, k), jnp.float32),
            pltpu.VMEM((rows, k), jnp.float32),
            pltpu.VMEM((n_j * blk, k), jnp.float32),
            pltpu.VMEM((2 * rows * Q_DEV, n_p2), jnp.float32),
        ],
    )(by_col, by_row)


def solution(mesh):
    return jax.shard_map(
        per_device,
        mesh=mesh,
        in_specs=(P("row", ("col", "chan"), None), P("row", "col", None), P("row", "col")),
        out_specs=P("chan", None, "row", None, "col", None),
        check_vma=False,
    )
```

```python
import functools

import jax
import ml_dtypes
import numpy as np
import jax.numpy as jnp
from jax import lax
from jax.sharding import PartitionSpec as P
from jax.experimental import pallas as pl
from jax.experimental.pallas import tpu as pltpu

NFFT = 2048
TAPS = 4
P_DEV = 8
Q_DEV = 4
CH_DEV = 16
SPECTRA = 64
LANES = 32
FRAMES = 67


def kernel_table(nfft, taps, chans):
    length = taps * nfft
    position = np.arange(length, dtype=np.float64)
    centre = (position - length / 2 + 0.5) / nfft
    window = np.sinc(centre) * (0.5 - 0.5 * np.cos(2.0 * np.pi * (position + 0.5) / length))
    window = window * np.sqrt(2.0 / np.sum(window * window))
    window = window.reshape(taps, nfft)
    sample = np.arange(nfft, dtype=np.int64)
    bin_index = nfft // 4 + np.arange(chans, dtype=np.int64)
    phase_index = bin_index[:, None] * sample[None, :] % nfft
    phases = phase_index.astype(np.float64) * (2.0 * np.pi / nfft)
    both_parts = np.stack([np.cos(phases).T, -np.sin(phases).T], -1)
    built = window.T[:, :, None, None] * both_parts[:, None, :, :]
    return jnp.asarray(built.reshape(nfft, taps * chans * 2).astype(ml_dtypes.bfloat16))


P_STEP = 2
F_PAD = 72


def _fb_kernel(x_ref, t_ref, o_ref, xs_ref, lhs_ref, acc_ref):
    n_pp, half_q, spectra = o_ref.shape[0], o_ref.shape[1], o_ref.shape[2]
    width = o_ref.shape[3]
    frames = spectra + TAPS - 1
    per_frame = t_ref.shape[0] // 128
    stride = per_frame * half_q
    for pp in range(n_pp):
        xs_ref[pp] = x_ref[pp].astype(jnp.float32)
    for pp in range(n_pp):
        for q in range(half_q):
            base = (pp * half_q + q) * F_PAD
            lhs_ref[pl.ds(base + frames, F_PAD - frames), :] = jnp.zeros(
                (F_PAD - frames, lhs_ref.shape[1]), jnp.float32
            )
            for j in range(per_frame):
                lhs_ref[pl.ds(base, frames), pl.ds(j * 128, 128)] = xs_ref[
                    pp, pl.ds(j * half_q + q, frames, stride=stride), :
                ]
    acc_ref[...] = jnp.dot(
        lhs_ref[...].astype(jnp.bfloat16), t_ref[...], preferred_element_type=jnp.float32
    )
    for pp in range(n_pp):
        for q in range(half_q):
            base = (pp * half_q + q) * F_PAD
            tap = None
            for m in range(TAPS):
                col = (m * width) // 128
                v = acc_ref[pl.ds(base + m, spectra), pl.ds(col * 128, 128)]
                shift = (m * width) % 128
                if shift:
                    v = pltpu.roll(v, 128 - shift, 1)
                v = v[:, :width]
                tap = v if tap is None else tap + v
            o_ref[pp, q] = tap.astype(o_ref.dtype)


def filter_bank(native, table, half_q):
    n_p, rows, lanes = native.shape
    n_k = table.shape[1]
    width = n_k // TAPS
    m_rows = P_STEP * half_q * F_PAD
    return pl.pallas_call(
        _fb_kernel,
        grid=(n_p // P_STEP,),
        out_shape=jax.ShapeDtypeStruct((n_p, half_q, SPECTRA, width), jnp.bfloat16),
        in_specs=[
            pl.BlockSpec((P_STEP, rows, lanes), lambda i: (i, 0, 0)),
            pl.BlockSpec(table.shape, lambda i: (0, 0)),
        ],
        out_specs=pl.BlockSpec((P_STEP, half_q, SPECTRA, width), lambda i: (i, 0, 0, 0)),
        scratch_shapes=[
            pltpu.VMEM((P_STEP, rows, lanes), jnp.float32),
            pltpu.VMEM((m_rows, table.shape[0]), jnp.float32),
            pltpu.VMEM((m_rows, n_k), jnp.float32),
        ],
    )(native, table)


N_CHUNK = 4


def _gather_plan(nz, nx):
    keys = []
    last = nz // 2
    for s in range(1, last + 1):
        for h in range(N_CHUNK):
            if s < last or nz % 2 or h < N_CHUNK // 2:
                keys.append(("rf", s, h))
            if s < last or (nz % 2 == 0 and h >= N_CHUNK // 2) or (nz % 2 and s <= (nz - 1) // 2):
                keys.append(("rb", s, h))
    for h in range(N_CHUNK):
        keys.append(("rf2" if h < N_CHUNK // 2 else "rb2", last, h))
    for off in range(nz):
        for h in range(N_CHUNK):
            if off != last:
                keys.append(("sib", off, h))
    for h in range(N_CHUNK):
        for kind in ("cf1", "cb1", "y0", "cf2", "y1", "of", "ob"):
            keys.append((kind, 0, h))
    return {k: i for i, k in enumerate(keys)}


def _gather_kernel(plan, x_ref, rowg_ref, colg_ref, send_sems, recv_sems, local_sems):
    nrow = lax.axis_size("row")
    ncol = lax.axis_size("col")
    r = lax.axis_index("row")
    c = lax.axis_index("col")
    ch = lax.axis_index("chan")
    nz = nrow // 2
    z = r // 2
    core = r % 2
    nx = ncol // 2
    yl = c // nx
    xx = c % nx
    cs = x_ref.shape[0] // N_CHUNK
    mesh_ids = pl.DeviceIdType.MESH

    def row_slot(zz, cc):
        return ((zz + nz) % nz) * 2 + cc

    def col_slot(yy, xv):
        return yy * nx + (xv + nx) % nx

    z_up = (row_slot(z + 1, core), c, ch)
    z_down = (row_slot(z - 1, core), c, ch)
    sibling = (row_slot(z, 1 - core), c, ch)
    z_up_x = (row_slot(z + 1, 1 - core), c, ch)
    z_down_x = (row_slot(z - 1, 1 - core), c, ch)
    x_up = (r, col_slot(yl, xx + 1), ch)
    x_down = (r, col_slot(yl, xx - 1), ch)
    y_other = (r, col_slot(1 - yl, xx), ch)

    barrier = pltpu.get_barrier_semaphore()
    neighbours = (z_up, z_down, z_up_x, z_down_x, sibling, x_up, x_down, y_other)
    for dev in neighbours:
        pl.semaphore_signal(barrier, inc=1, device_id=dev, device_id_type=mesh_ids)
    pl.semaphore_wait(barrier, len(neighbours))

    def chunk(ref, slot, h):
        return ref.at[slot, pl.ds(h * cs, cs)]

    def desc(src, dst, key, dev):
        i = plan[key]
        return pltpu.make_async_remote_copy(
            src_ref=src, dst_ref=dst, send_sem=send_sems.at[i],
            recv_sem=recv_sems.at[i], device_id=dev, device_id_type=mesh_ids)

    started = []

    def send(ref, slot, h, key, dev, from_input=False):
        src = x_ref.at[pl.ds(h * cs, cs)] if from_input else chunk(ref, slot, h)
        d = desc(src, chunk(ref, slot, h), key, dev)
        d.start()
        started.append(d)

    def wait_in(ref, slot, h, key):
        if key in plan:
            desc(chunk(ref, slot, h), chunk(ref, slot, h), key, z_up).wait_recv()

    local_row = pltpu.make_async_copy(x_ref, rowg_ref.at[r], local_sems.at[0])
    local_col = pltpu.make_async_copy(x_ref, colg_ref.at[c], local_sems.at[1])
    local_row.start()
    local_col.start()

    own_r = row_slot(z, core)
    own_c = col_slot(yl, xx)
    for h in range(N_CHUNK):
        if ("rf", 1, h) in plan:
            send(rowg_ref, own_r, h, ("rf", 1, h), z_up, True)
        if ("rb", 1, h) in plan:
            send(rowg_ref, own_r, h, ("rb", 1, h), z_down, True)
        send(rowg_ref, own_r, h, ("sib", 0, h), sibling, True)
        send(colg_ref, own_c, h, ("cf1", 0, h), x_up, True)
        send(colg_ref, own_c, h, ("cb1", 0, h), x_down, True)
        send(colg_ref, own_c, h, ("y0", 0, h), y_other, True)

    last = nz // 2
    for s in range(1, last + 1):
        for h in range(N_CHUNK):
            if ("rf", s, h) in plan:
                slot = row_slot(z - s, core)
                wait_in(rowg_ref, slot, h, ("rf", s, h))
                if ("rf", s + 1, h) in plan:
                    send(rowg_ref, slot, h, ("rf", s + 1, h), z_up)
                if ("rf2", s + 1, h) in plan:
                    send(rowg_ref, slot, h, ("rf2", s + 1, h), z_up_x)
                if ("sib", (nz - s) % nz, h) in plan:
                    send(rowg_ref, slot, h, ("sib", (nz - s) % nz, h), sibling)
            if ("rb", s, h) in plan:
                slot = row_slot(z + s, core)
                wait_in(rowg_ref, slot, h, ("rb", s, h))
                if ("rb", s + 1, h) in plan:
                    send(rowg_ref, slot, h, ("rb", s + 1, h), z_down)
                if ("rb2", s + 1, h) in plan:
                    send(rowg_ref, slot, h, ("rb2", s + 1, h), z_down_x)
                if ("sib", s, h) in plan:
                    send(rowg_ref, slot, h, ("sib", s, h), sibling)
            if s == 1:
                slot = col_slot(yl, xx - 1)
                wait_in(colg_ref, slot, h, ("cf1", 0, h))
                send(colg_ref, slot, h, ("cf2", 0, h), x_up)
                send(colg_ref, slot, h, ("y1", 0, h), y_other)
                slot = col_slot(1 - yl, xx)
                wait_in(colg_ref, slot, h, ("y0", 0, h))
                send(colg_ref, slot, h, ("ob", 0, h), x_down)
            if s == 2:
                slot = col_slot(1 - yl, xx - 1)
                wait_in(colg_ref, slot, h, ("y1", 0, h))
                send(colg_ref, slot, h, ("of", 0, h), x_up)

    for h in range(N_CHUNK):
        wait_in(colg_ref, col_slot(yl, xx + 1), h, ("cb1", 0, h))
        wait_in(colg_ref, col_slot(yl, xx - 2), h, ("cf2", 0, h))
        wait_in(colg_ref, col_slot(1 - yl, xx + 1), h, ("ob", 0, h))
        wait_in(colg_ref, col_slot(1 - yl, xx - 2), h, ("of", 0, h))
    for off in range(nz):
        for h in range(N_CHUNK):
            wait_in(rowg_ref, row_slot(z + off, 1 - core), h, ("sib", off, h))
    for h in range(N_CHUNK):
        wait_in(rowg_ref, row_slot(z - last, 1 - core), h, ("rf2", last, h))
        wait_in(rowg_ref, row_slot(z + last, 1 - core), h, ("rb2", last, h))
    for d in started:
        d.wait_send()
    local_row.wait()
    local_col.wait()


def gather_both(x):
    nrow = lax.axis_size("row")
    ncol = lax.axis_size("col")
    assert ncol == 8 and nrow % 4 == 0 and nrow >= 8 and x.shape[0] % N_CHUNK == 0
    plan = _gather_plan(nrow // 2, ncol // 2)
    any_spec = pl.BlockSpec(memory_space=pl.ANY)
    return pl.pallas_call(
        functools.partial(_gather_kernel, plan),
        out_shape=(
            jax.ShapeDtypeStruct((nrow,) + x.shape, x.dtype),
            jax.ShapeDtypeStruct((ncol,) + x.shape, x.dtype),
        ),
        in_specs=[any_spec],
        out_specs=(any_spec, any_spec),
        scratch_shapes=[
            pltpu.SemaphoreType.DMA((len(plan),)),
            pltpu.SemaphoreType.DMA((len(plan),)),
            pltpu.SemaphoreType.DMA((2,)),
        ],
        compiler_params=pltpu.CompilerParams(collective_id=0, has_side_effects=True),
    )(x)


def per_device(voltages, lane_map, input_flags):
    n_chan = lax.axis_size("chan")
    all_chans = CH_DEV * n_chan
    half_q = voltages.shape[1]
    table_rows = kernel_table(NFFT, TAPS, all_chans)
    lane_chunks = voltages.shape[2] // 128
    native = (
        voltages.reshape(P_DEV, half_q, lane_chunks, 128)
        .transpose(0, 2, 1, 3)
        .reshape(P_DEV, lane_chunks * half_q, 128)
    )
    filtered = filter_bank(native, table_rows, half_q)
    filtered = filtered.reshape(P_DEV, half_q, SPECTRA, all_chans, 2)
    filtered = filtered.transpose(3, 0, 1, 4, 2).reshape(all_chans, P_DEV, half_q, 2 * SPECTRA)
    me_chan = lax.axis_index("chan")
    halves = filtered.reshape(n_chan, CH_DEV, P_DEV, half_q, 2 * SPECTRA)
    kept = jnp.where(me_chan == 0, halves[0], halves[1])
    sent = jnp.where(me_chan == 0, halves[1], halves[0])
    received = lax.ppermute(sent, "chan", [(0, 1), (1, 0)])
    lane_index = lane_map.reshape(LANES)
    selector = (lane_index[:, None] == jnp.arange(LANES, dtype=jnp.int32)[None, :]).astype(
        jnp.bfloat16
    )
    by_holder = selector.reshape(LANES, P_DEV, n_chan, half_q)
    sel_kept = jnp.where(me_chan == 0, by_holder[:, :, 0], by_holder[:, :, 1]).reshape(LANES, -1)
    sel_recv = jnp.where(me_chan == 0, by_holder[:, :, 1], by_holder[:, :, 0]).reshape(LANES, -1)
    kept_rows = kept.reshape(CH_DEV, P_DEV * half_q, 2 * SPECTRA)
    recv_rows = received.reshape(CH_DEV, P_DEV * half_q, 2 * SPECTRA)
    reordered = jnp.einsum(
        "kl,clz->ckz", sel_kept, kept_rows, preferred_element_type=jnp.float32
    ) + jnp.einsum("kl,clz->ckz", sel_recv, recv_rows, preferred_element_type=jnp.float32)
    weights = input_flags.reshape(LANES).astype(jnp.float32)[None, :, None]
    channelised = (
        (reordered * weights).astype(jnp.bfloat16).reshape(CH_DEV, P_DEV, Q_DEV, 2 * SPECTRA)
    )
    by_row, by_col = gather_both(channelised.reshape(CH_DEV, P_DEV * Q_DEV, 2 * SPECTRA))
    n_row = by_row.shape[0]
    grid_cols = by_col.shape[0] * Q_DEV
    products = correlate(by_col, by_row)
    return products.reshape(CH_DEV, 2, P_DEV, grid_cols, Q_DEV, n_row * P_DEV)


CH_STEP = 4


def _corr_kernel(c_ref, g_ref, out_ref, cf_ref, lf_ref, rf_ref, acc_ref):
    n_i, blk_i, width = c_ref.shape[0], c_ref.shape[2], c_ref.shape[3]
    n_j, blk = g_ref.shape[0], g_ref.shape[2]
    n_q = Q_DEV
    n_pl = blk_i // n_q
    rows = n_i * blk_i
    n_p2 = n_j * blk // n_q
    lane = lax.broadcasted_iota(jnp.int32, (rows, width), 1)
    for cc in range(c_ref.shape[1]):
        for i in range(n_i):
            cf_ref[pl.ds(i * blk_i, blk_i), :] = c_ref[i, cc].astype(jnp.float32)
        for p in range(n_pl):
            for q in range(n_q):
                lf_ref[pl.ds(p * n_i * n_q + q, n_i, stride=n_q), :] = cf_ref[
                    pl.ds(p * n_q + q, n_i, stride=blk_i), :
                ]
        a32 = lf_ref[...]
        rolled = pltpu.roll(a32, width // 2, 1)
        a_rot = jnp.where(lane >= width // 2, -rolled, rolled)
        both = jnp.concatenate([a32, a_rot], axis=0).astype(out_ref.dtype)
        for j in range(n_j):
            rf_ref[pl.ds(j * blk, blk), :] = g_ref[j, cc].astype(jnp.float32)
        for q2 in range(n_q):
            b = rf_ref[pl.ds(q2, n_p2, stride=n_q), :].astype(out_ref.dtype)
            acc_ref[pl.ds(q2, 2 * rows, stride=n_q), :] = lax.dot_general(
                both, b, (((1,), (1,)), ((), ())), preferred_element_type=jnp.float32
            )
        out_ref[cc] = (acc_ref[...] * (1.0 / SPECTRA)).astype(out_ref.dtype).reshape(out_ref.shape[1:])


def correlate(by_col, by_row):
    n_i, n_c, blk_i, k = by_col.shape
    n_j, _, blk, _ = by_row.shape
    rows = n_i * blk_i
    n_p2 = n_j * blk // Q_DEV
    out_rows = rows * Q_DEV // P_DEV
    return pl.pallas_call(
        _corr_kernel,
        grid=(n_c // CH_STEP,),
        out_shape=jax.ShapeDtypeStruct((n_c, 2, P_DEV, out_rows, n_p2), jnp.bfloat16),
        in_specs=[
            pl.BlockSpec((n_i, CH_STEP, blk_i, k), lambda i: (0, i, 0, 0)),
            pl.BlockSpec((n_j, CH_STEP, blk, k), lambda i: (0, i, 0, 0)),
        ],
        out_specs=pl.BlockSpec((CH_STEP, 2, P_DEV, out_rows, n_p2), lambda i: (i, 0, 0, 0, 0)),
        scratch_shapes=[
            pltpu.VMEM((rows, k), jnp.float32),
            pltpu.VMEM((rows, k), jnp.float32),
            pltpu.VMEM((n_j * blk, k), jnp.float32),
            pltpu.VMEM((2 * rows * Q_DEV, n_p2), jnp.float32),
        ],
    )(by_col, by_row)


def solution(mesh):
    return jax.shard_map(
        per_device,
        mesh=mesh,
        in_specs=(P("row", ("col", "chan"), None), P("row", "col", None), P("row", "col")),
        out_specs=P("chan", None, "row", None, "col", None),
        check_vma=False,
    )
```

```python
import functools

import jax
import ml_dtypes
import numpy as np
import jax.numpy as jnp
from jax import lax
from jax.sharding import PartitionSpec as P
from jax.experimental import pallas as pl
from jax.experimental.pallas import tpu as pltpu

NFFT = 2048
TAPS = 4
P_DEV = 8
Q_DEV = 4
CH_DEV = 16
SPECTRA = 64
LANES = 32
FRAMES = 67


def kernel_table(nfft, taps, chans):
    length = taps * nfft
    position = np.arange(length, dtype=np.float64)
    centre = (position - length / 2 + 0.5) / nfft
    window = np.sinc(centre) * (0.5 - 0.5 * np.cos(2.0 * np.pi * (position + 0.5) / length))
    window = window * np.sqrt(2.0 / np.sum(window * window))
    window = window.reshape(taps, nfft)
    sample = np.arange(nfft, dtype=np.int64)
    bin_index = nfft // 4 + np.arange(chans, dtype=np.int64)
    phase_index = bin_index[:, None] * sample[None, :] % nfft
    phases = phase_index.astype(np.float64) * (2.0 * np.pi / nfft)
    both_parts = np.stack([np.cos(phases).T, -np.sin(phases).T], -1)
    built = window.T[:, :, None, None] * both_parts[:, None, :, :]
    return jnp.asarray(built.reshape(nfft, taps * chans * 2).astype(ml_dtypes.bfloat16))


P_STEP = 2
F_PAD = 72


def _fb_kernel(x_ref, t_ref, o_ref, xs_ref, lhs_ref, acc_ref):
    n_pp, half_q, spectra = o_ref.shape[0], o_ref.shape[1], o_ref.shape[2]
    width = o_ref.shape[3]
    frames = spectra + TAPS - 1
    per_frame = t_ref.shape[0] // 128
    stride = per_frame * half_q
    for pp in range(n_pp):
        xs_ref[pp] = x_ref[pp].astype(jnp.float32)
    for pp in range(n_pp):
        for q in range(half_q):
            base = (pp * half_q + q) * F_PAD
            lhs_ref[pl.ds(base + frames, F_PAD - frames), :] = jnp.zeros(
                (F_PAD - frames, lhs_ref.shape[1]), jnp.float32
            )
            for j in range(per_frame):
                lhs_ref[pl.ds(base, frames), pl.ds(j * 128, 128)] = xs_ref[
                    pp, pl.ds(j * half_q + q, frames, stride=stride), :
                ]
    acc_ref[...] = jnp.dot(
        lhs_ref[...].astype(jnp.bfloat16), t_ref[...], preferred_element_type=jnp.float32
    )
    for pp in range(n_pp):
        for q in range(half_q):
            base = (pp * half_q + q) * F_PAD
            tap = None
            for m in range(TAPS):
                col = (m * width) // 128
                v = acc_ref[pl.ds(base + m, spectra), pl.ds(col * 128, 128)]
                shift = (m * width) % 128
                if shift:
                    v = pltpu.roll(v, 128 - shift, 1)
                v = v[:, :width]
                tap = v if tap is None else tap + v
            o_ref[pp, q] = tap.astype(o_ref.dtype)


def filter_bank(native, table, half_q):
    n_p, rows, lanes = native.shape
    n_k = table.shape[1]
    width = n_k // TAPS
    m_rows = P_STEP * half_q * F_PAD
    return pl.pallas_call(
        _fb_kernel,
        grid=(n_p // P_STEP,),
        out_shape=jax.ShapeDtypeStruct((n_p, half_q, SPECTRA, width), jnp.bfloat16),
        in_specs=[
            pl.BlockSpec((P_STEP, rows, lanes), lambda i: (i, 0, 0)),
            pl.BlockSpec(table.shape, lambda i: (0, 0)),
        ],
        out_specs=pl.BlockSpec((P_STEP, half_q, SPECTRA, width), lambda i: (i, 0, 0, 0)),
        scratch_shapes=[
            pltpu.VMEM((P_STEP, rows, lanes), jnp.float32),
            pltpu.VMEM((m_rows, table.shape[0]), jnp.float32),
            pltpu.VMEM((m_rows, n_k), jnp.float32),
        ],
    )(native, table)


N_CHUNK = 4


def _gather_plan(nz, nx):
    keys = []
    last = nz // 2
    for s in range(1, last + 1):
        for h in range(N_CHUNK):
            if s < last or nz % 2 or h < N_CHUNK // 2:
                keys.append(("rf", s, h))
            if s < last or (nz % 2 == 0 and h >= N_CHUNK // 2) or (nz % 2 and s <= (nz - 1) // 2):
                keys.append(("rb", s, h))
    for h in range(N_CHUNK):
        keys.append(("rf2" if h < N_CHUNK // 2 else "rb2", last, h))
    for off in range(nz):
        for h in range(N_CHUNK):
            if off != last:
                keys.append(("sib", off, h))
    for h in range(N_CHUNK):
        for kind in ("cf1", "cb1", "y0", "cf2", "y1", "of", "ob"):
            keys.append((kind, 0, h))
    return {k: i for i, k in enumerate(keys)}


def _gather_kernel(plan, x_ref, rowg_ref, colg_ref, send_sems, recv_sems, local_sems):
    nrow = lax.axis_size("row")
    ncol = lax.axis_size("col")
    r = lax.axis_index("row")
    c = lax.axis_index("col")
    ch = lax.axis_index("chan")
    nz = nrow // 2
    z = r // 2
    core = r % 2
    nx = ncol // 2
    yl = c // nx
    xx = c % nx
    cs = x_ref.shape[0] // N_CHUNK
    mesh_ids = pl.DeviceIdType.MESH

    def row_slot(zz, cc):
        return ((zz + nz) % nz) * 2 + cc

    def col_slot(yy, xv):
        return yy * nx + (xv + nx) % nx

    z_up = (row_slot(z + 1, core), c, ch)
    z_down = (row_slot(z - 1, core), c, ch)
    sibling = (row_slot(z, 1 - core), c, ch)
    z_up_x = (row_slot(z + 1, 1 - core), c, ch)
    z_down_x = (row_slot(z - 1, 1 - core), c, ch)
    x_up = (r, col_slot(yl, xx + 1), ch)
    x_down = (r, col_slot(yl, xx - 1), ch)
    y_other = (r, col_slot(1 - yl, xx), ch)

    barrier = pltpu.get_barrier_semaphore()
    neighbours = (z_up, z_down, z_up_x, z_down_x, sibling, x_up, x_down, y_other)
    for dev in neighbours:
        pl.semaphore_signal(barrier, inc=1, device_id=dev, device_id_type=mesh_ids)
    pl.semaphore_wait(barrier, len(neighbours))

    def chunk(ref, slot, h):
        return ref.at[slot, pl.ds(h * cs, cs)]

    def desc(src, dst, key, dev):
        i = plan[key]
        return pltpu.make_async_remote_copy(
            src_ref=src, dst_ref=dst, send_sem=send_sems.at[i],
            recv_sem=recv_sems.at[i], device_id=dev, device_id_type=mesh_ids)

    started = []

    def send(ref, slot, h, key, dev, from_input=False):
        src = x_ref.at[pl.ds(h * cs, cs)] if from_input else chunk(ref, slot, h)
        d = desc(src, chunk(ref, slot, h), key, dev)
        d.start()
        started.append(d)

    def wait_in(ref, slot, h, key):
        if key in plan:
            desc(chunk(ref, slot, h), chunk(ref, slot, h), key, z_up).wait_recv()

    local_row = pltpu.make_async_copy(x_ref, rowg_ref.at[r], local_sems.at[0])
    local_col = pltpu.make_async_copy(x_ref, colg_ref.at[c], local_sems.at[1])
    local_row.start()
    local_col.start()

    own_r = row_slot(z, core)
    own_c = col_slot(yl, xx)
    for h in range(N_CHUNK):
        if ("rf", 1, h) in plan:
            send(rowg_ref, own_r, h, ("rf", 1, h), z_up, True)
        if ("rb", 1, h) in plan:
            send(rowg_ref, own_r, h, ("rb", 1, h), z_down, True)
        send(rowg_ref, own_r, h, ("sib", 0, h), sibling, True)
        send(colg_ref, own_c, h, ("cf1", 0, h), x_up, True)
        send(colg_ref, own_c, h, ("cb1", 0, h), x_down, True)
        send(colg_ref, own_c, h, ("y0", 0, h), y_other, True)

    last = nz // 2
    for s in range(1, last + 1):
        for h in range(N_CHUNK):
            if ("rf", s, h) in plan:
                slot = row_slot(z - s, core)
                wait_in(rowg_ref, slot, h, ("rf", s, h))
                if ("rf", s + 1, h) in plan:
                    send(rowg_ref, slot, h, ("rf", s + 1, h), z_up)
                if ("rf2", s + 1, h) in plan:
                    send(rowg_ref, slot, h, ("rf2", s + 1, h), z_up_x)
                if ("sib", (nz - s) % nz, h) in plan:
                    send(rowg_ref, slot, h, ("sib", (nz - s) % nz, h), sibling)
            if ("rb", s, h) in plan:
                slot = row_slot(z + s, core)
                wait_in(rowg_ref, slot, h, ("rb", s, h))
                if ("rb", s + 1, h) in plan:
                    send(rowg_ref, slot, h, ("rb", s + 1, h), z_down)
                if ("rb2", s + 1, h) in plan:
                    send(rowg_ref, slot, h, ("rb2", s + 1, h), z_down_x)
                if ("sib", s, h) in plan:
                    send(rowg_ref, slot, h, ("sib", s, h), sibling)
            if s == 1:
                slot = col_slot(yl, xx - 1)
                wait_in(colg_ref, slot, h, ("cf1", 0, h))
                send(colg_ref, slot, h, ("cf2", 0, h), x_up)
                send(colg_ref, slot, h, ("y1", 0, h), y_other)
                slot = col_slot(1 - yl, xx)
                wait_in(colg_ref, slot, h, ("y0", 0, h))
                send(colg_ref, slot, h, ("ob", 0, h), x_down)
            if s == 2:
                slot = col_slot(1 - yl, xx - 1)
                wait_in(colg_ref, slot, h, ("y1", 0, h))
                send(colg_ref, slot, h, ("of", 0, h), x_up)

    for h in range(N_CHUNK):
        wait_in(colg_ref, col_slot(yl, xx + 1), h, ("cb1", 0, h))
        wait_in(colg_ref, col_slot(yl, xx - 2), h, ("cf2", 0, h))
        wait_in(colg_ref, col_slot(1 - yl, xx + 1), h, ("ob", 0, h))
        wait_in(colg_ref, col_slot(1 - yl, xx - 2), h, ("of", 0, h))
    for off in range(nz):
        for h in range(N_CHUNK):
            wait_in(rowg_ref, row_slot(z + off, 1 - core), h, ("sib", off, h))
    for h in range(N_CHUNK):
        wait_in(rowg_ref, row_slot(z - last, 1 - core), h, ("rf2", last, h))
        wait_in(rowg_ref, row_slot(z + last, 1 - core), h, ("rb2", last, h))
    for d in started:
        d.wait_send()
    local_row.wait()
    local_col.wait()


def gather_both(x):
    nrow = lax.axis_size("row")
    ncol = lax.axis_size("col")
    assert ncol == 8 and nrow % 4 == 0 and nrow >= 8 and x.shape[0] % N_CHUNK == 0
    plan = _gather_plan(nrow // 2, ncol // 2)
    any_spec = pl.BlockSpec(memory_space=pl.ANY)
    return pl.pallas_call(
        functools.partial(_gather_kernel, plan),
        out_shape=(
            jax.ShapeDtypeStruct((nrow,) + x.shape, x.dtype),
            jax.ShapeDtypeStruct((ncol,) + x.shape, x.dtype),
        ),
        in_specs=[any_spec],
        out_specs=(any_spec, any_spec),
        scratch_shapes=[
            pltpu.SemaphoreType.DMA((len(plan),)),
            pltpu.SemaphoreType.DMA((len(plan),)),
            pltpu.SemaphoreType.DMA((2,)),
        ],
        compiler_params=pltpu.CompilerParams(collective_id=0, has_side_effects=True),
    )(x)


def per_device(voltages, lane_map, input_flags):
    n_chan = lax.axis_size("chan")
    all_chans = CH_DEV * n_chan
    half_q = voltages.shape[1]
    table_rows = kernel_table(NFFT, TAPS, all_chans)
    lane_chunks = voltages.shape[2] // 128
    native = (
        voltages.reshape(P_DEV, half_q, lane_chunks, 128)
        .transpose(0, 2, 1, 3)
        .reshape(P_DEV, lane_chunks * half_q, 128)
    )
    filtered = filter_bank(native, table_rows, half_q)
    filtered = filtered.reshape(P_DEV, half_q, SPECTRA, all_chans, 2)
    filtered = filtered.transpose(3, 0, 1, 4, 2).reshape(all_chans, P_DEV, half_q, 2 * SPECTRA)
    me_chan = lax.axis_index("chan")
    halves = filtered.reshape(n_chan, CH_DEV, P_DEV, half_q, 2 * SPECTRA)
    kept = jnp.where(me_chan == 0, halves[0], halves[1])
    sent = jnp.where(me_chan == 0, halves[1], halves[0])
    received = lax.ppermute(sent, "chan", [(0, 1), (1, 0)])
    lane_index = lane_map.reshape(LANES)
    selector = (lane_index[:, None] == jnp.arange(LANES, dtype=jnp.int32)[None, :]).astype(
        jnp.bfloat16
    )
    by_holder = selector.reshape(LANES, P_DEV, n_chan, half_q)
    sel_kept = jnp.where(me_chan == 0, by_holder[:, :, 0], by_holder[:, :, 1]).reshape(LANES, -1)
    sel_recv = jnp.where(me_chan == 0, by_holder[:, :, 1], by_holder[:, :, 0]).reshape(LANES, -1)
    kept_rows = kept.reshape(CH_DEV, P_DEV * half_q, 2 * SPECTRA)
    recv_rows = received.reshape(CH_DEV, P_DEV * half_q, 2 * SPECTRA)
    reordered = jnp.einsum(
        "kl,clz->ckz", sel_kept, kept_rows, preferred_element_type=jnp.float32
    ) + jnp.einsum("kl,clz->ckz", sel_recv, recv_rows, preferred_element_type=jnp.float32)
    weights = input_flags.reshape(LANES).astype(jnp.float32)[None, :, None]
    channelised = (
        (reordered * weights).astype(jnp.bfloat16).reshape(CH_DEV, P_DEV, Q_DEV, 2 * SPECTRA)
    )
    by_row, by_col = gather_both(channelised.reshape(CH_DEV, P_DEV * Q_DEV, 2 * SPECTRA))
    n_row = by_row.shape[0]
    grid_cols = by_col.shape[0] * Q_DEV
    products = correlate(by_col, by_row)
    return products.reshape(CH_DEV, 2, P_DEV, grid_cols, Q_DEV, n_row * P_DEV)


CH_STEP = 2


def _corr_kernel(c_ref, g_ref, out_ref, cf_ref, lf_ref, rf_ref, acc_ref):
    n_i, blk_i, width = c_ref.shape[0], c_ref.shape[2], c_ref.shape[3]
    n_j, blk = g_ref.shape[0], g_ref.shape[2]
    n_q = Q_DEV
    n_pl = blk_i // n_q
    rows = n_i * blk_i
    n_p2 = n_j * blk // n_q
    lane = lax.broadcasted_iota(jnp.int32, (rows, width), 1)
    for cc in range(c_ref.shape[1]):
        for i in range(n_i):
            cf_ref[pl.ds(i * blk_i, blk_i), :] = c_ref[i, cc].astype(jnp.float32)
        for p in range(n_pl):
            for q in range(n_q):
                lf_ref[pl.ds(p * n_i * n_q + q, n_i, stride=n_q), :] = cf_ref[
                    pl.ds(p * n_q + q, n_i, stride=blk_i), :
                ]
        a32 = lf_ref[...]
        rolled = pltpu.roll(a32, width // 2, 1)
        a_rot = jnp.where(lane >= width // 2, -rolled, rolled)
        both = jnp.concatenate([a32, a_rot], axis=0).astype(out_ref.dtype)
        for j in range(n_j):
            rf_ref[pl.ds(j * blk, blk), :] = g_ref[j, cc].astype(jnp.float32)
        for q2 in range(n_q):
            b = rf_ref[pl.ds(q2, n_p2, stride=n_q), :].astype(out_ref.dtype)
            acc_ref[pl.ds(q2, 2 * rows, stride=n_q), :] = lax.dot_general(
                both, b, (((1,), (1,)), ((), ())), preferred_element_type=jnp.float32
            )
        out_ref[cc] = (acc_ref[...] * (1.0 / SPECTRA)).astype(out_ref.dtype).reshape(out_ref.shape[1:])


def correlate(by_col, by_row):
    n_i, n_c, blk_i, k = by_col.shape
    n_j, _, blk, _ = by_row.shape
    rows = n_i * blk_i
    n_p2 = n_j * blk // Q_DEV
    out_rows = rows * Q_DEV // P_DEV
    return pl.pallas_call(
        _corr_kernel,
        grid=(n_c // CH_STEP,),
        out_shape=jax.ShapeDtypeStruct((n_c, 2, P_DEV, out_rows, n_p2), jnp.bfloat16),
        in_specs=[
            pl.BlockSpec((n_i, CH_STEP, blk_i, k), lambda i: (0, i, 0, 0)),
            pl.BlockSpec((n_j, CH_STEP, blk, k), lambda i: (0, i, 0, 0)),
        ],
        out_specs=pl.BlockSpec((CH_STEP, 2, P_DEV, out_rows, n_p2), lambda i: (i, 0, 0, 0, 0)),
        scratch_shapes=[
            pltpu.VMEM((rows, k), jnp.float32),
            pltpu.VMEM((rows, k), jnp.float32),
            pltpu.VMEM((n_j * blk, k), jnp.float32),
            pltpu.VMEM((2 * rows * Q_DEV, n_p2), jnp.float32),
        ],
    )(by_col, by_row)


def solution(mesh):
    return jax.shard_map(
        per_device,
        mesh=mesh,
        in_specs=(P("row", ("col", "chan"), None), P("row", "col", None), P("row", "col")),
        out_specs=P("chan", None, "row", None, "col", None),
        check_vma=False,
    )
```
